256 devices in a mesh: sub: 64 (over x_hi, y, z), dom: 4 (over x_lo, core).
Axes of the slice: x: 4 (x_hi: 2, x_lo: 2; x = x_hi * 2 + x_lo), y: 4, z: 8, core: 2. Of those that a mesh axis runs over, the one named last changes fastest.
Arguments:
- source_points: float32 [1024, 3, 4096], P(('sub', 'dom')), may hold values from -4 to 4
- boundary: float32 [1024, 8, 6, 128], P(('sub', 'dom')), may hold values from -4 to 4, as said below
- poses: float32 [12, 1024], replicated, may hold values from -2 to 2, as said below
- anchor: float32 [1024], P(('sub', 'dom')), may hold values from 0.3 to 3
- edge_target: int32 [1024, 4], P(('sub', 'dom')), may hold values from 0 to 47, as said below
- corr_tile: int32 [1024, 4, 4], P(('sub', 'dom')), may hold values from 0 to 7
- corr_source: int32 [1024, 4, 4, 128], P(('sub', 'dom')), may hold values from 0 to 4095
- corr_lane: int32 [1024, 4, 4, 128], P(('sub', 'dom')), may hold values from 0 to 127
Outputs:
- refined_pose: float32 [12, 1024], P(None, ('sub', 'dom'))
The draws below stay inside these ranges and needn't reach their ends.
Inputs may be any that keep to these rules, and one draw needn't show every extreme that they name: `poses`: each column holds a rotation matrix, row-major, followed by a translation. `boundary`: in every column of 6 entries the last 3 form a unit vector. `edge_target`: entry v of scan s names scan v % 16 of the previous (v // 16 = 0), the same (1) or the next (2) submap along the closed chain of submaps; it never names s itself; one scan may be named by several edges of s.
All inputs are finite; a program needn't handle non-finite values.
Results may differ from the reference program's by a relative error of at most 0.0001.
Values sent between devices are 32-bit elements; how exact they have to be, the bound alone decides.
A program may use at most 64 MiB of HBM per device.

```python
import math
import jax
import jax.numpy as jnp
from jax import lax

PTS = 4096
BND = 8
EDGES = 4
CT = 4
CG_ITERS = 2
GN_ITERS = 2
SCAN_SUB = 16
SCANS = 1024
N_SUB = 64


def cayley_drawn(vector):
    first, second, third = (vector[0], vector[1], vector[2])
    length_sq = first * first + second * second + third * third
    inverse = 1.0 / (1.0 + length_sq)
    trace_part = 1.0 - length_sq
    entries = [[trace_part + 2.0 * first * first, 2.0 * first * second - 2.0 * third, 2.0 * first * third + 2.0 * second], [2.0 * first * second + 2.0 * third, trace_part + 2.0 * second * second, 2.0 * second * third - 2.0 * first], [2.0 * first * third - 2.0 * second, 2.0 * second * third + 2.0 * first, trace_part + 2.0 * third * third]]
    return jnp.stack([jnp.stack(line) for line in entries]) * inverse


def draw_poses(key, part):
    key_turn, key_move = jax.random.split(jax.random.fold_in(key, 11), 2)
    growth = 0.5 + 1.5 * jnp.arange(SCANS, dtype=jnp.float32) / max(SCANS - 1, 1)
    turning = jax.random.uniform(key_turn, (3, SCANS), jnp.float32, -0.4, 0.4)
    moving = growth * jax.random.uniform(key_move, (3, SCANS), jnp.float32, -1.0, 1.0)
    rotation = cayley_drawn(turning).reshape(9, SCANS)
    return jnp.concatenate([rotation, moving], axis=0).astype(jnp.float32)


def draw_boundary(key, part):
    key_coord, key_height, key_angle = jax.random.split(jax.random.fold_in(key, 23), 3)
    coords = jnp.clip(jax.random.normal(key_coord, (SCANS, BND, 3, 128), jnp.float32), -4.0, 4.0)
    height = jax.random.uniform(key_height, (SCANS, BND, 128), jnp.float32, -1.0, 1.0)
    azimuth = jax.random.uniform(key_angle, (SCANS, BND, 128), jnp.float32, -jnp.pi, jnp.pi)
    radius = jnp.sqrt(jnp.maximum(1.0 - height * height, 0.0))
    normal = jnp.stack([radius * jnp.cos(azimuth), radius * jnp.sin(azimuth), height], axis=2)
    return jnp.concatenate([coords, normal], axis=2).astype(jnp.float32)


def draw_edge_target(key, part):
    own_slot = SCAN_SUB + jnp.arange(SCANS, dtype=jnp.int32) % SCAN_SUB
    raw_pick = jax.random.randint(jax.random.fold_in(key, 37), (SCANS, EDGES), 0, 3 * SCAN_SUB - 1, dtype=jnp.int32)
    return raw_pick + (raw_pick >= own_slot[:, None]).astype(jnp.int32)


def place_ends(array, rng, low, top_value):
    longest = array.shape.index(max(array.shape))
    spots = []
    for shift in (0, 1):
        where = [jax.random.randint(jax.random.fold_in(rng, axis), (), 0, length) for axis, length in enumerate(array.shape)]
        where[longest] = (where[longest] + shift) % array.shape[longest]
        spots.append(tuple(where))
    return array.at[spots[0]].set(low).at[spots[1]].set(top_value)


def shard_levels(own_key, shape, cuts, smallest, high):
    gain, own = 1.0, jax.random.fold_in(own_key, 6)
    for dim, shards_of in cuts:
        draws = jnp.exp(jax.random.uniform(jax.random.fold_in(own, dim), (shards_of,), jnp.float32, smallest / len(cuts), high / len(cuts)))
        gain = gain * jnp.repeat(draws, shape[dim] // shards_of).reshape([-1 if axis == dim else 1 for axis in range(len(shape))])
    return gain


def bell_draw(key, dims, scale, reach, pieces=(), kind=jnp.bfloat16):
    array = scale * jax.random.normal(key, dims, jnp.float32)
    if pieces:
        array = array * shard_levels(key, dims, pieces, -0.22, 0.18)
    return jnp.clip(array, -reach, reach).astype(kind)


def setup_inputs(seed: int = 0) -> dict:
    key_list = jax.random.split(jax.random.key(seed), 9)
    return {
        "source_points": bell_draw(key_list[0], (SCANS, 3, PTS), 1.0, 4.0, ((0, 256),), jnp.float32),
        "boundary": draw_boundary(jax.random.fold_in(key_list[8], 71), 0),
        "poses": draw_poses(jax.random.fold_in(key_list[8], 71), 0),
        "anchor": jnp.clip(jnp.exp(math.log(3.0) - 2.3025851 * jax.random.uniform(key_list[3], (SCANS,), jnp.float32) ** shard_levels(key_list[3], (SCANS,), ((0, 256),), -0.2, 0.2)), 0.3, 3.0),
        "edge_target": draw_edge_target(jax.random.fold_in(key_list[8], 71), 0),
        "corr_tile": place_ends(jax.random.randint(key_list[5], (SCANS, EDGES, CT), 0, BND), jax.random.fold_in(key_list[5], 1), 0, BND - 1).astype(jnp.int32),
        "corr_source": place_ends(jax.random.randint(key_list[6], (SCANS, EDGES, CT, 128), 0, PTS), jax.random.fold_in(key_list[6], 1), 0, PTS - 1).astype(jnp.int32),
        "corr_lane": place_ends(jax.random.randint(key_list[7], (SCANS, EDGES, CT, 128), 0, 128), jax.random.fold_in(key_list[7], 1), 0, 127).astype(jnp.int32),
    }


FINEST = lax.Precision.HIGHEST


def cayley(vector):
    first, second, third = vector[0], vector[1], vector[2]
    length_sq = first * first + second * second + third * third
    inverse = 1.0 / (1.0 + length_sq)
    trace_part = 1.0 - length_sq
    entries = [[trace_part + 2.0 * first * first, 2.0 * first * second - 2.0 * third, 2.0 * first * third + 2.0 * second],
               [2.0 * first * second + 2.0 * third, trace_part + 2.0 * second * second, 2.0 * second * third - 2.0 * first],
               [2.0 * first * third - 2.0 * second, 2.0 * second * third + 2.0 * first, trace_part + 2.0 * third * third]]
    return jnp.stack([jnp.stack(line) for line in entries]) * inverse


def rotate(matrix, vector):
    return jnp.stack([matrix[row_id, 0] * vector[0] + matrix[row_id, 1] * vector[1] + matrix[row_id, 2] * vector[2] for row_id in range(3)])


def update(pose, increment):
    rotation = pose[:9].reshape(3, 3, -1)
    turn_mat = cayley(0.5 * increment[:3])
    rotated = jnp.stack([jnp.stack([turn_mat[row_id, 0] * rotation[0, col_id] + turn_mat[row_id, 1] * rotation[1, col_id] + turn_mat[row_id, 2] * rotation[2, col_id] for col_id in range(3)]) for row_id in range(3)])
    moved_to = rotate(turn_mat, pose[9:]) + increment[3:]
    return jnp.concatenate([rotated.reshape(9, -1), moved_to], axis=0)


def scan_terms(points, pose_here, target_tiles, target_pose, sources, lane_ids):
    edge_count = sources.shape[0]
    picked = jnp.take(points, sources, axis=1)
    placed = rotate(pose_here[:9].reshape(3, 3), picked) + pose_here[9:, None, None, None]
    spread_lanes = jnp.broadcast_to(lane_ids[:, :, None, :], target_tiles.shape)
    chosen = jnp.take_along_axis(target_tiles, spread_lanes, axis=3)
    rotation = target_pose[:9].reshape(3, 3, edge_count)[:, :, :, None, None]
    shifted = target_pose[9:, :, None, None]
    target = rotate(rotation, jnp.stack([chosen[:, :, 0], chosen[:, :, 1], chosen[:, :, 2]])) + shifted
    normal = rotate(rotation, jnp.stack([chosen[:, :, 3], chosen[:, :, 4], chosen[:, :, 5]]))
    offset = target - placed
    misfit = normal[0] * offset[0] + normal[1] * offset[1] + normal[2] * offset[2]
    turned = jnp.stack([placed[1] * normal[2] - placed[2] * normal[1],
                        placed[2] * normal[0] - placed[0] * normal[2],
                        placed[0] * normal[1] - placed[1] * normal[0]])
    jacobian = jnp.concatenate([turned, normal], axis=0).reshape(6, edge_count, -1)
    samples = jacobian.shape[2]
    blocks = jnp.einsum("aem,bem->eab", jacobian, jacobian, precision=FINEST) / samples
    slopes = jnp.einsum("aem,em->ea", jacobian, misfit.reshape(edge_count, -1), precision=FINEST) / samples
    return blocks, slopes


def neighbours(edge_target):
    scan_ids = jnp.arange(SCANS, dtype=jnp.int32)
    submap = scan_ids // SCAN_SUB
    slot_ids = edge_target // SCAN_SUB
    return ((submap[:, None] + slot_ids - 1) % N_SUB) * SCAN_SUB + edge_target % SCAN_SUB


def reference(source_points, boundary, poses, anchor, edge_target, corr_tile, corr_source, corr_lane):
    far_end = neighbours(edge_target).astype(jnp.int32)
    source = jnp.broadcast_to(jnp.arange(SCANS, dtype=jnp.int32)[:, None], far_end.shape)
    from_end = source.reshape(-1)
    to_end = far_end.reshape(-1)
    current = poses
    for turn_id in range(GN_ITERS):
        def per_scan(per_item, current=current):
            points, pose_here, targets, tile_ids, sources, lane_ids = per_item
            return scan_terms(points, pose_here, boundary[targets[:, None], tile_ids], jnp.take(current, targets, axis=1), sources, lane_ids)

        blocks, slopes = lax.map(per_scan, (source_points, current.T, far_end, corr_tile, corr_source, corr_lane))
        blocks = blocks.reshape(-1, 6, 6)
        slopes = slopes.reshape(-1, 6)
        diag_terms = jnp.diagonal(blocks, axis1=1, axis2=2)
        empty = jnp.zeros((6, SCANS), jnp.float32)
        right_side = empty.at[:, from_end].add(slopes.T).at[:, to_end].add(-slopes.T)
        diagonal_sum = anchor[None, :] + empty.at[:, from_end].add(diag_terms.T).at[:, to_end].add(diag_terms.T)

        def apply_system(vector):
            spread = vector[:, from_end] - vector[:, to_end]
            pushed = jnp.einsum("kab,bk->ak", blocks, spread, precision=FINEST)
            return anchor[None, :] * vector + jnp.zeros_like(vector).at[:, from_end].add(pushed).at[:, to_end].add(-pushed)

        residual = right_side
        scaled = residual / diagonal_sum
        direction = scaled
        energy = jnp.sum(residual * scaled)
        increment = jnp.zeros((6, SCANS), jnp.float32)
        for sweep in range(CG_ITERS):
            image = apply_system(direction)
            step_len = energy / jnp.sum(direction * image)
            increment = increment + step_len * direction
            residual = residual - step_len * image
            if sweep + 1 < CG_ITERS:
                scaled = residual / diagonal_sum
                renewed = jnp.sum(residual * scaled)
                direction = scaled + (renewed / energy) * direction
                energy = renewed
        current = update(current, increment)
    return current
```

```python
import functools

import jax
import jax.numpy as jnp
from jax import lax
from jax.experimental import pallas as pl
from jax.experimental.pallas import tpu as pltpu
from jax.sharding import PartitionSpec as P

MESH = pl.DeviceIdType.MESH
F32 = jnp.float32
BF16 = jnp.bfloat16
GN_ITERS = 2
SCAN_DEV = 4
EDGE_SCAN = 4
CT = 4
EDGES = SCAN_DEV * EDGE_SCAN
REACH = 3
SLOTS = 2 * REACH + 1
TILES = 4 * SLOTS
PAD = 32
SAMPLES = CT * 128
PAIRS = [(a, b) for a in range(6) for b in range(a, 6)]


def iota(shape, dim):
    return lax.broadcasted_iota(jnp.int32, shape, dim)


def parts_of(value):
    first = value.astype(BF16)
    rest = value - first.astype(F32)
    second = rest.astype(BF16)
    third = (rest - second.astype(F32)).astype(BF16)
    return (third, second, first)


def dot(a, b):
    return jnp.dot(a, b, preferred_element_type=F32)


def pick_left(select, value):
    third, second, first = parts_of(value)
    return (dot(select, third) + dot(select, second)) + dot(select, first)


def pick_right(value, select):
    third, second, first = parts_of(value)
    return (dot(third, select) + dot(second, select)) + dot(first, select)


def pick_turned(select, value):
    turned = (((1,), (1,)), ((), ()))
    third, second, first = [
        lax.dot_general(select, part, turned, preferred_element_type=F32)
        for part in parts_of(value)
    ]
    return (third + second) + first


def cayley(first, second, third):
    length_sq = first * first + second * second + third * third
    inverse = 1.0 / (1.0 + length_sq)
    trace_part = 1.0 - length_sq
    entries = [
        trace_part + 2.0 * first * first,
        2.0 * first * second - 2.0 * third,
        2.0 * first * third + 2.0 * second,
        2.0 * first * second + 2.0 * third,
        trace_part + 2.0 * second * second,
        2.0 * second * third - 2.0 * first,
        2.0 * first * third - 2.0 * second,
        2.0 * second * third + 2.0 * first,
        trace_part + 2.0 * third * third,
    ]
    return [entry * inverse for entry in entries]


def kernel(
    groups,
    source_ref,
    boundary_ref,
    poses_ref,
    anchor_ref,
    target_ref,
    tile_ref,
    corr_source_ref,
    corr_lane_ref,
    out_ref,
    window,
    early,
    early_own,
    gram,
    gram_own,
    near,
    near_own,
    far,
    far_own,
    picked,
    chosen,
    comps,
    ends,
    win_send,
    win_recv,
    early_send,
    early_recv,
    gram_send,
    gram_recv,
    near_send,
    near_recv,
    far_send,
    far_recv,
    local_sem,
):
    sub = lax.axis_index("sub")
    dom = lax.axis_index("dom")
    half_groups = groups // 2
    sub_low = lax.rem(sub, half_groups)
    sub_high = sub // half_groups

    def near_by(offset):
        return lax.rem(sub + offset + groups, groups)

    window_partners = []
    halo_partners = []
    for offset in range(-REACH, REACH + 1):
        for turn in range(4):
            if offset == 0 and turn == 0:
                continue
            other = lax.rem(dom + turn, 4)
            device = (near_by(offset), other)
            halo_partners.append(
                (device, (REACH - offset) * 4 + dom, (REACH + offset) * 4 + other)
            )
            if abs(offset) <= 1:
                window_partners.append(
                    (device, (1 - offset) * 4 + dom, (1 + offset) * 4 + other)
                )
    near_partners = []
    for turn in range(1, 8):
        spot = lax.rem(sub_high * 4 + dom + turn, 8)
        device = ((spot // 4) * half_groups + sub_low, lax.rem(spot, 4))
        near_partners.append((device, sub_high * 4 + dom, spot))
    far_partners = []
    for turn in range(1, half_groups):
        spot = lax.rem(sub_low + turn, half_groups)
        far_partners.append(((sub_high * half_groups + spot, dom), sub_low, spot))

    barrier = pltpu.get_barrier_semaphore()
    everyone = halo_partners + near_partners + far_partners
    for device, _, _ in everyone:
        pl.semaphore_signal(barrier, inc=1, device_id=device, device_id_type=MESH)

    own_tiles = pltpu.make_async_copy(
        boundary_ref, window.at[pl.ds((4 + dom) * 32, 32)], local_sem
    )
    own_tiles.start()
    lane_row = iota((1, 128), 1)
    row = jnp.zeros((1, 128), F32)
    edge_of_row = iota((EDGES, 128), 0)
    own_target = jnp.zeros((EDGES, 128), jnp.int32)
    for edge in range(EDGES):
        value = target_ref[edge // EDGE_SCAN, edge % EDGE_SCAN]
        row = jnp.where(lane_row == edge, value.astype(F32), row)
        own_target = jnp.where(edge_of_row == edge, value, own_target)
    for scan in range(SCAN_DEV):
        row = jnp.where(lane_row == EDGES + scan, anchor_ref[scan], row)
    early_own[0] = row
    early[pl.ds(REACH * 4 + dom, 1)] = row.reshape(1, 1, 128)
    early[pl.ds(TILES, PAD - TILES)] = jnp.zeros((PAD - TILES, 1, 128), F32)
    for step in range(GN_ITERS):
        gram[step, pl.ds(TILES, PAD - TILES)] = jnp.zeros((PAD - TILES, 8, 128), F32)

    pl.semaphore_wait(barrier, len(everyone))

    def push(source, at_partner, here, send_sem, recv_sem, partners):
        copies = []
        for number, (device, mine, theirs) in enumerate(partners):
            copy = pltpu.make_async_remote_copy(
                src_ref=source,
                dst_ref=at_partner(mine),
                send_sem=send_sem(number),
                recv_sem=recv_sem(mine),
                device_id=device,
                device_id_type=MESH,
            )
            copy.start()
            arrival = pltpu.make_async_remote_copy(
                src_ref=source,
                dst_ref=here(theirs),
                send_sem=send_sem(number),
                recv_sem=recv_sem(theirs),
                device_id=device,
                device_id_type=MESH,
            )
            copies.append((copy, arrival))
        return copies

    started = []
    tile_slot = lambda slot: window.at[pl.ds(slot * 32, 32)]
    window_copies = push(
        boundary_ref,
        tile_slot,
        tile_slot,
        lambda n: win_send.at[n],
        lambda n: win_recv.at[n],
        window_partners,
    )
    early_slot = lambda slot: early.at[pl.ds(slot, 1)]
    early_copies = push(
        early_own,
        early_slot,
        early_slot,
        lambda n: early_send.at[n],
        lambda n: early_recv.at[n],
        halo_partners,
    )
    started += window_copies + early_copies

    def gather_scan(scan, carry):
        indices = corr_source_ref[scan].reshape(EDGE_SCAN * CT, 128)
        low = lax.bitwise_and(indices, 127)
        high = lax.shift_right_logical(indices, 7)
        found = [jnp.zeros((EDGE_SCAN * CT, 128), F32) for _ in range(3)]
        for block in range(32):
            here = high == block
            for comp in range(3):
                line = source_ref[scan, pl.ds(comp, 1), pl.ds(block * 128, 128)]
                wide = jnp.broadcast_to(line, (EDGE_SCAN * CT, 128))
                value = jnp.take_along_axis(wide, low, axis=1, mode="promise_in_bounds")
                found[comp] = jnp.where(here, value, found[comp])
        for comp in range(3):
            picked[comp, pl.ds(scan * 16, 16), :] = found[comp]
        return carry

    lax.fori_loop(0, SCAN_DEV, gather_scan, 0)

    start = near_by(-REACH) * 16
    first_tile = start // 128
    next_tile = lax.rem(first_tile + 1, groups * 16 // 128)
    pair = jnp.concatenate(
        [
            poses_ref[:, pl.ds(pl.multiple_of(first_tile * 128, 128), 128)],
            poses_ref[:, pl.ds(pl.multiple_of(next_tile * 128, 128), 128)],
        ],
        axis=1,
    )
    shift = lax.rem(256 - lax.rem(start, 128), 256)
    rolled = pltpu.roll(pair, shift, 1)[:, :128]
    pose = [rolled[k : k + 1] for k in range(12)]

    lane16 = iota((EDGES, 128), 1)
    own_source_lane = REACH * 16 + dom * SCAN_DEV + edge_of_row // EDGE_SCAN
    own_ends = jnp.concatenate(
        [
            (lane16 == own_source_lane).astype(F32),
            (lane16 == own_target + (REACH - 1) * 16).astype(F32),
        ],
        axis=0,
    ).astype(BF16)

    from_lane = iota((128, 128), 0)
    to_lane = iota((128, 128), 1)
    from_a = lax.shift_right_logical(from_lane, 3) & 7
    from_b = from_lane & 7
    to_half = lax.shift_right_logical(to_lane, 6)
    to_a = lax.shift_right_logical(to_lane, 3) & 7
    to_b = to_lane & 7
    used = (to_a < 6) & (to_b < 6) & (from_b < 6)
    as_select = lambda mask: mask.astype(F32).astype(BF16)
    over_b = as_select(used & (from_a == to_b))
    slopes_out = as_select(used & (from_a == 6) & (from_b == to_b))
    diagonal_out = as_select(used & (from_a == from_b) & (from_b == to_b))
    left = to_half == 0
    left_256 = iota((256, 128), 1) < 64

    for _, arrival in early_copies:
        arrival.wait_recv()
    rows = early[...].reshape(PAD, 128)
    rows_turned = jnp.concatenate([rows, jnp.zeros((128 - PAD, 128), F32)], axis=0).T
    lane8 = iota((8, 128), 1)
    row8 = iota((8, 128), 0)
    for tile in range(TILES):
        for half in range(2):
            target = rows_turned[half * 8 : half * 8 + 8, tile : tile + 1]
            target_lane = target + float((tile // 4 - 1) * 16)
            source_lane = tile * 4 + half * 2 + row8 // 4
            ends[pl.ds(tile * 8, 8), pl.ds(half * 128, 128)] = (
                lane8 == source_lane
            ).astype(F32) - (lane8.astype(F32) == target_lane).astype(F32)
    ends[pl.ds(TILES * 8, (PAD - TILES) * 8), :] = jnp.zeros(((PAD - TILES) * 8, 256), F32)
    ends_f32 = ends[...]
    ends_turned_f32 = ends_f32.T
    ends_in = ends_f32.astype(BF16)
    ends_out = ends_turned_f32.astype(BF16)
    ends_abs = jnp.abs(ends_turned_f32).astype(BF16)
    node = iota((128, PAD), 0)
    of_tile = as_select(node // 4 == iota((128, PAD), 1))
    anchor_rows = pick_left(of_tile, rows)
    node_128 = from_lane
    mine = to_lane == EDGES + (node_128 & 3)
    anchor = jnp.sum(jnp.where(mine, anchor_rows, 0.0), axis=1, keepdims=True)
    anchor = jnp.where(node_128 < TILES * 4, jnp.broadcast_to(anchor, (128, 128)), 1.0)
    own_nodes = (
        (node_128 // 4 == REACH * 4 + dom)
        & (to_lane < 6)
    )

    own_tiles.wait()
    for _, arrival in window_copies:
        arrival.wait_recv()

    def gather_edge(edge, carry):
        scan = edge // EDGE_SCAN
        slot = lax.rem(edge, EDGE_SCAN)
        first = target_ref[scan, slot] * 8
        lanes = corr_lane_ref[scan, slot]
        for chunk in range(CT):
            tile = window[first + tile_ref[scan, slot, chunk]]
            spread = jnp.broadcast_to(lanes[chunk : chunk + 1], (8, 128))
            value = jnp.take_along_axis(tile, spread, axis=1, mode="promise_in_bounds")
            chosen[pl.ds(pl.multiple_of(edge * 32 + chunk * 8, 8), 8), :] = value
        return carry

    lax.fori_loop(0, EDGES, gather_edge, 0)
    for chunk in range(CT):
        for comp in range(3):
            comps[comp, chunk] = picked[comp, pl.ds(chunk, EDGES, stride=CT), :]
        for comp in range(6):
            comps[3 + comp, chunk] = chosen[pl.ds(chunk * 8 + comp, EDGES, stride=32), :]

    msg_pos = lane8 & 63

    for step in range(GN_ITERS):
        pose_rows = jnp.concatenate(pose + [jnp.zeros((4, 128), F32)], axis=0)
        pose_ends = pick_turned(own_ends, pose_rows)
        message = jnp.zeros((8, 128), F32)
        for half in range(2):
            here = [
                jnp.broadcast_to(pose_ends[half * 8 : half * 8 + 8, k : k + 1], (8, 128))
                for k in range(12)
            ]
            there = [
                jnp.broadcast_to(
                    pose_ends[EDGES + half * 8 : EDGES + half * 8 + 8, k : k + 1], (8, 128)
                )
                for k in range(12)
            ]
            sums = {}
            for chunk in range(CT):
                data = [comps[k, chunk, pl.ds(half * 8, 8), :] for k in range(9)]

                def turn(matrix, vector):
                    return [
                        matrix[3 * i] * vector[0]
                        + matrix[3 * i + 1] * vector[1]
                        + matrix[3 * i + 2] * vector[2]
                        for i in range(3)
                    ]

                placed = [v + t for v, t in zip(turn(here[:9], data[0:3]), here[9:])]
                target = [v + t for v, t in zip(turn(there[:9], data[3:6]), there[9:])]
                normal = turn(there[:9], data[6:9])
                offset = [q - p for q, p in zip(target, placed)]
                misfit = normal[0] * offset[0] + normal[1] * offset[1] + normal[2] * offset[2]
                jac = [
                    placed[1] * normal[2] - placed[2] * normal[1],
                    placed[2] * normal[0] - placed[0] * normal[2],
                    placed[0] * normal[1] - placed[1] * normal[0],
                ] + normal
                for a, b in PAIRS:
                    term = jac[a] * jac[b]
                    sums[a, b] = sums[a, b] + term if chunk else term
                for b in range(6):
                    term = jac[b] * misfit
                    sums[6, b] = sums[6, b] + term if chunk else term
            in_half = lane8 // 64 == half
            for (a, b), value in sums.items():
                total = jnp.sum(value, axis=1, keepdims=True) * (1.0 / SAMPLES)
                place = msg_pos == a * 8 + b
                if a < 6:
                    place = place | (msg_pos == b * 8 + a)
                message = jnp.where(in_half & place, total, message)
        gram_own[step, 0] = message
        gram[step, pl.ds(REACH * 4 + dom, 1)] = message.reshape(1, 8, 128)
        gram_slot = lambda slot: gram.at[step, pl.ds(slot, 1)]
        gram_copies = push(
            gram_own.at[step],
            gram_slot,
            gram_slot,
            lambda n: gram_send.at[step, n],
            lambda n: gram_recv.at[step, n],
            halo_partners,
        )
        started += gram_copies
        for _, arrival in gram_copies:
            arrival.wait_recv()
        terms = gram[step].reshape(PAD * 8, 128)

        def at_nodes(select, value):
            both = pick_left(select, value)
            return jnp.where(left, both[:128], both[128:])

        def difference(select, value):
            twice = jnp.concatenate([value, value], axis=0)
            sides = iota((256, 128), 0) < 128
            return pick_left(select, jnp.where(sides == left_256, twice, 0.0))

        def apply_system(value):
            image = at_nodes(ends_out, terms * difference(ends_in, value))
            return pick_right(image, over_b) + anchor * value

        residual = pick_right(at_nodes(ends_out, terms), slopes_out)
        diagonal = pick_right(at_nodes(ends_abs, terms), diagonal_out) + anchor
        inverse = 1.0 / diagonal
        scaled = residual * inverse
        image = apply_system(scaled)
        second = image * inverse

        own_in = jnp.concatenate(
            [
                ends[pl.ds(pl.multiple_of((REACH * 4 + dom) * 8, 8), 8), :],
                jnp.zeros((8, 256), F32),
            ],
            axis=0,
        ).astype(BF16)
        own_diff = difference(own_in, second)
        first_row = as_select(
            (lax.shift_right_logical(from_lane, 6) == to_half)
            & (from_a == 0)
            & (from_b == to_a)
            & (to_a < 6)
        )
        own_diff_a = pick_right(own_diff, first_row)
        quad = (message * own_diff[:8]) * own_diff_a[:8]

        def inner(a, b):
            return jnp.sum(jnp.where(own_nodes, a * b, 0.0), keepdims=True)

        energy = inner(residual, scaled)
        curve = inner(scaled, image)
        cross = inner(second, image)
        bend = inner(anchor * second, second) + jnp.sum(quad, keepdims=True)
        sums_row = jnp.zeros((1, 128), F32)
        for number, value in enumerate((energy, curve, cross, bend)):
            sums_row = jnp.where(lane_row == number, value, sums_row)

        def exchange(value, own, buffer, spot, count, send, recv, partners):
            own[step, 0] = value
            buffer[step, pl.ds(spot, 1)] = value.reshape(1, 1, 128)
            slot = lambda n: buffer.at[step, pl.ds(n, 1)]
            copies = push(
                own.at[step],
                slot,
                slot,
                lambda n: send.at[step, n],
                lambda n: recv.at[step, n],
                partners,
            )
            for _, arrival in copies:
                arrival.wait_recv()
            gathered = buffer[step].reshape(count, 128)
            return copies, jnp.sum(gathered, axis=0, keepdims=True)

        scaled_turned = scaled.T[:8]
        second_turned = second.T[:8]
        copies, sums_row = exchange(
            sums_row, near_own, near, sub_high * 4 + dom, 8, near_send, near_recv, near_partners
        )
        started += copies
        copies, sums_row = exchange(
            sums_row, far_own, far, sub_low, half_groups, far_send, far_recv, far_partners
        )
        started += copies

        energy, curve, cross, bend = [sums_row[:, k : k + 1] for k in range(4)]
        step_one = energy / curve
        renewed = step_one * step_one * cross - energy
        ratio = renewed / energy
        curve_two = (
            curve
            - 2.0 * step_one * cross
            + step_one * step_one * bend
            + 2.0 * ratio * (curve - step_one * cross)
            + ratio * ratio * curve
        )
        step_two = renewed / curve_two
        increment = (step_one + step_two * (1.0 + ratio)) * scaled_turned - (
            step_two * step_one
        ) * second_turned
        inc = [increment[k : k + 1] for k in range(6)]
        turn_mat = cayley(0.5 * inc[0], 0.5 * inc[1], 0.5 * inc[2])
        rotated = [
            turn_mat[3 * i] * pose[j]
            + turn_mat[3 * i + 1] * pose[3 + j]
            + turn_mat[3 * i + 2] * pose[6 + j]
            for i in range(3)
            for j in range(3)
        ]
        moved = [
            turn_mat[3 * i] * pose[9]
            + turn_mat[3 * i + 1] * pose[10]
            + turn_mat[3 * i + 2] * pose[11]
            + inc[3 + i]
            for i in range(3)
        ]
        pose = rotated + moved

    final = jnp.concatenate(pose + [jnp.zeros((4, 128), F32)], axis=0)
    final = pltpu.roll(final, 128 - (REACH * 16 + dom * SCAN_DEV), 1)
    out_ref[...] = final[:12, :SCAN_DEV]

    for copy, _ in started:
        copy.wait_send()


def local(groups, source_points, boundary, poses, anchor, edge_target, corr_tile, corr_source, corr_lane):
    vmem = pl.BlockSpec(memory_space=pltpu.VMEM)
    smem = pl.BlockSpec(memory_space=pltpu.SMEM)
    dma = pltpu.SemaphoreType.DMA
    halo = TILES - 1
    far = groups // 2
    return pl.pallas_call(
        functools.partial(kernel, groups),
        out_shape=jax.ShapeDtypeStruct((12, SCAN_DEV), F32),
        in_specs=[vmem, vmem, vmem, smem, smem, smem, vmem, vmem],
        out_specs=vmem,
        scratch_shapes=[
            pltpu.VMEM((12 * 32, 8, 128), F32),
            pltpu.VMEM((PAD, 1, 128), F32),
            pltpu.VMEM((1, 1, 128), F32),
            pltpu.VMEM((GN_ITERS, PAD, 8, 128), F32),
            pltpu.VMEM((GN_ITERS, 1, 8, 128), F32),
            pltpu.VMEM((GN_ITERS, 8, 1, 128), F32),
            pltpu.VMEM((GN_ITERS, 1, 1, 128), F32),
            pltpu.VMEM((GN_ITERS, far, 1, 128), F32),
            pltpu.VMEM((GN_ITERS, 1, 1, 128), F32),
            pltpu.VMEM((3, 64, 128), F32),
            pltpu.VMEM((512, 128), F32),
            pltpu.VMEM((9, CT, EDGES, 128), F32),
            pltpu.VMEM((PAD * 8, 256), F32),
            dma((11,)),
            dma((12,)),
            dma((halo,)),
            dma((TILES,)),
            dma((GN_ITERS, halo)),
            dma((GN_ITERS, TILES)),
            dma((GN_ITERS, 7)),
            dma((GN_ITERS, 8)),
            dma((GN_ITERS, far - 1)),
            dma((GN_ITERS, far)),
            dma,
        ],
        compiler_params=pltpu.CompilerParams(collective_id=0, has_side_effects=True),
    )(
        source_points,
        jnp.pad(boundary.reshape(32, 6, 128), ((0, 0), (0, 2), (0, 0))),
        poses,
        anchor,
        edge_target,
        corr_tile,
        corr_source,
        corr_lane,
    )


def solution(mesh):
    both = ("sub", "dom")
    return jax.shard_map(
        functools.partial(local, mesh.shape["sub"]),
        mesh=mesh,
        in_specs=(
            P(both, None, None),
            P(both, None, None, None),
            P(),
            P(both),
            P(both, None),
            P(both, None, None),
            P(both, None, None, None),
            P(both, None, None, None),
        ),
        out_specs=P(None, both),
        check_vma=False,
    )
```

```python
import functools

import jax
import jax.numpy as jnp
from jax import lax
from jax.experimental import pallas as pl
from jax.experimental.pallas import tpu as pltpu
from jax.sharding import PartitionSpec as P

MESH = pl.DeviceIdType.MESH
F32 = jnp.float32
BF16 = jnp.bfloat16
GN_ITERS = 2
SCAN_DEV = 4
EDGE_SCAN = 4
CT = 4
EDGES = SCAN_DEV * EDGE_SCAN
REACH = 3
SLOTS = 2 * REACH + 1
TILES = 4 * SLOTS
PAD = 32
SAMPLES = CT * 128
ROWS = SCAN_DEV * 6 * 8
PARTS = 2
PART = ROWS // PARTS
PAIRS = [(a, b) for a in range(6) for b in range(a, 6)]


def iota(shape, dim):
    return lax.broadcasted_iota(jnp.int32, shape, dim)


def parts_of(value):
    first = value.astype(BF16)
    rest = value - first.astype(F32)
    second = rest.astype(BF16)
    third = (rest - second.astype(F32)).astype(BF16)
    return (third, second, first)


def dot(a, b):
    return jnp.dot(a, b, preferred_element_type=F32)


def pick_left(select, value):
    third, second, first = parts_of(value)
    return (dot(select, third) + dot(select, second)) + dot(select, first)


def pick_right(value, select):
    third, second, first = parts_of(value)
    return (dot(third, select) + dot(second, select)) + dot(first, select)


def pick_turned(select, value):
    turned = (((1,), (1,)), ((), ()))
    third, second, first = [
        lax.dot_general(select, part, turned, preferred_element_type=F32)
        for part in parts_of(value)
    ]
    return (third + second) + first


def cayley(first, second, third):
    length_sq = first * first + second * second + third * third
    inverse = 1.0 / (1.0 + length_sq)
    trace_part = 1.0 - length_sq
    entries = [
        trace_part + 2.0 * first * first,
        2.0 * first * second - 2.0 * third,
        2.0 * first * third + 2.0 * second,
        2.0 * first * second + 2.0 * third,
        trace_part + 2.0 * second * second,
        2.0 * second * third - 2.0 * first,
        2.0 * first * third - 2.0 * second,
        2.0 * second * third + 2.0 * first,
        trace_part + 2.0 * third * third,
    ]
    return [entry * inverse for entry in entries]


def kernel(
    groups,
    source_hbm,
    boundary_hbm,
    poses_hbm,
    anchor_ref,
    target_ref,
    tile_ref,
    corr_source_hbm,
    corr_lane_hbm,
    out_ref,
    corr_source_ref,
    corr_lane_ref,
    source_ref,
    poses_ref,
    window,
    early,
    gram,
    far,
    picked,
    chosen,
    comps,
    ends,
    win_send,
    win_recv,
    early_send,
    early_recv,
    gram_send,
    gram_recv,
    far_send,
    far_recv,
    load_sem,
):
    sub = lax.axis_index("sub")
    dom = lax.axis_index("dom")
    half_groups = groups // 2
    sub_low = lax.rem(sub, half_groups)
    sub_high = sub // half_groups

    def near_by(offset):
        return lax.rem(sub + offset + groups, groups)

    halo_partners = [
        ((near_by(offset), lax.bitwise_xor(dom, other)), (REACH - offset) * 4 + dom)
        for distance in range(REACH + 1)
        for offset in ((distance, -distance) if distance else (0,))
        for other in range(4)
        if distance or other
    ]
    sum_partners = [
        ((sub_high * half_groups + lax.rem(sub_low + turn, half_groups), dom), sub)
        for turn in range(1, half_groups)
    ] + [
        (
            (
                (1 - sub_high) * half_groups + lax.rem(sub_low + turn, half_groups),
                lax.bitwise_xor(dom, 2),
            ),
            sub,
        )
        for turn in range(half_groups)
    ]

    loads = [
        pltpu.make_async_copy(source, target, load_sem.at[number])
        for number, (source, target) in enumerate(
            (
                (boundary_hbm, window.at[pl.ds((4 + dom) * ROWS, ROWS)]),
                (corr_source_hbm, corr_source_ref),
                (source_hbm, source_ref),
                (poses_hbm, poses_ref),
                (corr_lane_hbm, corr_lane_ref),
            )
        )
    ]
    for load in loads:
        load.start()
    barrier = pltpu.get_barrier_semaphore()
    everyone = halo_partners + sum_partners
    for device, _ in everyone:
        pl.semaphore_signal(barrier, inc=1, device_id=device, device_id_type=MESH)

    pl.semaphore_wait(barrier, len(everyone))

    def push(copies, send_sem, recv_sem):
        for source, target, device in copies:
            pltpu.make_async_remote_copy(
                src_ref=source,
                dst_ref=target,
                send_sem=send_sem,
                recv_sem=recv_sem,
                device_id=device,
                device_id_type=MESH,
            ).start()

    def whole(ref, send_sem, recv_sem):
        return pltpu.make_async_remote_copy(
            src_ref=ref,
            dst_ref=ref,
            send_sem=send_sem,
            recv_sem=recv_sem,
            device_id=(sub, lax.bitwise_xor(dom, 1)),
            device_id_type=MESH,
        )

    own_slot = REACH * 4 + dom

    def halo_push(buffer, send, recv):
        own = buffer.at[pl.ds(own_slot, 1)]
        push(
            [(own, buffer.at[pl.ds(slot, 1)], device) for device, slot in halo_partners],
            send,
            recv,
        )
        return whole(buffer.at[pl.ds(0, TILES - 1)], send, recv)

    started = []
    loads[0].wait()
    sibling = lax.bitwise_xor(dom, 1)
    across = lax.bitwise_xor(dom, 2)
    to_sibling = (sub, sibling)
    to_across = (sub, across)

    to_next = lax.bitwise_xor(dom, 2 * (sub_low // (half_groups - 1)))
    to_last = lax.bitwise_xor(dom, 2 * (lax.rem(sub_low + half_groups - 1, half_groups) // (half_groups - 1)))

    def window_copy(number, part, slot, device):
        at = window.at[pl.ds(slot * ROWS + part * PART, PART)]
        return pltpu.make_async_remote_copy(
            src_ref=at,
            dst_ref=at,
            send_sem=win_send.at[number, part],
            recv_sem=win_recv.at[slot, part],
            device_id=device,
            device_id_type=MESH,
        )

    def window_copy_to(number, part, slot, slot_there, device):
        at = window.at[pl.ds(slot * ROWS + part * PART, PART)]
        there = window.at[pl.ds(slot_there * ROWS + part * PART, PART)]
        return pltpu.make_async_remote_copy(
            src_ref=at,
            dst_ref=there,
            send_sem=win_send.at[number, part],
            recv_sem=win_recv.at[slot_there, part],
            device_id=device,
            device_id_type=MESH,
        )

    def window_send(number, part, slot, device, slot_there=None):
        slot_there = slot if slot_there is None else slot_there
        copy = window_copy_to(number, part, slot, slot_there, device)
        copy.start()
        started.append(copy)

    def window_wait(part, slot):
        window_copy(0, part, slot, to_sibling).wait_recv()

    for part in range(PARTS):
        window_send(0, part, 4 + dom, (near_by(1), to_next), dom)
        window_send(1, part, 4 + dom, (near_by(-1), to_last), 8 + dom)
    for part in range(PARTS):
        window_send(2, part, 4 + dom, to_across)
    for part in range(PARTS):
        window_send(3, part, 4 + dom, to_sibling)
    lane_row = iota((1, 128), 1)
    row = jnp.zeros((1, 128), F32)
    edge_of_row = iota((EDGES, 128), 0)
    own_target = jnp.zeros((EDGES, 128), jnp.int32)
    for edge in range(EDGES):
        value = target_ref[edge // EDGE_SCAN, edge % EDGE_SCAN]
        row = jnp.where(lane_row == edge, value.astype(F32), row)
        own_target = jnp.where(edge_of_row == edge, value, own_target)
    for scan in range(SCAN_DEV):
        row = jnp.where(lane_row == EDGES + scan, anchor_ref[scan], row)
    early[pl.ds(own_slot, 1)] = row.reshape(1, 1, 128)
    early_copies = halo_push(early, early_send, early_recv)
    started.append(early_copies)
    early[pl.ds(TILES, 4)] = jnp.zeros((4, 1, 128), F32)
    for step in range(GN_ITERS):
        gram[step, pl.ds(TILES, 4)] = jnp.zeros((4, 8, 128), F32)

    def gather_scan(scan):
        indices = corr_source_ref[scan].reshape(EDGE_SCAN * CT, 128)
        low = lax.bitwise_and(indices, 127)
        high = lax.shift_right_logical(indices, 7)

        def gather_blocks(group, found):
            found = list(found)
            for number in range(8):
                block = group * 8 + number
                here = high == block
                for comp in range(3):
                    at = pl.multiple_of(block * 128, 128)
                    line = source_ref[comp, pl.ds(scan, 1), pl.ds(at, 128)]
                    wide = jnp.broadcast_to(line, (EDGE_SCAN * CT, 128))
                    value = jnp.take_along_axis(wide, low, axis=1, mode="promise_in_bounds")
                    found[comp] = jnp.where(here, value, found[comp])
            return tuple(found)

        empty = jnp.zeros((EDGE_SCAN * CT, 128), F32)
        found = lax.fori_loop(0, 4, gather_blocks, (empty, empty, empty))
        for comp in range(3):
            picked[comp, pl.ds(scan * 16, 16), :] = found[comp]

    loads[1].wait()
    loads[2].wait()
    for part in range(PARTS):
        gather_scan(part)
        for number, slot in ((4, to_last), (5, 8 + to_next)):
            window_wait(part, slot)
            window_send(number, part, slot, to_across)
            window_send(number + 2, part, slot, to_sibling)
        window_wait(part, 4 + across)
        window_send(8, part, 4 + across, to_sibling)
    gather_scan(2)
    gather_scan(3)
    for part in range(PARTS):
        for number, slot in (
            (9, lax.bitwise_xor(to_last, 2)),
            (10, 8 + lax.bitwise_xor(to_next, 2)),
        ):
            window_wait(part, slot)
            window_send(number, part, slot, to_sibling)

    loads[3].wait()
    start = near_by(-REACH) * 16
    first_tile = start // 128
    next_tile = lax.rem(first_tile + 1, groups * 16 // 128)
    pair = jnp.concatenate(
        [
            poses_ref[:, pl.ds(pl.multiple_of(first_tile * 128, 128), 128)],
            poses_ref[:, pl.ds(pl.multiple_of(next_tile * 128, 128), 128)],
        ],
        axis=1,
    )
    shift = lax.rem(256 - lax.rem(start, 128), 256)
    rolled = pltpu.roll(pair, shift, 1)[:, :128]
    pose = [rolled[k : k + 1] for k in range(12)]

    lane16 = iota((EDGES, 128), 1)
    own_source_lane = REACH * 16 + dom * SCAN_DEV + edge_of_row // EDGE_SCAN
    own_ends = jnp.concatenate(
        [
            (lane16 == own_source_lane).astype(F32),
            (lane16 == own_target + (REACH - 1) * 16).astype(F32),
        ],
        axis=0,
    ).astype(BF16)

    from_lane = iota((128, 128), 0)
    to_lane = iota((128, 128), 1)
    from_a = lax.shift_right_logical(from_lane, 3) & 7
    from_b = from_lane & 7
    to_half = lax.shift_right_logical(to_lane, 6)
    to_a = lax.shift_right_logical(to_lane, 3) & 7
    to_b = to_lane & 7
    used = (to_a < 6) & (to_b < 6) & (from_b < 6)
    as_select = lambda mask: mask.astype(F32).astype(BF16)
    over_b = as_select(used & (from_a == to_b))
    slopes_out = as_select(used & (from_a == 6) & (from_b == to_b))
    diagonal_out = as_select(used & (from_a == from_b) & (from_b == to_b))
    left = to_half == 0
    left_256 = iota((256, 128), 1) < 64

    early_copies.wait_recv()
    rows = early[...].reshape(PAD, 128)
    rows_turned = jnp.concatenate([rows, jnp.zeros((128 - PAD, 128), F32)], axis=0).T
    lane8 = iota((8, 128), 1)
    row8 = iota((8, 128), 0)
    for tile in range(TILES):
        for half in range(2):
            target = rows_turned[half * 8 : half * 8 + 8, tile : tile + 1]
            target_lane = target + float((tile // 4 - 1) * 16)
            source_lane = tile * 4 + half * 2 + row8 // 4
            ends[pl.ds(tile * 8, 8), pl.ds(half * 128, 128)] = (
                lane8 == source_lane
            ).astype(F32) - (lane8.astype(F32) == target_lane).astype(F32)
    ends[pl.ds(TILES * 8, (PAD - TILES) * 8), :] = jnp.zeros(((PAD - TILES) * 8, 256), F32)
    ends_f32 = ends[...]
    ends_turned_f32 = ends_f32.T
    ends_in = ends_f32.astype(BF16)
    ends_out = ends_turned_f32.astype(BF16)
    ends_abs = jnp.abs(ends_turned_f32).astype(BF16)
    node = iota((128, PAD), 0)
    of_tile = as_select(node // 4 == iota((128, PAD), 1))
    anchor_rows = pick_left(of_tile, rows)
    node_128 = from_lane
    mine = to_lane == EDGES + (node_128 & 3)
    anchor = jnp.sum(jnp.where(mine, anchor_rows, 0.0), axis=1, keepdims=True)
    anchor = jnp.where(node_128 < TILES * 4, jnp.broadcast_to(anchor, (128, 128)), 1.0)
    own_nodes = (node_128 // 16 == REACH) & (to_lane < 6)

    for part in range(PARTS):
        for other in (sibling, lax.bitwise_xor(dom, 3)):
            for offset in range(3):
                window_wait(part, offset * 4 + other)
    loads[4].wait()

    def gather_edge(edge, carry):
        scan = edge // EDGE_SCAN
        slot = lax.rem(edge, EDGE_SCAN)
        first = target_ref[scan, slot] * 48
        lanes = corr_lane_ref[scan, slot]
        for chunk in range(CT):
            tile = window[pl.ds(first + tile_ref[scan, slot, chunk], 8, stride=8), :]
            spread = jnp.broadcast_to(lanes[chunk : chunk + 1], (8, 128))
            value = jnp.take_along_axis(tile, spread, axis=1, mode="promise_in_bounds")
            chosen[pl.ds(pl.multiple_of(edge * 32 + chunk * 8, 8), 8), :] = value
        return carry

    lax.fori_loop(0, EDGES, gather_edge, 0)
    for chunk in range(CT):
        for comp in range(3):
            comps[comp, chunk] = picked[comp, pl.ds(chunk, EDGES, stride=CT), :]
        for comp in range(6):
            comps[3 + comp, chunk] = chosen[pl.ds(chunk * 8 + comp, EDGES, stride=32), :]

    msg_pos = lane8 & 63

    for step in range(GN_ITERS):
        pose_rows = jnp.concatenate(pose + [jnp.zeros((4, 128), F32)], axis=0)
        pose_ends = pick_turned(own_ends, pose_rows)
        message = jnp.zeros((8, 128), F32)
        for half in range(2):
            here = [
                jnp.broadcast_to(pose_ends[half * 8 : half * 8 + 8, k : k + 1], (8, 128))
                for k in range(12)
            ]
            there = [
                jnp.broadcast_to(
                    pose_ends[EDGES + half * 8 : EDGES + half * 8 + 8, k : k + 1], (8, 128)
                )
                for k in range(12)
            ]
            sums = {}
            for chunk in range(CT):
                data = [comps[k, chunk, pl.ds(half * 8, 8), :] for k in range(9)]

                def turn(matrix, vector):
                    return [
                        matrix[3 * i] * vector[0]
                        + matrix[3 * i + 1] * vector[1]
                        + matrix[3 * i + 2] * vector[2]
                        for i in range(3)
                    ]

                placed = [v + t for v, t in zip(turn(here[:9], data[0:3]), here[9:])]
                target = [v + t for v, t in zip(turn(there[:9], data[3:6]), there[9:])]
                normal = turn(there[:9], data[6:9])
                offset = [q - p for q, p in zip(target, placed)]
                misfit = normal[0] * offset[0] + normal[1] * offset[1] + normal[2] * offset[2]
                jac = [
                    placed[1] * normal[2] - placed[2] * normal[1],
                    placed[2] * normal[0] - placed[0] * normal[2],
                    placed[0] * normal[1] - placed[1] * normal[0],
                ] + normal
                for a, b in PAIRS:
                    term = jac[a] * jac[b]
                    sums[a, b] = sums[a, b] + term if chunk else term
                for b in range(6):
                    term = jac[b] * misfit
                    sums[6, b] = sums[6, b] + term if chunk else term
            in_half = lane8 // 64 == half
            for (a, b), value in sums.items():
                total = jnp.sum(value, axis=1, keepdims=True) * (1.0 / SAMPLES)
                place = msg_pos == a * 8 + b
                if a < 6:
                    place = place | (msg_pos == b * 8 + a)
                message = jnp.where(in_half & place, total, message)
        gram[step, pl.ds(own_slot, 1)] = message.reshape(1, 8, 128)
        gram_copies = halo_push(gram.at[step], gram_send.at[step], gram_recv.at[step])
        started.append(gram_copies)
        gram_copies.wait_recv()
        terms = gram[step].reshape(PAD * 8, 128)

        def at_nodes(select, value):
            both = pick_left(select, value)
            return jnp.where(left, both[:128], both[128:])

        def difference(select, value):
            twice = jnp.concatenate([value, value], axis=0)
            sides = iota((256, 128), 0) < 128
            return pick_left(select, jnp.where(sides == left_256, twice, 0.0))

        def apply_system(value):
            image = at_nodes(ends_out, terms * difference(ends_in, value))
            return pick_right(image, over_b) + anchor * value

        residual = pick_right(at_nodes(ends_out, terms), slopes_out)
        diagonal = pick_right(at_nodes(ends_abs, terms), diagonal_out) + anchor
        inverse = 1.0 / diagonal
        scaled = residual * inverse
        image = apply_system(scaled)
        second = image * inverse

        own_diff = difference(ends_in[REACH * 32 : REACH * 32 + 32], second)
        first_row = as_select(
            (lax.shift_right_logical(from_lane, 6) == to_half)
            & (from_a == 0)
            & (from_b == to_a)
            & (to_a < 6)
        )
        own_diff_a = pick_right(own_diff, first_row)
        quad = (terms[REACH * 32 : REACH * 32 + 32] * own_diff) * own_diff_a

        def inner(a, b):
            return jnp.sum(jnp.where(own_nodes, a * b, 0.0), keepdims=True)

        energy = inner(residual, scaled)
        curve = inner(scaled, image)
        cross = inner(second, image)
        bend = inner(anchor * second, second) + jnp.sum(quad, keepdims=True)
        sums_row = jnp.zeros((1, 128), F32)
        for number, value in enumerate((energy, curve, cross, bend)):
            sums_row = jnp.where(lane_row == number, value, sums_row)

        def exchange(value, buffer, spot, count, send, recv, partners):
            buffer[step, pl.ds(spot, 1)] = value.reshape(1, 1, 128)
            own = buffer.at[step, pl.ds(spot, 1)]
            push(
                [(own, buffer.at[step, pl.ds(at, 1)], device) for device, at in partners],
                send.at[step],
                recv.at[step],
            )
            others = whole(
                buffer.at[step, pl.ds(0, count - 1)], send.at[step], recv.at[step]
            )
            others.wait_recv()
            started.append(others)
            return jnp.sum(buffer[step].reshape(count, 128), axis=0, keepdims=True)

        scaled_turned = scaled.T[:8]
        second_turned = second.T[:8]
        sums_row = exchange(
            sums_row, far, sub, groups, far_send, far_recv, sum_partners
        )
        energy, curve, cross, bend = [sums_row[:, k : k + 1] for k in range(4)]
        step_one = energy / curve
        renewed = step_one * step_one * cross - energy
        ratio = renewed / energy
        curve_two = (
            curve
            - 2.0 * step_one * cross
            + step_one * step_one * bend
            + 2.0 * ratio * (curve - step_one * cross)
            + ratio * ratio * curve
        )
        step_two = renewed / curve_two
        increment = (step_one + step_two * (1.0 + ratio)) * scaled_turned - (
            step_two * step_one
        ) * second_turned
        inc = [increment[k : k + 1] for k in range(6)]
        turn_mat = cayley(0.5 * inc[0], 0.5 * inc[1], 0.5 * inc[2])
        rotated = [
            turn_mat[3 * i] * pose[j]
            + turn_mat[3 * i + 1] * pose[3 + j]
            + turn_mat[3 * i + 2] * pose[6 + j]
            for i in range(3)
            for j in range(3)
        ]
        moved = [
            turn_mat[3 * i] * pose[9]
            + turn_mat[3 * i + 1] * pose[10]
            + turn_mat[3 * i + 2] * pose[11]
            + inc[3 + i]
            for i in range(3)
        ]
        pose = rotated + moved

    final = jnp.concatenate(pose + [jnp.zeros((4, 128), F32)], axis=0)
    final = pltpu.roll(final, 128 - (REACH * 16 + dom * SCAN_DEV), 1)
    out_ref[...] = final.T[:SCAN_DEV, :12]

    for copy in started:
        copy.wait_send()


def local(groups, source_points, boundary, poses, anchor, edge_target, corr_tile, corr_source, corr_lane):
    vmem = pl.BlockSpec(memory_space=pltpu.VMEM)
    smem = pl.BlockSpec(memory_space=pltpu.SMEM)
    hbm = pl.BlockSpec(memory_space=pl.ANY)
    dma = pltpu.SemaphoreType.DMA
    return pl.pallas_call(
        functools.partial(kernel, groups),
        out_shape=jax.ShapeDtypeStruct((SCAN_DEV, 12), F32),
        in_specs=[hbm, hbm, hbm, smem, smem, smem, hbm, hbm],
        out_specs=vmem,
        scratch_shapes=[
            pltpu.VMEM(corr_source.shape, jnp.int32),
            pltpu.VMEM(corr_lane.shape, jnp.int32),
            pltpu.VMEM((3, SCAN_DEV, source_points.shape[2]), F32),
            pltpu.VMEM(poses.shape, F32),
            pltpu.VMEM((12 * ROWS + 16, 128), F32),
            pltpu.VMEM((PAD, 1, 128), F32),
            pltpu.VMEM((GN_ITERS, PAD, 8, 128), F32),
            pltpu.VMEM((GN_ITERS, groups, 1, 128), F32),
            pltpu.VMEM((3, 64, 128), F32),
            pltpu.VMEM((512, 128), F32),
            pltpu.VMEM((9, CT, EDGES, 128), F32),
            pltpu.VMEM((PAD * 8, 256), F32),
            dma((11, PARTS)),
            dma((12, PARTS)),
            dma,
            dma,
            dma((GN_ITERS,)),
            dma((GN_ITERS,)),
            dma((GN_ITERS,)),
            dma((GN_ITERS,)),
            dma((5,)),
        ],
        compiler_params=pltpu.CompilerParams(collective_id=0, has_side_effects=True),
    )(
        source_points.transpose(1, 0, 2),
        boundary.transpose(0, 2, 1, 3).reshape(ROWS, 128),
        poses,
        anchor,
        edge_target,
        corr_tile,
        corr_source,
        corr_lane,
    ).T


def solution(mesh):
    both = ("sub", "dom")
    return jax.shard_map(
        functools.partial(local, mesh.shape["sub"]),
        mesh=mesh,
        in_specs=(
            P(both, None, None),
            P(both, None, None, None),
            P(),
            P(both),
            P(both, None),
            P(both, None, None),
            P(both, None, None, None),
            P(both, None, None, None),
        ),
        out_specs=P(None, both),
        check_vma=False,
    )
```

```python
import functools

import jax
import jax.numpy as jnp
from jax import lax
from jax.experimental import pallas as pl
from jax.experimental.pallas import tpu as pltpu
from jax.sharding import PartitionSpec as P

MESH = pl.DeviceIdType.MESH
F32 = jnp.float32
BF16 = jnp.bfloat16
GN_ITERS = 2
SCAN_DEV = 4
EDGE_SCAN = 4
CT = 4
EDGES = SCAN_DEV * EDGE_SCAN
REACH = 3
SLOTS = 2 * REACH + 1
TILES = 4 * SLOTS
PAD = 32
SAMPLES = CT * 128
ROWS = SCAN_DEV * 6 * 8
PARTS = 2
PART = ROWS // PARTS
PAIRS = [(a, b) for a in range(6) for b in range(a, 6)]


def iota(shape, dim):
    return lax.broadcasted_iota(jnp.int32, shape, dim)


def parts_of(value, count=2):
    parts = []
    for _ in range(count):
        parts.append(value.astype(BF16))
        value = value - parts[-1].astype(F32)
    return parts[::-1]


def dot(a, b):
    return jnp.dot(a, b, preferred_element_type=F32)


def pick_left(select, value):
    second, first = parts_of(value)
    return dot(select, second) + dot(select, first)


def pick_right(value, select):
    second, first = parts_of(value)
    return dot(second, select) + dot(first, select)


def pick_turned(select, value):
    turned = (((1,), (1,)), ((), ()))
    third, second, first = [
        lax.dot_general(select, part, turned, preferred_element_type=F32)
        for part in parts_of(value, 3)
    ]
    return (third + second) + first


def cayley(first, second, third):
    length_sq = first * first + second * second + third * third
    inverse = 1.0 / (1.0 + length_sq)
    trace_part = 1.0 - length_sq
    entries = [
        trace_part + 2.0 * first * first,
        2.0 * first * second - 2.0 * third,
        2.0 * first * third + 2.0 * second,
        2.0 * first * second + 2.0 * third,
        trace_part + 2.0 * second * second,
        2.0 * second * third - 2.0 * first,
        2.0 * first * third - 2.0 * second,
        2.0 * second * third + 2.0 * first,
        trace_part + 2.0 * third * third,
    ]
    return [entry * inverse for entry in entries]


def kernel(
    groups,
    source_hbm,
    boundary_hbm,
    poses_hbm,
    anchor_ref,
    target_ref,
    tile_ref,
    corr_source_hbm,
    corr_lane_hbm,
    out_ref,
    corr_source_ref,
    corr_lane_ref,
    source_ref,
    poses_ref,
    window,
    early,
    gram,
    far,
    picked,
    chosen,
    comps,
    ends,
    win_send,
    win_recv,
    early_send,
    early_recv,
    gram_send,
    gram_recv,
    far_send,
    far_recv,
    load_sem,
    word,
):
    sub = lax.axis_index("sub")
    dom = lax.axis_index("dom")
    half_groups = groups // 2
    sub_low = lax.rem(sub, half_groups)
    sub_high = sub // half_groups

    def near_by(offset):
        return lax.rem(sub + offset + groups, groups)

    halo_partners = [
        ((near_by(offset), lax.bitwise_xor(dom, other)), (REACH - offset) * 4 + dom)
        for distance in range(REACH, -1, -1)
        for offset in ((distance, -distance) if distance else (0,))
        for other in range(4)
        if distance or other
    ]
    sum_partners = [
        ((sub_high * half_groups + lax.rem(sub_low + turn, half_groups), dom), sub)
        for turn in range(1, half_groups)
    ] + [
        (
            (
                (1 - sub_high) * half_groups + lax.rem(sub_low + turn, half_groups),
                lax.bitwise_xor(dom, 2),
            ),
            sub,
        )
        for turn in range(half_groups)
    ]

    loads = [
        pltpu.make_async_copy(source, target, load_sem.at[number])
        for number, (source, target) in enumerate(
            (
                (boundary_hbm, window.at[pl.ds((4 + dom) * ROWS, ROWS)]),
                (corr_source_hbm, corr_source_ref),
                (source_hbm, source_ref),
                (poses_hbm, poses_ref),
                (corr_lane_hbm, corr_lane_ref),
            )
        )
    ]
    for load in loads:
        load.start()
    barrier = pltpu.get_barrier_semaphore()
    z_size = groups // 8
    z_spot = lax.rem(sub, z_size)
    y_spot = lax.rem(sub // z_size, 4)
    z_line = [
        (sub - z_spot + lax.rem(z_spot + turn, z_size), dom) for turn in range(1, z_size)
    ]
    y_line = [
        (
            sub_high * half_groups + lax.rem(y_spot + turn, 4) * z_size + z_spot,
            dom,
        )
        for turn in range(1, 4)
    ]
    x_line = [((1 - sub_high) * half_groups + sub_low, lax.bitwise_xor(dom, 2))]

    def signal_all(semaphore, devices):
        for device in devices:
            pl.semaphore_signal(semaphore, inc=1, device_id=device, device_id_type=MESH)

    greeted = [device for device, _ in halo_partners] + z_line + y_line + x_line
    signal_all(barrier, greeted)

    pl.semaphore_wait(barrier, len(greeted))
    started = []

    def push(copies, send_sem, recv_sem):
        for source, target, device in copies:
            pltpu.make_async_remote_copy(
                src_ref=source,
                dst_ref=target,
                send_sem=send_sem,
                recv_sem=recv_sem,
                device_id=device,
                device_id_type=MESH,
            ).start()

    def whole(ref, send_sem, recv_sem):
        return pltpu.make_async_remote_copy(
            src_ref=ref,
            dst_ref=ref,
            send_sem=send_sem,
            recv_sem=recv_sem,
            device_id=(sub, lax.bitwise_xor(dom, 1)),
            device_id_type=MESH,
        )

    own_slot = REACH * 4 + dom

    def halo_push(buffer, send, recv):
        own = buffer.at[pl.ds(own_slot, 1)]
        push(
            [(own, buffer.at[pl.ds(slot, 1)], device) for device, slot in halo_partners],
            send,
            recv,
        )
        return whole(buffer.at[pl.ds(0, TILES - 1)], send, recv)

    loads[0].wait()
    sibling = lax.bitwise_xor(dom, 1)
    across = lax.bitwise_xor(dom, 2)
    to_sibling = (sub, sibling)
    to_across = (sub, across)

    to_next = lax.bitwise_xor(dom, 2 * (sub_low // (half_groups - 1)))
    to_last = lax.bitwise_xor(dom, 2 * (lax.rem(sub_low + half_groups - 1, half_groups) // (half_groups - 1)))

    def window_copy(number, part, slot, device):
        at = window.at[pl.ds(slot * ROWS + part * PART, PART)]
        return pltpu.make_async_remote_copy(
            src_ref=at,
            dst_ref=at,
            send_sem=win_send.at[number, part],
            recv_sem=win_recv.at[slot, part],
            device_id=device,
            device_id_type=MESH,
        )

    def window_copy_to(number, part, slot, slot_there, device):
        at = window.at[pl.ds(slot * ROWS + part * PART, PART)]
        there = window.at[pl.ds(slot_there * ROWS + part * PART, PART)]
        return pltpu.make_async_remote_copy(
            src_ref=at,
            dst_ref=there,
            send_sem=win_send.at[number, part],
            recv_sem=win_recv.at[slot_there, part],
            device_id=device,
            device_id_type=MESH,
        )

    def window_send(number, part, slot, device, slot_there=None):
        slot_there = slot if slot_there is None else slot_there
        copy = window_copy_to(number, part, slot, slot_there, device)
        copy.start()
        started.append(copy)

    def window_wait(part, slot):
        window_copy(0, part, slot, to_sibling).wait_recv()

    for part in range(PARTS):
        window_send(0, part, 4 + dom, (near_by(1), to_next), dom)
        window_send(1, part, 4 + dom, (near_by(-1), to_last), 8 + dom)
    for part in range(PARTS):
        window_send(2, part, 4 + dom, to_across)
    for part in range(PARTS):
        window_send(3, part, 4 + dom, to_sibling)
    lane_row = iota((1, 128), 1)
    row = jnp.zeros((1, 128), F32)
    edge_of_row = iota((EDGES, 128), 0)
    own_target = jnp.zeros((EDGES, 128), jnp.int32)
    for edge in range(EDGES):
        value = target_ref[edge // EDGE_SCAN, edge % EDGE_SCAN]
        row = jnp.where(lane_row == edge, value.astype(F32), row)
        own_target = jnp.where(edge_of_row == edge, value, own_target)
    for scan in range(SCAN_DEV):
        row = jnp.where(lane_row == EDGES + scan, anchor_ref[scan], row)
    early[pl.ds(own_slot, 1)] = row.reshape(1, 1, 128)
    early_copies = halo_push(early, early_send, early_recv)
    signal_all(word.at[0], y_line)
    started.append(early_copies)
    early[pl.ds(TILES, 4)] = jnp.zeros((4, 1, 128), F32)
    for step in range(GN_ITERS):
        gram[step, pl.ds(TILES, 4)] = jnp.zeros((4, 8, 128), F32)

    def gather_scan(scan):
        indices = corr_source_ref[scan].reshape(EDGE_SCAN * CT, 128)
        low = lax.bitwise_and(indices, 127)
        high = lax.shift_right_logical(indices, 7)

        def gather_blocks(group, found):
            found = list(found)
            for number in range(8):
                block = group * 8 + number
                here = high == block
                for comp in range(3):
                    at = pl.multiple_of(block * 128, 128)
                    line = source_ref[comp, pl.ds(scan, 1), pl.ds(at, 128)]
                    wide = jnp.broadcast_to(line, (EDGE_SCAN * CT, 128))
                    value = jnp.take_along_axis(wide, low, axis=1, mode="promise_in_bounds")
                    found[comp] = jnp.where(here, value, found[comp])
            return tuple(found)

        empty = jnp.zeros((EDGE_SCAN * CT, 128), F32)
        found = lax.fori_loop(0, 4, gather_blocks, (empty, empty, empty))
        for comp in range(3):
            picked[comp, pl.ds(scan * 16, 16), :] = found[comp]

    loads[1].wait()
    loads[2].wait()
    for part in range(PARTS):
        gather_scan(part)
        for number, slot in ((4, to_last), (5, 8 + to_next)):
            window_wait(part, slot)
            window_send(number, part, slot, to_across)
            window_send(number + 2, part, slot, to_sibling)
        window_wait(part, 4 + across)
        window_send(8, part, 4 + across, to_sibling)
    pl.semaphore_wait(word.at[0], len(y_line))
    signal_all(word.at[1], x_line)
    gather_scan(2)
    gather_scan(3)
    for part in range(PARTS):
        for number, slot in (
            (9, lax.bitwise_xor(to_last, 2)),
            (10, 8 + lax.bitwise_xor(to_next, 2)),
        ):
            window_wait(part, slot)
            window_send(number, part, slot, to_sibling)

    loads[3].wait()
    start = near_by(-REACH) * 16
    first_tile = start // 128
    next_tile = lax.rem(first_tile + 1, groups * 16 // 128)
    pair = jnp.concatenate(
        [
            poses_ref[:, pl.ds(pl.multiple_of(first_tile * 128, 128), 128)],
            poses_ref[:, pl.ds(pl.multiple_of(next_tile * 128, 128), 128)],
        ],
        axis=1,
    )
    shift = lax.rem(256 - lax.rem(start, 128), 256)
    rolled = pltpu.roll(pair, shift, 1)[:, :128]
    pose = [rolled[k : k + 1] for k in range(12)]

    lane16 = iota((EDGES, 128), 1)
    own_source_lane = REACH * 16 + dom * SCAN_DEV + edge_of_row // EDGE_SCAN
    own_ends = jnp.concatenate(
        [
            (lane16 == own_source_lane).astype(F32),
            (lane16 == own_target + (REACH - 1) * 16).astype(F32),
        ],
        axis=0,
    ).astype(BF16)

    from_lane = iota((128, 128), 0)
    to_lane = iota((128, 128), 1)
    from_a = lax.shift_right_logical(from_lane, 3) & 7
    from_b = from_lane & 7
    to_half = lax.shift_right_logical(to_lane, 6)
    to_a = lax.shift_right_logical(to_lane, 3) & 7
    to_b = to_lane & 7
    used = (to_a < 6) & (to_b < 6) & (from_b < 6)
    as_select = lambda mask: mask.astype(F32).astype(BF16)
    over_b = as_select(used & (from_a == to_b))
    slopes_out = as_select(used & (from_a == 6) & (from_b == to_b))
    diagonal_out = as_select(used & (from_a == from_b) & (from_b == to_b))
    left = to_half == 0
    left_256 = iota((256, 128), 1) < 64

    early_copies.wait_recv()
    rows = early[...].reshape(PAD, 128)
    rows_turned = jnp.concatenate([rows, jnp.zeros((128 - PAD, 128), F32)], axis=0).T
    lane8 = iota((8, 128), 1)
    row8 = iota((8, 128), 0)
    for tile in range(TILES):
        for half in range(2):
            target = rows_turned[half * 8 : half * 8 + 8, tile : tile + 1]
            target_lane = target + float((tile // 4 - 1) * 16)
            source_lane = tile * 4 + half * 2 + row8 // 4
            ends[pl.ds(tile * 8, 8), pl.ds(half * 128, 128)] = (
                lane8 == source_lane
            ).astype(F32) - (lane8.astype(F32) == target_lane).astype(F32)
    ends[pl.ds(TILES * 8, (PAD - TILES) * 8), :] = jnp.zeros(((PAD - TILES) * 8, 256), F32)
    ends_f32 = ends[...]
    ends_turned_f32 = ends_f32.T
    ends_in = ends_f32.astype(BF16)
    ends_out = ends_turned_f32.astype(BF16)
    ends_abs = jnp.abs(ends_turned_f32).astype(BF16)
    node = iota((128, PAD), 0)
    of_tile = as_select(node // 4 == iota((128, PAD), 1))
    anchor_rows = pick_left(of_tile, rows)
    node_128 = from_lane
    mine = to_lane == EDGES + (node_128 & 3)
    anchor = jnp.sum(jnp.where(mine, anchor_rows, 0.0), axis=1, keepdims=True)
    anchor = jnp.where(node_128 < TILES * 4, jnp.broadcast_to(anchor, (128, 128)), 1.0)
    own_nodes = (node_128 // 16 == REACH) & (to_lane < 6)

    for part in range(PARTS):
        for other in (sibling, lax.bitwise_xor(dom, 3)):
            for offset in range(3):
                window_wait(part, offset * 4 + other)
    pl.semaphore_wait(word.at[1], len(x_line))
    loads[4].wait()

    def gather_edge(edge, carry):
        scan = edge // EDGE_SCAN
        slot = lax.rem(edge, EDGE_SCAN)
        first = target_ref[scan, slot] * 48
        lanes = corr_lane_ref[scan, slot]
        for chunk in range(CT):
            tile = window[pl.ds(first + tile_ref[scan, slot, chunk], 8, stride=8), :]
            spread = jnp.broadcast_to(lanes[chunk : chunk + 1], (8, 128))
            value = jnp.take_along_axis(tile, spread, axis=1, mode="promise_in_bounds")
            chosen[pl.ds(pl.multiple_of(edge * 32 + chunk * 8, 8), 8), :] = value
        return carry

    lax.fori_loop(0, EDGES, gather_edge, 0, unroll=True)
    for chunk in range(CT):
        for comp in range(3):
            comps[comp, chunk] = picked[comp, pl.ds(chunk, EDGES, stride=CT), :]
        for comp in range(6):
            comps[3 + comp, chunk] = chosen[pl.ds(chunk * 8 + comp, EDGES, stride=32), :]

    msg_pos = lane8 & 63

    for step in range(GN_ITERS):
        pose_rows = jnp.concatenate(pose + [jnp.zeros((4, 128), F32)], axis=0)
        pose_ends = pick_turned(own_ends, pose_rows)
        message = jnp.zeros((8, 128), F32)
        for half in range(2):
            here = [
                jnp.broadcast_to(pose_ends[half * 8 : half * 8 + 8, k : k + 1], (8, 128))
                for k in range(12)
            ]
            there = [
                jnp.broadcast_to(
                    pose_ends[EDGES + half * 8 : EDGES + half * 8 + 8, k : k + 1], (8, 128)
                )
                for k in range(12)
            ]
            sums = {}
            for chunk in range(CT):
                data = [comps[k, chunk, pl.ds(half * 8, 8), :] for k in range(9)]

                def turn(matrix, vector):
                    return [
                        matrix[3 * i] * vector[0]
                        + matrix[3 * i + 1] * vector[1]
                        + matrix[3 * i + 2] * vector[2]
                        for i in range(3)
                    ]

                placed = [v + t for v, t in zip(turn(here[:9], data[0:3]), here[9:])]
                target = [v + t for v, t in zip(turn(there[:9], data[3:6]), there[9:])]
                normal = turn(there[:9], data[6:9])
                offset = [q - p for q, p in zip(target, placed)]
                misfit = normal[0] * offset[0] + normal[1] * offset[1] + normal[2] * offset[2]
                jac = [
                    placed[1] * normal[2] - placed[2] * normal[1],
                    placed[2] * normal[0] - placed[0] * normal[2],
                    placed[0] * normal[1] - placed[1] * normal[0],
                ] + normal
                for a, b in PAIRS:
                    term = jac[a] * jac[b]
                    sums[a, b] = sums[a, b] + term if chunk else term
                for b in range(6):
                    term = jac[b] * misfit
                    sums[6, b] = sums[6, b] + term if chunk else term
            in_half = lane8 // 64 == half
            for (a, b), value in sums.items():
                total = jnp.sum(value, axis=1, keepdims=True) * (1.0 / SAMPLES)
                place = msg_pos == a * 8 + b
                if a < 6:
                    place = place | (msg_pos == b * 8 + a)
                message = jnp.where(in_half & place, total, message)
        gram[step, pl.ds(own_slot, 1)] = message.reshape(1, 8, 128)
        gram_copies = halo_push(gram.at[step], gram_send.at[step], gram_recv.at[step])
        started.append(gram_copies)
        gram_copies.wait_recv()
        terms = gram[step].reshape(PAD * 8, 128)

        def at_nodes(select, value):
            both = pick_left(select, value)
            return jnp.where(left, both[:128], both[128:])

        def difference(select, value):
            twice = jnp.concatenate([value, value], axis=0)
            sides = iota((256, 128), 0) < 128
            return pick_left(select, jnp.where(sides == left_256, twice, 0.0))

        def apply_system(value):
            image = at_nodes(ends_out, terms * difference(ends_in, value))
            return pick_right(image, over_b) + anchor * value

        residual = pick_right(at_nodes(ends_out, terms), slopes_out)
        diagonal = pick_right(at_nodes(ends_abs, terms), diagonal_out) + anchor
        inverse = 1.0 / diagonal
        scaled = residual * inverse
        image = apply_system(scaled)
        second = image * inverse

        own_diff = difference(ends_in[REACH * 32 : REACH * 32 + 32], second)
        first_row = as_select(
            (lax.shift_right_logical(from_lane, 6) == to_half)
            & (from_a == 0)
            & (from_b == to_a)
            & (to_a < 6)
        )
        own_diff_a = pick_right(own_diff, first_row)
        quad = (terms[REACH * 32 : REACH * 32 + 32] * own_diff) * own_diff_a

        def inner(a, b):
            return jnp.sum(jnp.where(own_nodes, a * b, 0.0), keepdims=True)

        energy = inner(residual, scaled)
        curve = inner(scaled, image)
        cross = inner(second, image)
        bend = inner(anchor * second, second) + jnp.sum(quad, keepdims=True)
        sums_row = jnp.zeros((1, 128), F32)
        for number, value in enumerate((energy, curve, cross, bend)):
            sums_row = jnp.where(lane_row == number, value, sums_row)

        def exchange(value, buffer, spot, count, send, recv, partners):
            buffer[step, pl.ds(spot, 1)] = value.reshape(1, 1, 128)
            own = buffer.at[step, pl.ds(spot, 1)]
            push(
                [(own, buffer.at[step, pl.ds(at, 1)], device) for device, at in partners],
                send.at[step],
                recv.at[step],
            )
            others = whole(
                buffer.at[step, pl.ds(0, count - 1)], send.at[step], recv.at[step]
            )
            others.wait_recv()
            started.append(others)
            return jnp.sum(buffer[step].reshape(count, 128), axis=0, keepdims=True)

        scaled_turned = scaled.T[:8]
        second_turned = second.T[:8]
        sums_row = exchange(
            sums_row, far, sub, groups, far_send, far_recv, sum_partners
        )
        energy, curve, cross, bend = [sums_row[:, k : k + 1] for k in range(4)]
        step_one = energy / curve
        renewed = step_one * step_one * cross - energy
        ratio = renewed / energy
        curve_two = (
            curve
            - 2.0 * step_one * cross
            + step_one * step_one * bend
            + 2.0 * ratio * (curve - step_one * cross)
            + ratio * ratio * curve
        )
        step_two = renewed / curve_two
        increment = (step_one + step_two * (1.0 + ratio)) * scaled_turned - (
            step_two * step_one
        ) * second_turned
        inc = [increment[k : k + 1] for k in range(6)]
        turn_mat = cayley(0.5 * inc[0], 0.5 * inc[1], 0.5 * inc[2])
        rotated = [
            turn_mat[3 * i] * pose[j]
            + turn_mat[3 * i + 1] * pose[3 + j]
            + turn_mat[3 * i + 2] * pose[6 + j]
            for i in range(3)
            for j in range(3)
        ]
        moved = [
            turn_mat[3 * i] * pose[9]
            + turn_mat[3 * i + 1] * pose[10]
            + turn_mat[3 * i + 2] * pose[11]
            + inc[3 + i]
            for i in range(3)
        ]
        pose = rotated + moved

    final = jnp.concatenate(pose + [jnp.zeros((4, 128), F32)], axis=0)
    final = pltpu.roll(final, 128 - (REACH * 16 + dom * SCAN_DEV), 1)
    out_ref[...] = final.T[:SCAN_DEV, :12]

    for copy in started:
        copy.wait_send()


def local(groups, source_points, boundary, poses, anchor, edge_target, corr_tile, corr_source, corr_lane):
    vmem = pl.BlockSpec(memory_space=pltpu.VMEM)
    smem = pl.BlockSpec(memory_space=pltpu.SMEM)
    hbm = pl.BlockSpec(memory_space=pl.ANY)
    dma = pltpu.SemaphoreType.DMA
    return pl.pallas_call(
        functools.partial(kernel, groups),
        out_shape=pltpu.VMEM((SCAN_DEV, 12), F32),
        in_specs=[hbm, hbm, hbm, smem, smem, smem, hbm, hbm],
        out_specs=vmem,
        scratch_shapes=[
            pltpu.VMEM(corr_source.shape, jnp.int32),
            pltpu.VMEM(corr_lane.shape, jnp.int32),
            pltpu.VMEM((3, SCAN_DEV, source_points.shape[2]), F32),
            pltpu.VMEM(poses.shape, F32),
            pltpu.VMEM((12 * ROWS + 16, 128), F32),
            pltpu.VMEM((PAD, 1, 128), F32),
            pltpu.VMEM((GN_ITERS, PAD, 8, 128), F32),
            pltpu.VMEM((GN_ITERS, groups, 1, 128), F32),
            pltpu.VMEM((3, 64, 128), F32),
            pltpu.VMEM((512, 128), F32),
            pltpu.VMEM((9, CT, EDGES, 128), F32),
            pltpu.VMEM((PAD * 8, 256), F32),
            dma((11, PARTS)),
            dma((12, PARTS)),
            dma,
            dma,
            dma((GN_ITERS,)),
            dma((GN_ITERS,)),
            dma((GN_ITERS,)),
            dma((GN_ITERS,)),
            dma((5,)),
            pltpu.SemaphoreType.REGULAR((2,)),
        ],
        compiler_params=pltpu.CompilerParams(collective_id=0, has_side_effects=True),
    )(
        source_points.transpose(1, 0, 2),
        boundary.transpose(0, 2, 1, 3).reshape(ROWS, 128),
        poses,
        anchor,
        edge_target,
        corr_tile,
        corr_source,
        corr_lane,
    ).T


def solution(mesh):
    both = ("sub", "dom")
    return jax.shard_map(
        functools.partial(local, mesh.shape["sub"]),
        mesh=mesh,
        in_specs=(
            P(both, None, None),
            P(both, None, None, None),
            P(),
            P(both),
            P(both, None),
            P(both, None, None),
            P(both, None, None, None),
            P(both, None, None, None),
        ),
        out_specs=P(None, both),
        check_vma=False,
    )
```

```python
import functools

import jax
import jax.numpy as jnp
from jax import lax
from jax.experimental import pallas as pl
from jax.experimental.pallas import tpu as pltpu
from jax.sharding import PartitionSpec as P

MESH = pl.DeviceIdType.MESH
F32 = jnp.float32
BF16 = jnp.bfloat16
GN_ITERS = 2
SCAN_DEV = 4
EDGE_SCAN = 4
CT = 4
EDGES = SCAN_DEV * EDGE_SCAN
REACH = 3
SLOTS = 2 * REACH + 1
TILES = 4 * SLOTS
PAD = 32
SAMPLES = CT * 128
ROWS = SCAN_DEV * 6 * 8
PARTS = 2
PART = ROWS // PARTS
PAIRS = [(a, b) for a in range(6) for b in range(a, 6)]


def iota(shape, dim):
    return lax.broadcasted_iota(jnp.int32, shape, dim)


def parts_of(value, count=2):
    parts = []
    for _ in range(count):
        parts.append(value.astype(BF16))
        value = value - parts[-1].astype(F32)
    return parts[::-1]


def dot(a, b):
    return jnp.dot(a, b, preferred_element_type=F32)


def rows_times(value, select):
    stacked = jnp.concatenate([part.astype(F32) for part in parts_of(value, 3)], axis=0)
    product = dot(stacked.astype(BF16), select)
    return (product[0:8] + product[8:16]) + product[16:24]


def regroup(tiles):
    group = lax.shift_right_logical(iota((8, 128), 1), 4)
    for bit in range(3):
        size = 1 << bit
        low = lax.bitwise_and(group, size) == 0
        tiles = list(tiles)
        for first in range(8):
            if first & size:
                continue
            one, two = tiles[first], tiles[first + size]
            tiles[first] = jnp.where(low, one, pltpu.roll(two, size * 16, 1))
            tiles[first + size] = jnp.where(low, pltpu.roll(one, 128 - size * 16, 1), two)
    return tiles


def pick_turned(select, value):
    turned = (((1,), (1,)), ((), ()))
    third, second, first = [
        lax.dot_general(select, part, turned, preferred_element_type=F32)
        for part in parts_of(value, 3)
    ]
    return (third + second) + first


def cayley(first, second, third):
    length_sq = first * first + second * second + third * third
    inverse = 1.0 / (1.0 + length_sq)
    trace_part = 1.0 - length_sq
    entries = [
        trace_part + 2.0 * first * first,
        2.0 * first * second - 2.0 * third,
        2.0 * first * third + 2.0 * second,
        2.0 * first * second + 2.0 * third,
        trace_part + 2.0 * second * second,
        2.0 * second * third - 2.0 * first,
        2.0 * first * third - 2.0 * second,
        2.0 * second * third + 2.0 * first,
        trace_part + 2.0 * third * third,
    ]
    return [entry * inverse for entry in entries]


def kernel(
    groups,
    source_hbm,
    boundary_hbm,
    poses_hbm,
    anchor_ref,
    target_ref,
    tile_ref,
    corr_source_hbm,
    corr_lane_hbm,
    out_ref,
    corr_source_ref,
    corr_lane_ref,
    source_ref,
    poses_ref,
    window,
    early,
    gram,
    far,
    picked,
    chosen,
    comps,
    ends,
    win_send,
    win_recv,
    early_send,
    early_recv,
    gram_send,
    gram_recv,
    far_send,
    far_recv,
    load_sem,
    word,
):
    sub = lax.axis_index("sub")
    dom = lax.axis_index("dom")
    half_groups = groups // 2
    sub_low = lax.rem(sub, half_groups)
    sub_high = sub // half_groups

    def near_by(offset):
        return lax.rem(sub + offset + groups, groups)

    halo_partners = [
        ((near_by(offset), lax.bitwise_xor(dom, other)), (REACH - offset) * 4 + dom)
        for distance in range(REACH, -1, -1)
        for offset in ((distance, -distance) if distance else (0,))
        for other in range(4)
        if distance or other
    ]
    sum_partners = [
        ((sub_high * half_groups + lax.rem(sub_low + turn, half_groups), dom), sub)
        for turn in range(1, half_groups)
    ] + [
        (
            (
                (1 - sub_high) * half_groups + lax.rem(sub_low + turn, half_groups),
                lax.bitwise_xor(dom, 2),
            ),
            sub,
        )
        for turn in range(half_groups)
    ]

    loads = [
        pltpu.make_async_copy(source, target, load_sem.at[number])
        for number, (source, target) in enumerate(
            (
                (boundary_hbm, window.at[pl.ds((4 + dom) * ROWS, ROWS)]),
                (corr_source_hbm, corr_source_ref),
                (source_hbm, source_ref),
                (poses_hbm, poses_ref),
                (corr_lane_hbm, corr_lane_ref),
            )
        )
    ]
    for load in loads:
        load.start()
    barrier = pltpu.get_barrier_semaphore()
    z_size = groups // 8
    z_spot = lax.rem(sub, z_size)
    y_spot = lax.rem(sub // z_size, 4)
    z_line = [
        (sub - z_spot + lax.rem(z_spot + turn, z_size), dom) for turn in range(1, z_size)
    ]
    y_line = [
        (
            sub_high * half_groups + lax.rem(y_spot + turn, 4) * z_size + z_spot,
            dom,
        )
        for turn in range(1, 4)
    ]
    x_line = [((1 - sub_high) * half_groups + sub_low, lax.bitwise_xor(dom, 2))]

    def signal_all(semaphore, devices):
        for device in devices:
            pl.semaphore_signal(semaphore, inc=1, device_id=device, device_id_type=MESH)

    greeted = [device for device, _ in halo_partners] + z_line + y_line + x_line
    signal_all(barrier, greeted)

    pl.semaphore_wait(barrier, len(greeted))
    started = []

    def push(copies, send_sem, recv_sem):
        for source, target, device in copies:
            pltpu.make_async_remote_copy(
                src_ref=source,
                dst_ref=target,
                send_sem=send_sem,
                recv_sem=recv_sem,
                device_id=device,
                device_id_type=MESH,
            ).start()

    def whole(ref, send_sem, recv_sem):
        return pltpu.make_async_remote_copy(
            src_ref=ref,
            dst_ref=ref,
            send_sem=send_sem,
            recv_sem=recv_sem,
            device_id=(sub, lax.bitwise_xor(dom, 1)),
            device_id_type=MESH,
        )

    own_slot = REACH * 4 + dom

    def halo_push(buffer, send, recv):
        own = buffer.at[pl.ds(own_slot, 1)]
        push(
            [(own, buffer.at[pl.ds(slot, 1)], device) for device, slot in halo_partners],
            send,
            recv,
        )
        return whole(buffer.at[pl.ds(0, TILES - 1)], send, recv)

    loads[0].wait()
    sibling = lax.bitwise_xor(dom, 1)
    across = lax.bitwise_xor(dom, 2)
    to_sibling = (sub, sibling)
    to_across = (sub, across)

    to_next = lax.bitwise_xor(dom, 2 * (sub_low // (half_groups - 1)))
    to_last = lax.bitwise_xor(dom, 2 * (lax.rem(sub_low + half_groups - 1, half_groups) // (half_groups - 1)))

    def window_copy(number, part, slot, device):
        at = window.at[pl.ds(slot * ROWS + part * PART, PART)]
        return pltpu.make_async_remote_copy(
            src_ref=at,
            dst_ref=at,
            send_sem=win_send.at[number, part],
            recv_sem=win_recv.at[slot, part],
            device_id=device,
            device_id_type=MESH,
        )

    def window_copy_to(number, part, slot, slot_there, device):
        at = window.at[pl.ds(slot * ROWS + part * PART, PART)]
        there = window.at[pl.ds(slot_there * ROWS + part * PART, PART)]
        return pltpu.make_async_remote_copy(
            src_ref=at,
            dst_ref=there,
            send_sem=win_send.at[number, part],
            recv_sem=win_recv.at[slot_there, part],
            device_id=device,
            device_id_type=MESH,
        )

    def window_send(number, part, slot, device, slot_there=None):
        slot_there = slot if slot_there is None else slot_there
        copy = window_copy_to(number, part, slot, slot_there, device)
        copy.start()
        started.append(copy)

    def window_wait(part, slot):
        window_copy(0, part, slot, to_sibling).wait_recv()

    for part in range(PARTS):
        window_send(0, part, 4 + dom, (near_by(1), to_next), dom)
        window_send(1, part, 4 + dom, (near_by(-1), to_last), 8 + dom)
    for part in range(PARTS):
        window_send(2, part, 4 + dom, to_across)
    for part in range(PARTS):
        window_send(3, part, 4 + dom, to_sibling)
    lane_row = iota((1, 128), 1)
    row = jnp.zeros((1, 128), F32)
    edge_of_row = iota((EDGES, 128), 0)
    own_target = jnp.zeros((EDGES, 128), jnp.int32)
    for edge in range(EDGES):
        value = target_ref[edge // EDGE_SCAN, edge % EDGE_SCAN]
        row = jnp.where(lane_row == edge, value.astype(F32), row)
        own_target = jnp.where(edge_of_row == edge, value, own_target)
    for scan in range(SCAN_DEV):
        row = jnp.where(lane_row == EDGES + scan, anchor_ref[scan], row)
    early[pl.ds(own_slot, 1)] = row.reshape(1, 1, 128)
    early_copies = halo_push(early, early_send, early_recv)
    signal_all(word.at[0], y_line)
    started.append(early_copies)
    early[pl.ds(TILES, 4)] = jnp.zeros((4, 1, 128), F32)
    for step in range(GN_ITERS):
        gram[step, pl.ds(TILES, 4)] = jnp.zeros((4, 8, 128), F32)

    def gather_scan(scan):
        indices = corr_source_ref[scan].reshape(EDGE_SCAN * CT, 128)
        low = lax.bitwise_and(indices, 127)
        high = lax.shift_right_logical(indices, 7)

        def gather_blocks(group, found):
            found = list(found)
            for number in range(8):
                block = group * 8 + number
                here = high == block
                for comp in range(3):
                    at = pl.multiple_of(block * 128, 128)
                    line = source_ref[comp, pl.ds(scan, 1), pl.ds(at, 128)]
                    wide = jnp.broadcast_to(line, (EDGE_SCAN * CT, 128))
                    value = jnp.take_along_axis(wide, low, axis=1, mode="promise_in_bounds")
                    found[comp] = jnp.where(here, value, found[comp])
            return tuple(found)

        empty = jnp.zeros((EDGE_SCAN * CT, 128), F32)
        found = lax.fori_loop(0, 4, gather_blocks, (empty, empty, empty))
        for comp in range(3):
            picked[comp, pl.ds(scan * 16, 16), :] = found[comp]

    loads[1].wait()
    loads[2].wait()
    for part in range(PARTS):
        gather_scan(part)
        for number, slot in ((4, to_last), (5, 8 + to_next)):
            window_wait(part, slot)
            window_send(number, part, slot, to_across)
            window_send(number + 2, part, slot, to_sibling)
        window_wait(part, 4 + across)
        window_send(8, part, 4 + across, to_sibling)
    pl.semaphore_wait(word.at[0], len(y_line))
    signal_all(word.at[1], x_line)
    gather_scan(2)
    gather_scan(3)
    for part in range(PARTS):
        for number, slot in (
            (9, lax.bitwise_xor(to_last, 2)),
            (10, 8 + lax.bitwise_xor(to_next, 2)),
        ):
            window_wait(part, slot)
            window_send(number, part, slot, to_sibling)

    loads[3].wait()
    start = near_by(-REACH) * 16
    first_tile = start // 128
    next_tile = lax.rem(first_tile + 1, groups * 16 // 128)
    pair = jnp.concatenate(
        [
            poses_ref[:, pl.ds(pl.multiple_of(first_tile * 128, 128), 128)],
            poses_ref[:, pl.ds(pl.multiple_of(next_tile * 128, 128), 128)],
        ],
        axis=1,
    )
    shift = lax.rem(256 - lax.rem(start, 128), 256)
    rolled = pltpu.roll(pair, shift, 1)[:, :128]
    pose = [rolled[k : k + 1] for k in range(12)]

    lane16 = iota((EDGES, 128), 1)
    own_source_lane = REACH * 16 + dom * SCAN_DEV + edge_of_row // EDGE_SCAN
    own_ends = jnp.concatenate(
        [
            (lane16 == own_source_lane).astype(F32),
            (lane16 == own_target + (REACH - 1) * 16).astype(F32),
        ],
        axis=0,
    ).astype(BF16)

    row_of = iota((16, 6 * 128), 0) == lax.shift_right_logical(iota((16, 6 * 128), 1), 7)
    into_rows = jnp.where(row_of, 1.0, 0.0).astype(BF16)

    early_copies.wait_recv()
    rows = early[...].reshape(PAD, 128)
    rows_turned = jnp.concatenate([rows, jnp.zeros((128 - PAD, 128), F32)], axis=0).T
    lane8 = iota((8, 128), 1)
    row8 = iota((8, 128), 0)
    for tile in range(TILES):
        target = rows_turned[:EDGES, tile : tile + 1]
        target_lane = target + float((tile // 4 - 1) * 16)
        source_lane = tile * 4 + edge_of_row // EDGE_SCAN
        ends[pl.ds(tile * EDGES, EDGES), :] = (lane16 == source_lane).astype(F32) - (
            lane16.astype(F32) == target_lane
        ).astype(F32)
    ends[pl.ds(TILES * EDGES, (PAD - TILES) * EDGES), :] = jnp.zeros(
        ((PAD - TILES) * EDGES, 128), F32
    )
    ends_f32 = ends[...]
    ends_out = ends_f32.astype(BF16)
    ends_abs = jnp.abs(ends_f32).astype(BF16)
    ends_in = ends_f32.T.astype(BF16)
    of_tile = jnp.where(iota((128, 128), 0) == iota((128, 128), 1) // 4, 1.0, 0.0).astype(BF16)
    anchor_rows = rows_times(rows_turned[EDGES : EDGES + 8], of_tile)
    anchor = jnp.sum(
        jnp.where(row8 == lax.bitwise_and(lane8, 3), anchor_rows, 0.0), axis=0, keepdims=True
    )
    anchor = jnp.broadcast_to(anchor, (8, 128))
    anchor = jnp.where(lane8 < TILES * 4, anchor, 1.0)
    own_nodes = (lane8 // 16 == REACH) & (row8 < 6)
    own_edges = (lane8 >= 64) & (row8 < 6)

    for part in range(PARTS):
        for other in (sibling, lax.bitwise_xor(dom, 3)):
            for offset in range(3):
                window_wait(part, offset * 4 + other)
    pl.semaphore_wait(word.at[1], len(x_line))
    loads[4].wait()

    def gather_edge(edge, carry):
        scan = edge // EDGE_SCAN
        slot = lax.rem(edge, EDGE_SCAN)
        first = target_ref[scan, slot] * 48
        lanes = corr_lane_ref[scan, slot]
        for chunk in range(CT):
            tile = window[pl.ds(first + tile_ref[scan, slot, chunk], 8, stride=8), :]
            spread = jnp.broadcast_to(lanes[chunk : chunk + 1], (8, 128))
            value = jnp.take_along_axis(tile, spread, axis=1, mode="promise_in_bounds")
            chosen[pl.ds(pl.multiple_of(edge * 32 + chunk * 8, 8), 8), :] = value
        return carry

    lax.fori_loop(0, EDGES, gather_edge, 0, unroll=True)
    for chunk in range(CT):
        for comp in range(3):
            comps[comp, chunk] = picked[comp, pl.ds(chunk, EDGES, stride=CT), :]
        for comp in range(6):
            comps[3 + comp, chunk] = chosen[pl.ds(chunk * 8 + comp, EDGES, stride=32), :]


    for step in range(GN_ITERS):
        pose_rows = jnp.concatenate(pose + [jnp.zeros((4, 128), F32)], axis=0)
        pose_ends = pick_turned(own_ends, pose_rows)
        here = [
            jnp.broadcast_to(pose_ends[:EDGES, k : k + 1], (EDGES, 128)) for k in range(12)
        ]
        there = [
            jnp.broadcast_to(pose_ends[EDGES:, k : k + 1], (EDGES, 128)) for k in range(12)
        ]
        sums = {}
        for chunk in range(CT):
            data = [comps[k, chunk] for k in range(9)]

            def turn(matrix, vector):
                return [
                    matrix[3 * i] * vector[0]
                    + matrix[3 * i + 1] * vector[1]
                    + matrix[3 * i + 2] * vector[2]
                    for i in range(3)
                ]

            placed = [v + t for v, t in zip(turn(here[:9], data[0:3]), here[9:])]
            target = [v + t for v, t in zip(turn(there[:9], data[3:6]), there[9:])]
            normal = turn(there[:9], data[6:9])
            offset = [q - p for q, p in zip(target, placed)]
            misfit = normal[0] * offset[0] + normal[1] * offset[1] + normal[2] * offset[2]
            jac = [
                placed[1] * normal[2] - placed[2] * normal[1],
                placed[2] * normal[0] - placed[0] * normal[2],
                placed[0] * normal[1] - placed[1] * normal[0],
            ] + normal
            for a, b in PAIRS:
                term = jac[a] * jac[b]
                sums[a, b] = sums[a, b] + term if chunk else term
            for a in range(6):
                term = jac[a] * misfit
                sums[a, 6] = sums[a, 6] + term if chunk else term
        nothing = jnp.zeros((EDGES, 128), F32)
        message = None
        split = {key: parts_of(value) for key, value in sums.items()}
        for part in range(2):
            spread = jnp.concatenate(
                [
                    jnp.concatenate(
                        [split[min(a, b), max(a, b)][part] for b in range(7)]
                        + [nothing.astype(BF16)],
                        axis=0,
                    )
                    for a in range(6)
                ],
                axis=1,
            )
            term = lax.dot_general(
                into_rows, spread, (((1,), (1,)), ((), ())), preferred_element_type=F32
            )
            message = term if message is None else message + term
        message = message[:8] * (1.0 / SAMPLES)
        gram[step, pl.ds(own_slot, 1)] = message.reshape(1, 8, 128)
        gram_copies = halo_push(gram.at[step], gram_send.at[step], gram_recv.at[step])
        started.append(gram_copies)
        gram_copies.wait_recv()
        tiles = gram[step]
        grouped = [regroup([tiles[8 * g + t] for t in range(8)]) for g in range(PAD // 8)]
        blocks = [
            jnp.concatenate([group[b] for group in grouped], axis=1) for b in range(7)
        ]
        diagonal_terms = jnp.zeros((8, PAD * EDGES), F32)
        row_all = iota((8, PAD * EDGES), 0)
        for b in range(6):
            diagonal_terms = jnp.where(row_all == b, blocks[b], diagonal_terms)
        residual = rows_times(blocks[6], ends_out)
        diagonal = rows_times(diagonal_terms, ends_abs) + anchor
        inverse = 1.0 / diagonal
        scaled = residual * inverse
        spread = rows_times(scaled, ends_in)
        pushed = blocks[0] * spread[0:1]
        for b in range(1, 6):
            pushed = pushed + blocks[b] * spread[b : b + 1]
        image = rows_times(pushed, ends_out) + anchor * scaled
        second = image * inverse
        own_diff = rows_times(second, ends_in[:, 128:256])
        own_pushed = grouped[1][0] * own_diff[0:1]
        for b in range(1, 6):
            own_pushed = own_pushed + grouped[1][b] * own_diff[b : b + 1]

        def inner(a, b, mask=own_nodes):
            return jnp.sum(jnp.where(mask, a * b, 0.0), keepdims=True)

        energy = inner(residual, scaled)
        curve = inner(scaled, image)
        cross = inner(second, image)
        bend = inner(anchor * second, second) + inner(own_pushed, own_diff, own_edges)
        sums_row = jnp.zeros((1, 128), F32)
        for number, value in enumerate((energy, curve, cross, bend)):
            sums_row = jnp.where(lane_row == number, value, sums_row)

        def exchange(value, buffer, spot, count, send, recv, partners):
            buffer[step, pl.ds(spot, 1)] = value.reshape(1, 1, 128)
            own = buffer.at[step, pl.ds(spot, 1)]
            push(
                [(own, buffer.at[step, pl.ds(at, 1)], device) for device, at in partners],
                send.at[step],
                recv.at[step],
            )
            others = whole(
                buffer.at[step, pl.ds(0, count - 1)], send.at[step], recv.at[step]
            )
            others.wait_recv()
            started.append(others)
            return jnp.sum(buffer[step].reshape(count, 128), axis=0, keepdims=True)

        sums_row = exchange(
            sums_row, far, sub, groups, far_send, far_recv, sum_partners
        )
        energy, curve, cross, bend = [sums_row[:, k : k + 1] for k in range(4)]
        step_one = energy / curve
        renewed = step_one * step_one * cross - energy
        ratio = renewed / energy
        curve_two = (
            curve
            - 2.0 * step_one * cross
            + step_one * step_one * bend
            + 2.0 * ratio * (curve - step_one * cross)
            + ratio * ratio * curve
        )
        step_two = renewed / curve_two
        increment = (step_one + step_two * (1.0 + ratio)) * scaled - (
            step_two * step_one
        ) * second
        inc = [increment[k : k + 1] for k in range(6)]
        turn_mat = cayley(0.5 * inc[0], 0.5 * inc[1], 0.5 * inc[2])
        rotated = [
            turn_mat[3 * i] * pose[j]
            + turn_mat[3 * i + 1] * pose[3 + j]
            + turn_mat[3 * i + 2] * pose[6 + j]
            for i in range(3)
            for j in range(3)
        ]
        moved = [
            turn_mat[3 * i] * pose[9]
            + turn_mat[3 * i + 1] * pose[10]
            + turn_mat[3 * i + 2] * pose[11]
            + inc[3 + i]
            for i in range(3)
        ]
        pose = rotated + moved

    final = jnp.concatenate(pose + [jnp.zeros((4, 128), F32)], axis=0)
    final = pltpu.roll(final, 128 - (REACH * 16 + dom * SCAN_DEV), 1)
    out_ref[...] = final.T[:SCAN_DEV, :12]

    for copy in started:
        copy.wait_send()


def local(groups, source_points, boundary, poses, anchor, edge_target, corr_tile, corr_source, corr_lane):
    vmem = pl.BlockSpec(memory_space=pltpu.VMEM)
    smem = pl.BlockSpec(memory_space=pltpu.SMEM)
    hbm = pl.BlockSpec(memory_space=pl.ANY)
    dma = pltpu.SemaphoreType.DMA
    return pl.pallas_call(
        functools.partial(kernel, groups),
        out_shape=pltpu.VMEM((SCAN_DEV, 12), F32),
        in_specs=[hbm, hbm, hbm, smem, smem, smem, hbm, hbm],
        out_specs=vmem,
        scratch_shapes=[
            pltpu.VMEM(corr_source.shape, jnp.int32),
            pltpu.VMEM(corr_lane.shape, jnp.int32),
            pltpu.VMEM((3, SCAN_DEV, source_points.shape[2]), F32),
            pltpu.VMEM(poses.shape, F32),
            pltpu.VMEM((12 * ROWS + 16, 128), F32),
            pltpu.VMEM((PAD, 1, 128), F32),
            pltpu.VMEM((GN_ITERS, PAD, 8, 128), F32),
            pltpu.VMEM((GN_ITERS, groups, 1, 128), F32),
            pltpu.VMEM((3, 64, 128), F32),
            pltpu.VMEM((512, 128), F32),
            pltpu.VMEM((9, CT, EDGES, 128), F32),
            pltpu.VMEM((PAD * EDGES, 128), F32),
            dma((11, PARTS)),
            dma((12, PARTS)),
            dma,
            dma,
            dma((GN_ITERS,)),
            dma((GN_ITERS,)),
            dma((GN_ITERS,)),
            dma((GN_ITERS,)),
            dma((5,)),
            pltpu.SemaphoreType.REGULAR((2,)),
        ],
        compiler_params=pltpu.CompilerParams(collective_id=0, has_side_effects=True),
    )(
        source_points.transpose(1, 0, 2),
        boundary.transpose(0, 2, 1, 3).reshape(ROWS, 128),
        poses,
        anchor,
        edge_target,
        corr_tile,
        corr_source,
        corr_lane,
    ).T


def solution(mesh):
    both = ("sub", "dom")
    return jax.shard_map(
        functools.partial(local, mesh.shape["sub"]),
        mesh=mesh,
        in_specs=(
            P(both, None, None),
            P(both, None, None, None),
            P(),
            P(both),
            P(both, None),
            P(both, None, None),
            P(both, None, None, None),
            P(both, None, None, None),
        ),
        out_specs=P(None, both),
        check_vma=False,
    )
```

```python
import functools

import jax
import jax.numpy as jnp
from jax import lax
from jax.experimental import pallas as pl
from jax.experimental.pallas import tpu as pltpu
from jax.sharding import PartitionSpec as P

MESH = pl.DeviceIdType.MESH
F32 = jnp.float32
BF16 = jnp.bfloat16
GN_ITERS = 2
SCAN_DEV = 4
EDGE_SCAN = 4
CT = 4
EDGES = SCAN_DEV * EDGE_SCAN
REACH = 3
SLOTS = 2 * REACH + 1
TILES = 4 * SLOTS
PAD = 32
SAMPLES = CT * 128
ROWS = SCAN_DEV * 6 * 8
PARTS = 2
PART = ROWS // PARTS
PAIRS = [(a, b) for a in range(6) for b in range(a, 6)]


def iota(shape, dim):
    return lax.broadcasted_iota(jnp.int32, shape, dim)


def parts_of(value, count=2):
    parts = []
    for _ in range(count):
        parts.append(value.astype(BF16))
        value = value - parts[-1].astype(F32)
    return parts[::-1]


def dot(a, b):
    return jnp.dot(a, b, preferred_element_type=F32)


def rows_times(value, select):
    stacked = jnp.concatenate([part.astype(F32) for part in parts_of(value, 3)], axis=0)
    product = dot(stacked.astype(BF16), select)
    return (product[0:8] + product[8:16]) + product[16:24]


def regroup(tiles):
    group = lax.shift_right_logical(iota((8, 128), 1), 4)
    for bit in range(3):
        size = 1 << bit
        low = lax.bitwise_and(group, size) == 0
        tiles = list(tiles)
        for first in range(8):
            if first & size:
                continue
            one, two = tiles[first], tiles[first + size]
            tiles[first] = jnp.where(low, one, pltpu.roll(two, size * 16, 1))
            tiles[first + size] = jnp.where(low, pltpu.roll(one, 128 - size * 16, 1), two)
    return tiles


def pick_turned(select, value):
    turned = (((1,), (1,)), ((), ()))
    third, second, first = [
        lax.dot_general(select, part, turned, preferred_element_type=F32)
        for part in parts_of(value, 3)
    ]
    return (third + second) + first


def cayley(first, second, third):
    length_sq = first * first + second * second + third * third
    inverse = 1.0 / (1.0 + length_sq)
    trace_part = 1.0 - length_sq
    entries = [
        trace_part + 2.0 * first * first,
        2.0 * first * second - 2.0 * third,
        2.0 * first * third + 2.0 * second,
        2.0 * first * second + 2.0 * third,
        trace_part + 2.0 * second * second,
        2.0 * second * third - 2.0 * first,
        2.0 * first * third - 2.0 * second,
        2.0 * second * third + 2.0 * first,
        trace_part + 2.0 * third * third,
    ]
    return [entry * inverse for entry in entries]


def kernel(
    groups,
    source_hbm,
    boundary_hbm,
    poses_hbm,
    anchor_ref,
    target_ref,
    tile_ref,
    corr_source_hbm,
    corr_lane_hbm,
    out_ref,
    corr_source_ref,
    corr_lane_ref,
    source_ref,
    poses_ref,
    window,
    early,
    gram,
    far,
    picked,
    chosen,
    comps,
    ends,
    win_send,
    win_recv,
    early_send,
    early_recv,
    gram_send,
    gram_recv,
    far_send,
    far_recv,
    load_sem,
    word,
):
    sub = lax.axis_index("sub")
    dom = lax.axis_index("dom")
    half_groups = groups // 2
    sub_low = lax.rem(sub, half_groups)
    sub_high = sub // half_groups

    def near_by(offset):
        return lax.rem(sub + offset + groups, groups)

    halo_partners = [
        ((near_by(offset), lax.bitwise_xor(dom, other)), (REACH - offset) * 4 + dom)
        for distance in range(REACH, -1, -1)
        for offset in ((distance, -distance) if distance else (0,))
        for other in range(4)
        if distance or other
    ]
    z_size = groups // 8
    z_spot = lax.rem(sub, z_size)
    y_spot = lax.rem(sub // z_size, 4)

    def hops(step, size):
        return min(step, size - step)

    moves = [
        (x_step, y_step, z_step)
        for x_step in range(2)
        for y_step in range(4)
        for z_step in range(z_size)
        if x_step or y_step or z_step
    ]
    moves.sort(key=lambda move: -(move[0] + hops(move[1], 4) + hops(move[2], z_size)))
    sum_partners = []
    for x_step, y_step, z_step in moves:
        half = 1 - sub_high if x_step else sub_high
        y_there = lax.rem(y_spot + y_step, 4)
        z_there = lax.rem(z_spot + z_step, z_size)
        place = half * half_groups + y_there * z_size + z_there
        sum_partners.append(((place, lax.bitwise_xor(dom, 2 * x_step)), sub))

    loads = [
        pltpu.make_async_copy(source, target, load_sem.at[number])
        for number, (source, target) in enumerate(
            (
                (boundary_hbm, window.at[pl.ds((4 + dom) * ROWS, ROWS)]),
                (corr_source_hbm, corr_source_ref),
                (source_hbm, source_ref),
                (poses_hbm, poses_ref),
                (corr_lane_hbm, corr_lane_ref),
            )
        )
    ]
    for load in loads:
        load.start()
    barrier = pltpu.get_barrier_semaphore()
    z_line = [
        (sub - z_spot + lax.rem(z_spot + turn, z_size), dom) for turn in range(1, z_size)
    ]
    y_line = [
        (
            sub_high * half_groups + lax.rem(y_spot + turn, 4) * z_size + z_spot,
            dom,
        )
        for turn in range(1, 4)
    ]
    x_line = [((1 - sub_high) * half_groups + sub_low, lax.bitwise_xor(dom, 2))]

    def signal_all(semaphore, devices):
        for device in devices:
            pl.semaphore_signal(semaphore, inc=1, device_id=device, device_id_type=MESH)

    greeted = [device for device, _ in halo_partners] + z_line + y_line + x_line
    signal_all(barrier, greeted)

    pl.semaphore_wait(barrier, len(greeted))
    started = []

    def push(copies, send_sem, recv_sem):
        for source, target, device in copies:
            pltpu.make_async_remote_copy(
                src_ref=source,
                dst_ref=target,
                send_sem=send_sem,
                recv_sem=recv_sem,
                device_id=device,
                device_id_type=MESH,
            ).start()

    def whole(ref, send_sem, recv_sem):
        return pltpu.make_async_remote_copy(
            src_ref=ref,
            dst_ref=ref,
            send_sem=send_sem,
            recv_sem=recv_sem,
            device_id=(sub, lax.bitwise_xor(dom, 1)),
            device_id_type=MESH,
        )

    own_slot = REACH * 4 + dom

    def halo_push(buffer, rows, send, recv):
        at = lambda slot, count=1: buffer.at[pl.ds(slot, count), pl.ds(0, rows)]
        push(
            [(at(own_slot), at(slot), device) for device, slot in halo_partners], send, recv
        )
        return whole(at(0, TILES - 1), send, recv)

    loads[0].wait()
    sibling = lax.bitwise_xor(dom, 1)
    across = lax.bitwise_xor(dom, 2)
    to_sibling = (sub, sibling)
    to_across = (sub, across)

    to_next = lax.bitwise_xor(dom, 2 * (sub_low // (half_groups - 1)))
    to_last = lax.bitwise_xor(dom, 2 * (lax.rem(sub_low + half_groups - 1, half_groups) // (half_groups - 1)))

    def window_copy(number, part, slot, device):
        at = window.at[pl.ds(slot * ROWS + part * PART, PART)]
        return pltpu.make_async_remote_copy(
            src_ref=at,
            dst_ref=at,
            send_sem=win_send.at[number, part],
            recv_sem=win_recv.at[slot, part],
            device_id=device,
            device_id_type=MESH,
        )

    def window_copy_to(number, part, slot, slot_there, device):
        at = window.at[pl.ds(slot * ROWS + part * PART, PART)]
        there = window.at[pl.ds(slot_there * ROWS + part * PART, PART)]
        return pltpu.make_async_remote_copy(
            src_ref=at,
            dst_ref=there,
            send_sem=win_send.at[number, part],
            recv_sem=win_recv.at[slot_there, part],
            device_id=device,
            device_id_type=MESH,
        )

    def window_send(number, part, slot, device, slot_there=None):
        slot_there = slot if slot_there is None else slot_there
        copy = window_copy_to(number, part, slot, slot_there, device)
        copy.start()
        started.append(copy)

    def window_wait(part, slot):
        window_copy(0, part, slot, to_sibling).wait_recv()

    for part in range(PARTS):
        window_send(0, part, 4 + dom, (near_by(1), to_next), dom)
        window_send(1, part, 4 + dom, (near_by(-1), to_last), 8 + dom)
    for part in range(PARTS):
        window_send(2, part, 4 + dom, to_across)
    for part in range(PARTS):
        window_send(3, part, 4 + dom, to_sibling)
    lane_row = iota((1, 128), 1)
    row = jnp.zeros((1, 128), F32)
    edge_of_row = iota((EDGES, 128), 0)
    own_target = jnp.zeros((EDGES, 128), jnp.int32)
    for edge in range(EDGES):
        value = target_ref[edge // EDGE_SCAN, edge % EDGE_SCAN]
        row = jnp.where(lane_row == edge, value.astype(F32), row)
        own_target = jnp.where(edge_of_row == edge, value, own_target)
    for scan in range(SCAN_DEV):
        row = jnp.where(lane_row == EDGES + scan, anchor_ref[scan], row)
    early[pl.ds(own_slot, 1)] = row.reshape(1, 1, 128)
    early_copies = halo_push(early, 1, early_send, early_recv)
    signal_all(word.at[0], y_line)
    started.append(early_copies)
    early[pl.ds(TILES, 4)] = jnp.zeros((4, 1, 128), F32)
    for step in range(GN_ITERS):
        gram[step, pl.ds(TILES, 4)] = jnp.zeros((4, 8, 128), F32)
        gram[step, pl.ds(0, TILES), pl.ds(6, 2)] = jnp.zeros((TILES, 2, 128), F32)

    def gather_scan(scan):
        indices = corr_source_ref[scan].reshape(EDGE_SCAN * CT, 128)
        low = lax.bitwise_and(indices, 127)
        high = lax.shift_right_logical(indices, 7)

        def gather_blocks(group, found):
            found = list(found)
            for number in range(8):
                block = group * 8 + number
                here = high == block
                for comp in range(3):
                    at = pl.multiple_of(block * 128, 128)
                    line = source_ref[comp, pl.ds(scan, 1), pl.ds(at, 128)]
                    wide = jnp.broadcast_to(line, (EDGE_SCAN * CT, 128))
                    value = jnp.take_along_axis(wide, low, axis=1, mode="promise_in_bounds")
                    found[comp] = jnp.where(here, value, found[comp])
            return tuple(found)

        empty = jnp.zeros((EDGE_SCAN * CT, 128), F32)
        found = lax.fori_loop(0, 4, gather_blocks, (empty, empty, empty))
        for comp in range(3):
            picked[comp, pl.ds(scan * 16, 16), :] = found[comp]

    loads[1].wait()
    loads[2].wait()
    for part in range(PARTS):
        gather_scan(part)
        for number, slot in ((4, to_last), (5, 8 + to_next)):
            window_wait(part, slot)
            window_send(number, part, slot, to_across)
            window_send(number + 2, part, slot, to_sibling)
        window_wait(part, 4 + across)
        window_send(8, part, 4 + across, to_sibling)
    pl.semaphore_wait(word.at[0], len(y_line))
    signal_all(word.at[1], x_line)
    gather_scan(2)
    gather_scan(3)
    for part in range(PARTS):
        for number, slot in (
            (9, lax.bitwise_xor(to_last, 2)),
            (10, 8 + lax.bitwise_xor(to_next, 2)),
        ):
            window_wait(part, slot)
            window_send(number, part, slot, to_sibling)

    loads[3].wait()
    start = near_by(-REACH) * 16
    first_tile = start // 128
    next_tile = lax.rem(first_tile + 1, groups * 16 // 128)
    pair = jnp.concatenate(
        [
            poses_ref[:, pl.ds(pl.multiple_of(first_tile * 128, 128), 128)],
            poses_ref[:, pl.ds(pl.multiple_of(next_tile * 128, 128), 128)],
        ],
        axis=1,
    )
    shift = lax.rem(256 - lax.rem(start, 128), 256)
    rolled = pltpu.roll(pair, shift, 1)[:, :128]
    pose = [rolled[k : k + 1] for k in range(12)]

    lane16 = iota((EDGES, 128), 1)
    own_source_lane = REACH * 16 + dom * SCAN_DEV + edge_of_row // EDGE_SCAN
    own_ends = jnp.concatenate(
        [
            (lane16 == own_source_lane).astype(F32),
            (lane16 == own_target + (REACH - 1) * 16).astype(F32),
        ],
        axis=0,
    ).astype(BF16)

    row_of = iota((16, 6 * 128), 0) == lax.shift_right_logical(iota((16, 6 * 128), 1), 7)
    into_rows = jnp.where(row_of, 1.0, 0.0).astype(BF16)

    early_copies.wait_recv()
    rows = early[...].reshape(PAD, 128)
    rows_turned = jnp.concatenate([rows, jnp.zeros((128 - PAD, 128), F32)], axis=0).T
    lane8 = iota((8, 128), 1)
    row8 = iota((8, 128), 0)
    for tile in range(TILES):
        target = rows_turned[:EDGES, tile : tile + 1]
        target_lane = target + float((tile // 4 - 1) * 16)
        source_lane = tile * 4 + edge_of_row // EDGE_SCAN
        ends[pl.ds(tile * EDGES, EDGES), :] = (lane16 == source_lane).astype(F32) - (
            lane16.astype(F32) == target_lane
        ).astype(F32)
    ends[pl.ds(TILES * EDGES, (PAD - TILES) * EDGES), :] = jnp.zeros(
        ((PAD - TILES) * EDGES, 128), F32
    )
    ends_f32 = ends[...]
    ends_out = ends_f32.astype(BF16)
    ends_abs = jnp.abs(ends_f32).astype(BF16)
    node_of = iota((128, PAD * EDGES), 0)
    ends_turned = ends_f32.T
    far_end = jnp.sum(
        jnp.where(ends_turned < 0.0, node_of, 0), axis=0, keepdims=True
    )
    near_lanes = []
    far_lanes = []
    for group in range(PAD // 8):
        near_lanes.append(group * 32 + lane8 // EDGE_SCAN)
        far_lanes.append(
            jnp.broadcast_to(far_end[:, group * 128 : group * 128 + 128], (8, 128))
        )

    def along_edges(value, group):
        near = jnp.take_along_axis(value, near_lanes[group], axis=1, mode="promise_in_bounds")
        far_value = jnp.take_along_axis(
            value, far_lanes[group], axis=1, mode="promise_in_bounds"
        )
        return near - far_value

    of_tile = jnp.where(iota((128, 128), 0) == iota((128, 128), 1) // 4, 1.0, 0.0).astype(BF16)
    anchor_rows = rows_times(rows_turned[EDGES : EDGES + 8], of_tile)
    anchor = jnp.sum(
        jnp.where(row8 == lax.bitwise_and(lane8, 3), anchor_rows, 0.0), axis=0, keepdims=True
    )
    anchor = jnp.broadcast_to(anchor, (8, 128))
    anchor = jnp.where(lane8 < TILES * 4, anchor, 1.0)
    for part in range(PARTS):
        for other in (sibling, lax.bitwise_xor(dom, 3)):
            for offset in range(3):
                window_wait(part, offset * 4 + other)
    pl.semaphore_wait(word.at[1], len(x_line))
    loads[4].wait()

    def gather_edge(edge, carry):
        scan = edge // EDGE_SCAN
        slot = lax.rem(edge, EDGE_SCAN)
        first = target_ref[scan, slot] * 48
        lanes = corr_lane_ref[scan, slot]
        for chunk in range(CT):
            tile = window[pl.ds(first + tile_ref[scan, slot, chunk], 8, stride=8), :]
            spread = jnp.broadcast_to(lanes[chunk : chunk + 1], (8, 128))
            value = jnp.take_along_axis(tile, spread, axis=1, mode="promise_in_bounds")
            chosen[pl.ds(pl.multiple_of(edge * 32 + chunk * 8, 8), 8), :] = value
        return carry

    lax.fori_loop(0, EDGES, gather_edge, 0, unroll=True)
    for chunk in range(CT):
        for comp in range(3):
            comps[comp, chunk] = picked[comp, pl.ds(chunk, EDGES, stride=CT), :]
        for comp in range(6):
            comps[3 + comp, chunk] = chosen[pl.ds(chunk * 8 + comp, EDGES, stride=32), :]


    for step in range(GN_ITERS):
        pose_rows = jnp.concatenate(pose + [jnp.zeros((4, 128), F32)], axis=0)
        pose_ends = pick_turned(own_ends, pose_rows)
        here = [
            jnp.broadcast_to(pose_ends[:EDGES, k : k + 1], (EDGES, 128)) for k in range(12)
        ]
        there = [
            jnp.broadcast_to(pose_ends[EDGES:, k : k + 1], (EDGES, 128)) for k in range(12)
        ]
        sums = {}
        for chunk in range(CT):
            data = [comps[k, chunk] for k in range(9)]

            def turn(matrix, vector):
                return [
                    matrix[3 * i] * vector[0]
                    + matrix[3 * i + 1] * vector[1]
                    + matrix[3 * i + 2] * vector[2]
                    for i in range(3)
                ]

            placed = [v + t for v, t in zip(turn(here[:9], data[0:3]), here[9:])]
            target = [v + t for v, t in zip(turn(there[:9], data[3:6]), there[9:])]
            normal = turn(there[:9], data[6:9])
            offset = [q - p for q, p in zip(target, placed)]
            misfit = normal[0] * offset[0] + normal[1] * offset[1] + normal[2] * offset[2]
            jac = [
                placed[1] * normal[2] - placed[2] * normal[1],
                placed[2] * normal[0] - placed[0] * normal[2],
                placed[0] * normal[1] - placed[1] * normal[0],
            ] + normal
            for a, b in PAIRS:
                term = jac[a] * jac[b]
                sums[a, b] = sums[a, b] + term if chunk else term
            for a in range(6):
                term = jac[a] * misfit
                sums[a, 6] = sums[a, 6] + term if chunk else term
        nothing = jnp.zeros((EDGES, 128), F32)
        message = None
        split = {key: parts_of(value) for key, value in sums.items()}
        for part in range(2):
            spread = jnp.concatenate(
                [
                    jnp.concatenate(
                        [split[min(a, b), max(a, b)][part] for b in range(7)]
                        + [nothing.astype(BF16)],
                        axis=0,
                    )
                    for a in range(6)
                ],
                axis=1,
            )
            term = lax.dot_general(
                into_rows, spread, (((1,), (1,)), ((), ())), preferred_element_type=F32
            )
            message = term if message is None else message + term
        message = message[:8] * (1.0 / SAMPLES)
        gram[step, pl.ds(own_slot, 1)] = message.reshape(1, 8, 128)
        gram_copies = halo_push(gram.at[step], 6, gram_send.at[step], gram_recv.at[step])
        started.append(gram_copies)
        gram_copies.wait_recv()
        tiles = gram[step]
        grouped = [regroup([tiles[8 * g + t] for t in range(8)]) for g in range(PAD // 8)]
        blocks = [
            jnp.concatenate([group[b] for group in grouped], axis=1) for b in range(7)
        ]
        diagonal_terms = jnp.zeros((8, PAD * EDGES), F32)
        row_all = iota((8, PAD * EDGES), 0)
        for b in range(6):
            diagonal_terms = jnp.where(row_all == b, blocks[b], diagonal_terms)
        residual = rows_times(blocks[6], ends_out)
        diagonal = rows_times(diagonal_terms, ends_abs) + anchor
        inverse = 1.0 / diagonal
        scaled = residual * inverse

        def push_edges(group, difference):
            pushed = grouped[group][0] * difference[0:1]
            for b in range(1, 6):
                pushed = pushed + grouped[group][b] * difference[b : b + 1]
            return pushed

        pushed = jnp.concatenate(
            [push_edges(group, along_edges(scaled, group)) for group in range(PAD // 8)],
            axis=1,
        )
        image = rows_times(pushed, ends_out) + anchor * scaled
        second = image * inverse
        own_diff = along_edges(second, 1)
        own_pushed = push_edges(1, own_diff)

        own = slice(REACH * 16, REACH * 16 + 16)
        packed = jnp.concatenate(
            [
                (residual * scaled)[:, own],
                (scaled * image)[:, own],
                (second * image)[:, own],
                (anchor * second * second)[:, own],
                (own_pushed * own_diff)[:, 64:],
            ],
            axis=1,
        )
        sums_row = jnp.sum(jnp.where(row8 < 6, packed, 0.0), axis=0, keepdims=True)

        def exchange(value, buffer, spot, count, send, recv, partners):
            buffer[step, pl.ds(spot, 1)] = value.reshape(1, 1, 128)
            own = buffer.at[step, pl.ds(spot, 1)]
            push(
                [(own, buffer.at[step, pl.ds(at, 1)], device) for device, at in partners],
                send.at[step],
                recv.at[step],
            )
            others = whole(
                buffer.at[step, pl.ds(0, count - 1)], send.at[step], recv.at[step]
            )
            others.wait_recv()
            started.append(others)
            return jnp.sum(buffer[step].reshape(count, 128), axis=0, keepdims=True)

        sums_row = exchange(
            sums_row, far, sub, groups, far_send, far_recv, sum_partners
        )
        part_of = jnp.minimum(lane_row // 16, 3)
        energy, curve, cross, bend = [
            jnp.sum(jnp.where(part_of == k, sums_row, 0.0), axis=1, keepdims=True)
            for k in range(4)
        ]
        step_one = energy / curve
        renewed = step_one * step_one * cross - energy
        ratio = renewed / energy
        curve_two = (
            curve
            - 2.0 * step_one * cross
            + step_one * step_one * bend
            + 2.0 * ratio * (curve - step_one * cross)
            + ratio * ratio * curve
        )
        step_two = renewed / curve_two
        increment = (step_one + step_two * (1.0 + ratio)) * scaled - (
            step_two * step_one
        ) * second
        inc = [increment[k : k + 1] for k in range(6)]
        turn_mat = cayley(0.5 * inc[0], 0.5 * inc[1], 0.5 * inc[2])
        rotated = [
            turn_mat[3 * i] * pose[j]
            + turn_mat[3 * i + 1] * pose[3 + j]
            + turn_mat[3 * i + 2] * pose[6 + j]
            for i in range(3)
            for j in range(3)
        ]
        moved = [
            turn_mat[3 * i] * pose[9]
            + turn_mat[3 * i + 1] * pose[10]
            + turn_mat[3 * i + 2] * pose[11]
            + inc[3 + i]
            for i in range(3)
        ]
        pose = rotated + moved

    final = jnp.concatenate(pose + [jnp.zeros((4, 128), F32)], axis=0)
    final = pltpu.roll(final, 128 - (REACH * 16 + dom * SCAN_DEV), 1)
    out_ref[...] = final.T[:SCAN_DEV, :12]

    for copy in started:
        copy.wait_send()


def local(groups, source_points, boundary, poses, anchor, edge_target, corr_tile, corr_source, corr_lane):
    vmem = pl.BlockSpec(memory_space=pltpu.VMEM)
    smem = pl.BlockSpec(memory_space=pltpu.SMEM)
    hbm = pl.BlockSpec(memory_space=pl.ANY)
    dma = pltpu.SemaphoreType.DMA
    return pl.pallas_call(
        functools.partial(kernel, groups),
        out_shape=pltpu.VMEM((SCAN_DEV, 12), F32),
        in_specs=[hbm, hbm, hbm, smem, smem, smem, hbm, hbm],
        out_specs=vmem,
        scratch_shapes=[
            pltpu.VMEM(corr_source.shape, jnp.int32),
            pltpu.VMEM(corr_lane.shape, jnp.int32),
            pltpu.VMEM((3, SCAN_DEV, source_points.shape[2]), F32),
            pltpu.VMEM(poses.shape, F32),
            pltpu.VMEM((12 * ROWS + 16, 128), F32),
            pltpu.VMEM((PAD, 1, 128), F32),
            pltpu.VMEM((GN_ITERS, PAD, 8, 128), F32),
            pltpu.VMEM((GN_ITERS, groups, 1, 128), F32),
            pltpu.VMEM((3, 64, 128), F32),
            pltpu.VMEM((512, 128), F32),
            pltpu.VMEM((9, CT, EDGES, 128), F32),
            pltpu.VMEM((PAD * EDGES, 128), F32),
            dma((11, PARTS)),
            dma((12, PARTS)),
            dma,
            dma,
            dma((GN_ITERS,)),
            dma((GN_ITERS,)),
            dma((GN_ITERS,)),
            dma((GN_ITERS,)),
            dma((5,)),
            pltpu.SemaphoreType.REGULAR((2,)),
        ],
        compiler_params=pltpu.CompilerParams(collective_id=0, has_side_effects=True),
    )(
        source_points.transpose(1, 0, 2),
        boundary.transpose(0, 2, 1, 3).reshape(ROWS, 128),
        poses,
        anchor,
        edge_target,
        corr_tile,
        corr_source,
        corr_lane,
    ).T


def solution(mesh):
    both = ("sub", "dom")
    return jax.shard_map(
        functools.partial(local, mesh.shape["sub"]),
        mesh=mesh,
        in_specs=(
            P(both, None, None),
            P(both, None, None, None),
            P(),
            P(both),
            P(both, None),
            P(both, None, None),
            P(both, None, None, None),
            P(both, None, None, None),
        ),
        out_specs=P(None, both),
        check_vma=False,
    )
```

```python
import functools

import jax
import jax.numpy as jnp
from jax import lax
from jax.experimental import pallas as pl
from jax.experimental.pallas import tpu as pltpu
from jax.sharding import PartitionSpec as P

MESH = pl.DeviceIdType.MESH
F32 = jnp.float32
BF16 = jnp.bfloat16
GN_ITERS = 2
SCAN_DEV = 4
EDGE_SCAN = 4
CT = 4
EDGES = SCAN_DEV * EDGE_SCAN
REACH = 3
SLOTS = 2 * REACH + 1
TILES = 4 * SLOTS
PAD = 32
SAMPLES = CT * 128
ROWS = SCAN_DEV * 6 * 8
PARTS = 2
PART = ROWS // PARTS
PAIRS = [(a, b) for a in range(6) for b in range(a, 6)]


def iota(shape, dim):
    return lax.broadcasted_iota(jnp.int32, shape, dim)


def parts_of(value, count=2):
    parts = []
    for _ in range(count):
        parts.append(value.astype(BF16))
        value = value - parts[-1].astype(F32)
    return parts[::-1]


def dot(a, b):
    return jnp.dot(a, b, preferred_element_type=F32)


def moved_pose(pose, inc):
    turn_mat = cayley(0.5 * inc[0], 0.5 * inc[1], 0.5 * inc[2])
    rotated = [
        turn_mat[3 * i] * pose[j]
        + turn_mat[3 * i + 1] * pose[3 + j]
        + turn_mat[3 * i + 2] * pose[6 + j]
        for i in range(3)
        for j in range(3)
    ]
    moved = [
        turn_mat[3 * i] * pose[9]
        + turn_mat[3 * i + 1] * pose[10]
        + turn_mat[3 * i + 2] * pose[11]
        + inc[3 + i]
        for i in range(3)
    ]
    return rotated + moved


def rows_times(value, select):
    stacked = jnp.concatenate([part.astype(F32) for part in parts_of(value, 3)], axis=0)
    product = dot(stacked.astype(BF16), select)
    return (product[0:8] + product[8:16]) + product[16:24]


def regroup(tiles):
    group = lax.shift_right_logical(iota((8, 128), 1), 4)
    for bit in range(3):
        size = 1 << bit
        low = lax.bitwise_and(group, size) == 0
        tiles = list(tiles)
        for first in range(8):
            if first & size:
                continue
            one, two = tiles[first], tiles[first + size]
            tiles[first] = jnp.where(low, one, pltpu.roll(two, size * 16, 1))
            tiles[first + size] = jnp.where(low, pltpu.roll(one, 128 - size * 16, 1), two)
    return tiles


def pick_turned(select, value):
    turned = (((1,), (1,)), ((), ()))
    third, second, first = [
        lax.dot_general(select, part, turned, preferred_element_type=F32)
        for part in parts_of(value, 3)
    ]
    return (third + second) + first


def cayley(first, second, third):
    length_sq = first * first + second * second + third * third
    inverse = 1.0 / (1.0 + length_sq)
    trace_part = 1.0 - length_sq
    entries = [
        trace_part + 2.0 * first * first,
        2.0 * first * second - 2.0 * third,
        2.0 * first * third + 2.0 * second,
        2.0 * first * second + 2.0 * third,
        trace_part + 2.0 * second * second,
        2.0 * second * third - 2.0 * first,
        2.0 * first * third - 2.0 * second,
        2.0 * second * third + 2.0 * first,
        trace_part + 2.0 * third * third,
    ]
    return [entry * inverse for entry in entries]


def kernel(
    groups,
    source_hbm,
    boundary_hbm,
    poses_hbm,
    anchor_ref,
    target_ref,
    tile_ref,
    corr_source_hbm,
    corr_lane_hbm,
    out_ref,
    corr_source_ref,
    corr_lane_ref,
    source_ref,
    poses_ref,
    window,
    early,
    gram,
    far,
    picked,
    chosen,
    comps,
    ends,
    win_send,
    win_recv,
    early_send,
    early_recv,
    gram_send,
    gram_recv,
    far_send,
    far_recv,
    load_sem,
    word,
):
    sub = lax.axis_index("sub")
    dom = lax.axis_index("dom")
    half_groups = groups // 2
    sub_low = lax.rem(sub, half_groups)
    sub_high = sub // half_groups

    def near_by(offset):
        return lax.rem(sub + offset + groups, groups)

    halo_partners = [
        ((near_by(offset), lax.bitwise_xor(dom, other)), (REACH - offset) * 4 + dom)
        for distance in range(REACH, -1, -1)
        for offset in ((distance, -distance) if distance else (0,))
        for other in range(4)
        if distance or other
    ]
    z_size = groups // 8
    z_spot = lax.rem(sub, z_size)
    y_spot = lax.rem(sub // z_size, 4)

    def hops(step, size):
        return min(step, size - step)

    moves = [
        (x_step, y_step, z_step)
        for x_step in range(2)
        for y_step in range(4)
        for z_step in range(z_size)
        if x_step or y_step or z_step
    ]
    moves.sort(key=lambda move: -(move[0] + hops(move[1], 4) + hops(move[2], z_size)))
    sum_partners = []
    for x_step, y_step, z_step in moves:
        half = 1 - sub_high if x_step else sub_high
        y_there = lax.rem(y_spot + y_step, 4)
        z_there = lax.rem(z_spot + z_step, z_size)
        place = half * half_groups + y_there * z_size + z_there
        sum_partners.append(((place, lax.bitwise_xor(dom, 2 * x_step)), sub))

    loads = [
        pltpu.make_async_copy(source, target, load_sem.at[number])
        for number, (source, target) in enumerate(
            (
                (boundary_hbm, window.at[pl.ds((4 + dom) * ROWS, ROWS)]),
                (corr_source_hbm, corr_source_ref),
                (source_hbm, source_ref),
                (poses_hbm, poses_ref),
                (corr_lane_hbm, corr_lane_ref),
            )
        )
    ]
    for load in loads:
        load.start()
    barrier = pltpu.get_barrier_semaphore()
    z_line = [
        (sub - z_spot + lax.rem(z_spot + turn, z_size), dom) for turn in range(1, z_size)
    ]
    y_line = [
        (
            sub_high * half_groups + lax.rem(y_spot + turn, 4) * z_size + z_spot,
            dom,
        )
        for turn in range(1, 4)
    ]
    x_line = [((1 - sub_high) * half_groups + sub_low, lax.bitwise_xor(dom, 2))]

    def signal_all(semaphore, devices):
        for device in devices:
            pl.semaphore_signal(semaphore, inc=1, device_id=device, device_id_type=MESH)

    chain_line = []
    for offset in (1, -1, 2, -2, 3, -3):
        inside = (sub_low + offset + half_groups) // half_groups
        crosses = lax.bitwise_xor(inside, 1)
        flip = 2 * jnp.minimum(crosses, 1)
        chain_line.append((near_by(offset), lax.bitwise_xor(dom, flip)))
        if abs(offset) == 1:
            chain_line.append((near_by(offset), lax.bitwise_xor(dom, 2 - flip)))
    group_line = [(sub, lax.bitwise_xor(dom, other)) for other in (1, 2, 3)]
    greeted = chain_line + group_line + z_line + y_line + x_line
    signal_all(barrier, greeted)

    pl.semaphore_wait(barrier, len(greeted))
    started = []

    def push(copies, send_sem, recv_sem):
        for source, target, device in copies:
            pltpu.make_async_remote_copy(
                src_ref=source,
                dst_ref=target,
                send_sem=send_sem,
                recv_sem=recv_sem,
                device_id=device,
                device_id_type=MESH,
            ).start()

    def whole(ref, send_sem, recv_sem):
        return pltpu.make_async_remote_copy(
            src_ref=ref,
            dst_ref=ref,
            send_sem=send_sem,
            recv_sem=recv_sem,
            device_id=(sub, lax.bitwise_xor(dom, 1)),
            device_id_type=MESH,
        )

    own_slot = REACH * 4 + dom

    def halo_push(buffer, rows, send, recv):
        at = lambda slot, count=1: buffer.at[pl.ds(slot, count), pl.ds(0, rows)]
        push(
            [(at(own_slot), at(slot), device) for device, slot in halo_partners], send, recv
        )
        return whole(at(0, TILES - 1), send, recv)

    loads[0].wait()
    sibling = lax.bitwise_xor(dom, 1)
    across = lax.bitwise_xor(dom, 2)
    to_sibling = (sub, sibling)
    to_across = (sub, across)

    to_next = lax.bitwise_xor(dom, 2 * (sub_low // (half_groups - 1)))
    to_last = lax.bitwise_xor(dom, 2 * (lax.rem(sub_low + half_groups - 1, half_groups) // (half_groups - 1)))

    def window_copy(number, part, slot, device):
        at = window.at[pl.ds(slot * ROWS + part * PART, PART)]
        return pltpu.make_async_remote_copy(
            src_ref=at,
            dst_ref=at,
            send_sem=win_send.at[number, part],
            recv_sem=win_recv.at[slot, part],
            device_id=device,
            device_id_type=MESH,
        )

    def window_copy_to(number, part, slot, slot_there, device):
        at = window.at[pl.ds(slot * ROWS + part * PART, PART)]
        there = window.at[pl.ds(slot_there * ROWS + part * PART, PART)]
        return pltpu.make_async_remote_copy(
            src_ref=at,
            dst_ref=there,
            send_sem=win_send.at[number, part],
            recv_sem=win_recv.at[slot_there, part],
            device_id=device,
            device_id_type=MESH,
        )

    def window_send(number, part, slot, device, slot_there=None):
        slot_there = slot if slot_there is None else slot_there
        copy = window_copy_to(number, part, slot, slot_there, device)
        copy.start()
        started.append(copy)

    def window_wait(part, slot):
        window_copy(0, part, slot, to_sibling).wait_recv()

    for part in range(PARTS):
        window_send(0, part, 4 + dom, (near_by(1), to_next), dom)
        window_send(1, part, 4 + dom, (near_by(-1), to_last), 8 + dom)
    for part in range(1, PARTS):
        window_send(4, part, 4 + dom, (near_by(1), lax.bitwise_xor(to_next, 2)), dom)
        window_send(5, part, 4 + dom, (near_by(-1), lax.bitwise_xor(to_last, 2)), 8 + dom)
    for part in range(PARTS):
        window_send(2, part, 4 + dom, to_across)
    for part in range(PARTS):
        window_send(3, part, 4 + dom, to_sibling)
    lane_row = iota((1, 128), 1)
    row = jnp.zeros((1, 128), F32)
    edge_of_row = iota((EDGES, 128), 0)
    own_target = jnp.zeros((EDGES, 128), jnp.int32)
    for edge in range(EDGES):
        value = target_ref[edge // EDGE_SCAN, edge % EDGE_SCAN]
        row = jnp.where(lane_row == edge, value.astype(F32), row)
        own_target = jnp.where(edge_of_row == edge, value, own_target)
    for scan in range(SCAN_DEV):
        row = jnp.where(lane_row == EDGES + scan, anchor_ref[scan], row)
    early[pl.ds(own_slot, 1)] = row.reshape(1, 1, 128)
    signal_all(word.at[0], y_line)
    signal_all(word.at[2], group_line)
    pl.semaphore_wait(word.at[2], len(group_line))
    early_copies = halo_push(early, 1, early_send, early_recv)
    started.append(early_copies)
    early[pl.ds(TILES, 4)] = jnp.zeros((4, 1, 128), F32)
    for step in range(GN_ITERS):
        gram[step, pl.ds(TILES, 4)] = jnp.zeros((4, 8, 128), F32)
        gram[step, pl.ds(0, TILES), pl.ds(6, 2)] = jnp.zeros((TILES, 2, 128), F32)

    def gather_scan(scan):
        indices = corr_source_ref[scan].reshape(EDGE_SCAN * CT, 128)
        low = lax.bitwise_and(indices, 127)
        high = lax.shift_right_logical(indices, 7)

        def gather_blocks(group, found):
            found = list(found)
            for number in range(8):
                block = group * 8 + number
                here = high == block
                for comp in range(3):
                    at = pl.multiple_of(block * 128, 128)
                    line = source_ref[comp, pl.ds(scan, 1), pl.ds(at, 128)]
                    wide = jnp.broadcast_to(line, (EDGE_SCAN * CT, 128))
                    value = jnp.take_along_axis(wide, low, axis=1, mode="promise_in_bounds")
                    found[comp] = jnp.where(here, value, found[comp])
            return tuple(found)

        empty = jnp.zeros((EDGE_SCAN * CT, 128), F32)
        found = lax.fori_loop(0, 4, gather_blocks, (empty, empty, empty))
        for comp in range(3):
            picked[comp, pl.ds(scan * 16, 16), :] = found[comp]

    loads[1].wait()
    loads[2].wait()
    for part in range(PARTS):
        gather_scan(part)
        for number, slot in ((4, to_last), (5, 8 + to_next)):
            window_wait(part, slot)
            if part == 0:
                window_send(number, part, slot, to_across)
            window_send(number + 2, part, slot, to_sibling)
        window_wait(part, 4 + across)
        window_send(8, part, 4 + across, to_sibling)
    pl.semaphore_wait(word.at[0], len(y_line))
    signal_all(word.at[1], x_line)
    gather_scan(2)
    gather_scan(3)
    for part in range(PARTS):
        for number, slot in (
            (9, lax.bitwise_xor(to_last, 2)),
            (10, 8 + lax.bitwise_xor(to_next, 2)),
        ):
            window_wait(part, slot)
            window_send(number, part, slot, to_sibling)

    loads[3].wait()
    start = near_by(-REACH) * 16
    first_tile = start // 128
    next_tile = lax.rem(first_tile + 1, groups * 16 // 128)
    pair = jnp.concatenate(
        [
            poses_ref[:, pl.ds(pl.multiple_of(first_tile * 128, 128), 128)],
            poses_ref[:, pl.ds(pl.multiple_of(next_tile * 128, 128), 128)],
        ],
        axis=1,
    )
    shift = lax.rem(256 - lax.rem(start, 128), 256)
    rolled = pltpu.roll(pair, shift, 1)[:, :128]
    pose = [rolled[k : k + 1] for k in range(12)]

    lane16 = iota((EDGES, 128), 1)
    own_source_lane = REACH * 16 + dom * SCAN_DEV + edge_of_row // EDGE_SCAN
    own_ends = jnp.concatenate(
        [
            (lane16 == own_source_lane).astype(F32),
            (lane16 == own_target + (REACH - 1) * 16).astype(F32),
        ],
        axis=0,
    ).astype(BF16)

    row_of = iota((16, 6 * 128), 0) == lax.shift_right_logical(iota((16, 6 * 128), 1), 7)
    into_rows = jnp.where(row_of, 1.0, 0.0).astype(BF16)

    pose_rows = jnp.concatenate(pose + [jnp.zeros((4, 128), F32)], axis=0)
    pose_ends = pick_turned(own_ends, pose_rows)
    end_poses = [
        [
            jnp.broadcast_to(
                pose_ends[end * EDGES : (end + 1) * EDGES, k : k + 1], (EDGES, 128)
            )
            for k in range(12)
        ]
        for end in range(2)
    ]

    lane8 = iota((8, 128), 1)
    row8 = iota((8, 128), 0)
    for part in range(PARTS):
        for other in (sibling, lax.bitwise_xor(dom, 3)):
            for offset in range(3):
                window_wait(part, offset * 4 + other)
    pl.semaphore_wait(word.at[1], len(x_line))
    loads[4].wait()

    def gather_edge(edge, carry):
        scan = edge // EDGE_SCAN
        slot = lax.rem(edge, EDGE_SCAN)
        first = target_ref[scan, slot] * 48
        lanes = corr_lane_ref[scan, slot]
        for chunk in range(CT):
            tile = window[pl.ds(first + tile_ref[scan, slot, chunk], 8, stride=8), :]
            spread = jnp.broadcast_to(lanes[chunk : chunk + 1], (8, 128))
            value = jnp.take_along_axis(tile, spread, axis=1, mode="promise_in_bounds")
            chosen[pl.ds(pl.multiple_of(edge * 32 + chunk * 8, 8), 8), :] = value
        return carry

    lax.fori_loop(0, EDGES, gather_edge, 0, unroll=True)
    for chunk in range(CT):
        for comp in range(3):
            comps[comp, chunk] = picked[comp, pl.ds(chunk, EDGES, stride=CT), :]
        for comp in range(6):
            comps[3 + comp, chunk] = chosen[pl.ds(chunk * 8 + comp, EDGES, stride=32), :]


    for step in range(GN_ITERS):
        here, there = end_poses
        sums = {}
        for chunk in range(CT):
            data = [comps[k, chunk] for k in range(9)]

            def turn(matrix, vector):
                return [
                    matrix[3 * i] * vector[0]
                    + matrix[3 * i + 1] * vector[1]
                    + matrix[3 * i + 2] * vector[2]
                    for i in range(3)
                ]

            placed = [v + t for v, t in zip(turn(here[:9], data[0:3]), here[9:])]
            target = [v + t for v, t in zip(turn(there[:9], data[3:6]), there[9:])]
            normal = turn(there[:9], data[6:9])
            offset = [q - p for q, p in zip(target, placed)]
            misfit = normal[0] * offset[0] + normal[1] * offset[1] + normal[2] * offset[2]
            jac = [
                placed[1] * normal[2] - placed[2] * normal[1],
                placed[2] * normal[0] - placed[0] * normal[2],
                placed[0] * normal[1] - placed[1] * normal[0],
            ] + normal
            for a, b in PAIRS:
                term = jac[a] * jac[b]
                sums[a, b] = sums[a, b] + term if chunk else term
            for a in range(6):
                term = jac[a] * misfit
                sums[a, 6] = sums[a, 6] + term if chunk else term
        nothing = jnp.zeros((EDGES, 128), F32)
        message = None
        split = {key: parts_of(value) for key, value in sums.items()}
        for part in range(2):
            spread = jnp.concatenate(
                [
                    jnp.concatenate(
                        [split[min(a, b), max(a, b)][part] for b in range(7)]
                        + [nothing.astype(BF16)],
                        axis=0,
                    )
                    for a in range(6)
                ],
                axis=1,
            )
            term = lax.dot_general(
                into_rows, spread, (((1,), (1,)), ((), ())), preferred_element_type=F32
            )
            message = term if message is None else message + term
        message = message[:8] * (1.0 / SAMPLES)
        gram[step, pl.ds(own_slot, 1)] = message.reshape(1, 8, 128)
        gram_copies = halo_push(gram.at[step], 6, gram_send.at[step], gram_recv.at[step])
        if step == 0:
            for copy in started:
                copy.wait_send()
            started = []
            early_copies.wait_recv()
            rows = early[...].reshape(PAD, 128)
            rows_turned = jnp.concatenate([rows, jnp.zeros((128 - PAD, 128), F32)], axis=0).T
            lane8 = iota((8, 128), 1)
            row8 = iota((8, 128), 0)
            for tile in range(TILES):
                target = rows_turned[:EDGES, tile : tile + 1]
                target_lane = target + float((tile // 4 - 1) * 16)
                source_lane = tile * 4 + edge_of_row // EDGE_SCAN
                ends[pl.ds(tile * EDGES, EDGES), :] = (lane16 == source_lane).astype(F32) - (
                    lane16.astype(F32) == target_lane
                ).astype(F32)
            ends[pl.ds(TILES * EDGES, (PAD - TILES) * EDGES), :] = jnp.zeros(
                ((PAD - TILES) * EDGES, 128), F32
            )
            ends_f32 = ends[...]
            ends_out = ends_f32.astype(BF16)
            ends_abs = jnp.abs(ends_f32).astype(BF16)
            node_of = iota((128, PAD * EDGES), 0)
            ends_turned = ends_f32.T
            far_end = jnp.sum(
                jnp.where(ends_turned < 0.0, node_of, 0), axis=0, keepdims=True
            )
            near_lanes = []
            far_lanes = []
            for group in range(PAD // 8):
                near_lanes.append(group * 32 + lane8 // EDGE_SCAN)
                far_lanes.append(
                    jnp.broadcast_to(far_end[:, group * 128 : group * 128 + 128], (8, 128))
                )

            def along_edges(value, group):
                near = jnp.take_along_axis(value, near_lanes[group], axis=1, mode="promise_in_bounds")
                far_value = jnp.take_along_axis(
                    value, far_lanes[group], axis=1, mode="promise_in_bounds"
                )
                return near - far_value

            of_tile = jnp.where(iota((128, 128), 0) == iota((128, 128), 1) // 4, 1.0, 0.0).astype(BF16)
            anchor_rows = rows_times(rows_turned[EDGES : EDGES + 8], of_tile)
            anchor = jnp.sum(
                jnp.where(row8 == lax.bitwise_and(lane8, 3), anchor_rows, 0.0), axis=0, keepdims=True
            )
            anchor = jnp.broadcast_to(anchor, (8, 128))
            anchor = jnp.where(lane8 < TILES * 4, anchor, 1.0)
        gram_copies.wait_recv()
        tiles = gram[step]
        grouped = [regroup([tiles[8 * g + t] for t in range(8)]) for g in range(PAD // 8)]
        blocks = [
            jnp.concatenate([group[b] for group in grouped], axis=1) for b in range(7)
        ]
        diagonal_terms = jnp.zeros((8, PAD * EDGES), F32)
        row_all = iota((8, PAD * EDGES), 0)
        for b in range(6):
            diagonal_terms = jnp.where(row_all == b, blocks[b], diagonal_terms)
        residual = rows_times(blocks[6], ends_out)
        diagonal = rows_times(diagonal_terms, ends_abs) + anchor
        inverse = 1.0 / diagonal
        scaled = residual * inverse

        def push_edges(group, difference):
            pushed = grouped[group][0] * difference[0:1]
            for b in range(1, 6):
                pushed = pushed + grouped[group][b] * difference[b : b + 1]
            return pushed

        pushed = jnp.concatenate(
            [push_edges(group, along_edges(scaled, group)) for group in range(PAD // 8)],
            axis=1,
        )
        image = rows_times(pushed, ends_out) + anchor * scaled
        second = image * inverse
        own_diff = along_edges(second, 1)
        own_pushed = push_edges(1, own_diff)

        own = slice(REACH * 16, REACH * 16 + 16)
        packed = jnp.concatenate(
            [
                (residual * scaled)[:, own],
                (scaled * image)[:, own],
                (second * image)[:, own],
                (anchor * second * second)[:, own],
                (own_pushed * own_diff)[:, 64:],
            ],
            axis=1,
        )
        sums_row = jnp.sum(jnp.where(row8 < 6, packed, 0.0), axis=0, keepdims=True)

        far[step, pl.ds(sub, 1)] = sums_row.reshape(1, 1, 128)
        own_sum = far.at[step, pl.ds(sub, 1)]
        push(
            [(own_sum, far.at[step, pl.ds(at, 1)], device) for device, at in sum_partners],
            far_send.at[step],
            far_recv.at[step],
        )
        sum_copies = whole(
            far.at[step, pl.ds(0, groups - 1)], far_send.at[step], far_recv.at[step]
        )
        gram_copies.wait_send()
        if step + 1 < GN_ITERS:
            both = pick_turned(own_ends, jnp.concatenate([scaled, second], axis=0))
            first_ends, second_ends = [
                [
                    [
                        jnp.broadcast_to(
                            both[end * EDGES : (end + 1) * EDGES, at + k : at + k + 1],
                            (EDGES, 128),
                        )
                        for k in range(6)
                    ]
                    for end in range(2)
                ]
                for at in (0, 8)
            ]
        sum_copies.wait_recv()
        started.append(sum_copies)
        sums_row = jnp.sum(far[step].reshape(groups, 128), axis=0, keepdims=True)

        part_of = jnp.minimum(lane_row // 16, 3)
        energy, curve, cross, bend = [
            jnp.sum(jnp.where(part_of == k, sums_row, 0.0), axis=1, keepdims=True)
            for k in range(4)
        ]
        step_one = energy / curve
        renewed = step_one * step_one * cross - energy
        ratio = renewed / energy
        curve_two = (
            curve
            - 2.0 * step_one * cross
            + step_one * step_one * bend
            + 2.0 * ratio * (curve - step_one * cross)
            + ratio * ratio * curve
        )
        step_two = renewed / curve_two
        first_factor = step_one + step_two * (1.0 + ratio)
        second_factor = -step_two * step_one
        increment = first_factor * scaled + second_factor * second
        pose = moved_pose(pose, [increment[k : k + 1] for k in range(6)])
        if step + 1 < GN_ITERS:
            end_poses = [
                moved_pose(
                    end_poses[end],
                    [
                        first_factor * first_ends[end][k] + second_factor * second_ends[end][k]
                        for k in range(6)
                    ],
                )
                for end in range(2)
            ]

    final = jnp.concatenate(pose + [jnp.zeros((4, 128), F32)], axis=0)
    final = pltpu.roll(final, 128 - (REACH * 16 + dom * SCAN_DEV), 1)
    out_ref[...] = final.T[:SCAN_DEV, :12]

    for copy in started:
        copy.wait_send()


def local(groups, source_points, boundary, poses, anchor, edge_target, corr_tile, corr_source, corr_lane):
    vmem = pl.BlockSpec(memory_space=pltpu.VMEM)
    smem = pl.BlockSpec(memory_space=pltpu.SMEM)
    hbm = pl.BlockSpec(memory_space=pl.ANY)
    dma = pltpu.SemaphoreType.DMA
    return pl.pallas_call(
        functools.partial(kernel, groups),
        out_shape=pltpu.VMEM((SCAN_DEV, 12), F32),
        in_specs=[hbm, hbm, hbm, smem, smem, smem, hbm, hbm],
        out_specs=vmem,
        scratch_shapes=[
            pltpu.VMEM(corr_source.shape, jnp.int32),
            pltpu.VMEM(corr_lane.shape, jnp.int32),
            pltpu.VMEM((3, SCAN_DEV, source_points.shape[2]), F32),
            pltpu.VMEM(poses.shape, F32),
            pltpu.VMEM((12 * ROWS + 16, 128), F32),
            pltpu.VMEM((PAD, 1, 128), F32),
            pltpu.VMEM((GN_ITERS, PAD, 8, 128), F32),
            pltpu.VMEM((GN_ITERS, groups, 1, 128), F32),
            pltpu.VMEM((3, 64, 128), F32),
            pltpu.VMEM((512, 128), F32),
            pltpu.VMEM((9, CT, EDGES, 128), F32),
            pltpu.VMEM((PAD * EDGES, 128), F32),
            dma((11, PARTS)),
            dma((12, PARTS)),
            dma,
            dma,
            dma((GN_ITERS,)),
            dma((GN_ITERS,)),
            dma((GN_ITERS,)),
            dma((GN_ITERS,)),
            dma((5,)),
            pltpu.SemaphoreType.REGULAR((3,)),
        ],
        compiler_params=pltpu.CompilerParams(collective_id=0, has_side_effects=True),
    )(
        source_points.transpose(1, 0, 2),
        boundary.transpose(0, 2, 1, 3).reshape(ROWS, 128),
        poses,
        anchor,
        edge_target,
        corr_tile,
        corr_source,
        corr_lane,
    ).T


def solution(mesh):
    both = ("sub", "dom")
    return jax.shard_map(
        functools.partial(local, mesh.shape["sub"]),
        mesh=mesh,
        in_specs=(
            P(both, None, None),
            P(both, None, None, None),
            P(),
            P(both),
            P(both, None),
            P(both, None, None),
            P(both, None, None, None),
            P(both, None, None, None),
        ),
        out_specs=P(None, both),
        check_vma=False,
    )
```

```python
import functools

import jax
import jax.numpy as jnp
from jax import lax
from jax.experimental import pallas as pl
from jax.experimental.pallas import tpu as pltpu
from jax.sharding import PartitionSpec as P

MESH = pl.DeviceIdType.MESH
F32 = jnp.float32
BF16 = jnp.bfloat16
GN_ITERS = 2
SCAN_DEV = 4
EDGE_SCAN = 4
CT = 4
EDGES = SCAN_DEV * EDGE_SCAN
REACH = 3
SLOTS = 2 * REACH + 1
TILES = 4 * SLOTS
PAD = 32
SAMPLES = CT * 128
ROWS = SCAN_DEV * 6 * 8
PARTS = 2
PART = ROWS // PARTS
PAIRS = [(a, b) for a in range(6) for b in range(a, 6)]


def iota(shape, dim):
    return lax.broadcasted_iota(jnp.int32, shape, dim)


def parts_of(value, count=2):
    parts = []
    for _ in range(count):
        parts.append(value.astype(BF16))
        value = value - parts[-1].astype(F32)
    return parts[::-1]


def dot(a, b):
    return jnp.dot(a, b, preferred_element_type=F32)


def moved_pose(pose, inc):
    turn_mat = cayley(0.5 * inc[0], 0.5 * inc[1], 0.5 * inc[2])
    rotated = [
        turn_mat[3 * i] * pose[j]
        + turn_mat[3 * i + 1] * pose[3 + j]
        + turn_mat[3 * i + 2] * pose[6 + j]
        for i in range(3)
        for j in range(3)
    ]
    moved = [
        turn_mat[3 * i] * pose[9]
        + turn_mat[3 * i + 1] * pose[10]
        + turn_mat[3 * i + 2] * pose[11]
        + inc[3 + i]
        for i in range(3)
    ]
    return rotated + moved


def rows_times(value, select):
    stacked = jnp.concatenate([part.astype(F32) for part in parts_of(value, 3)], axis=0)
    product = dot(stacked.astype(BF16), select)
    return (product[0:8] + product[8:16]) + product[16:24]


def regroup(tiles):
    group = lax.shift_right_logical(iota((8, 128), 1), 4)
    for bit in range(3):
        size = 1 << bit
        low = lax.bitwise_and(group, size) == 0
        tiles = list(tiles)
        for first in range(8):
            if first & size:
                continue
            one, two = tiles[first], tiles[first + size]
            tiles[first] = jnp.where(low, one, pltpu.roll(two, size * 16, 1))
            tiles[first + size] = jnp.where(low, pltpu.roll(one, 128 - size * 16, 1), two)
    return tiles


def pick_turned(select, value):
    turned = (((1,), (1,)), ((), ()))
    third, second, first = [
        lax.dot_general(select, part, turned, preferred_element_type=F32)
        for part in parts_of(value, 3)
    ]
    return (third + second) + first


def cayley(first, second, third):
    length_sq = first * first + second * second + third * third
    inverse = 1.0 / (1.0 + length_sq)
    trace_part = 1.0 - length_sq
    entries = [
        trace_part + 2.0 * first * first,
        2.0 * first * second - 2.0 * third,
        2.0 * first * third + 2.0 * second,
        2.0 * first * second + 2.0 * third,
        trace_part + 2.0 * second * second,
        2.0 * second * third - 2.0 * first,
        2.0 * first * third - 2.0 * second,
        2.0 * second * third + 2.0 * first,
        trace_part + 2.0 * third * third,
    ]
    return [entry * inverse for entry in entries]


def kernel(
    groups,
    source_hbm,
    boundary_hbm,
    poses_hbm,
    anchor_hbm,
    target_hbm,
    tile_hbm,
    corr_source_hbm,
    corr_lane_hbm,
    out_ref,
    anchor_ref,
    target_ref,
    tile_ref,
    corr_source_ref,
    corr_lane_ref,
    source_ref,
    poses_ref,
    window,
    early,
    gram,
    far,
    picked,
    chosen,
    comps,
    ends,
    win_send,
    win_recv,
    early_send,
    early_recv,
    gram_send,
    gram_recv,
    far_send,
    far_recv,
    load_sem,
    word,
):
    sub = lax.axis_index("sub")
    dom = lax.axis_index("dom")
    half_groups = groups // 2
    sub_low = lax.rem(sub, half_groups)
    sub_high = sub // half_groups

    def near_by(offset):
        return lax.rem(sub + offset + groups, groups)

    halo_partners = [
        ((near_by(offset), lax.bitwise_xor(dom, other)), (REACH - offset) * 4 + dom)
        for distance in range(REACH, -1, -1)
        for offset in ((distance, -distance) if distance else (0,))
        for other in range(4)
        if distance or other
    ]
    z_size = groups // 8
    z_spot = lax.rem(sub, z_size)
    y_spot = lax.rem(sub // z_size, 4)

    def hops(step, size):
        return min(step, size - step)

    moves = [
        (x_step, y_step, z_step)
        for x_step in range(2)
        for y_step in range(4)
        for z_step in range(z_size)
        if x_step or y_step or z_step
    ]
    moves.sort(key=lambda move: -(move[0] + hops(move[1], 4) + hops(move[2], z_size)))
    sum_partners = []
    for x_step, y_step, z_step in moves:
        half = 1 - sub_high if x_step else sub_high
        y_there = lax.rem(y_spot + y_step, 4)
        z_there = lax.rem(z_spot + z_step, z_size)
        place = half * half_groups + y_there * z_size + z_there
        sum_partners.append(((place, lax.bitwise_xor(dom, 2 * x_step)), sub))

    loads = [
        pltpu.make_async_copy(source, target, load_sem.at[number])
        for number, (source, target) in enumerate(
            (
                (boundary_hbm, window.at[pl.ds((4 + dom) * ROWS, ROWS)]),
                (corr_source_hbm, corr_source_ref),
                (source_hbm, source_ref),
                (poses_hbm, poses_ref),
                (corr_lane_hbm, corr_lane_ref),
                (anchor_hbm, anchor_ref),
                (target_hbm, target_ref),
                (tile_hbm, tile_ref),
            )
        )
    ]
    for load in loads:
        load.start()
    barrier = pltpu.get_barrier_semaphore()
    z_line = [
        (sub - z_spot + lax.rem(z_spot + turn, z_size), dom) for turn in range(1, z_size)
    ]
    y_line = [
        (
            sub_high * half_groups + lax.rem(y_spot + turn, 4) * z_size + z_spot,
            dom,
        )
        for turn in range(1, 4)
    ]
    x_line = [((1 - sub_high) * half_groups + sub_low, lax.bitwise_xor(dom, 2))]

    def signal_all(semaphore, devices):
        for device in devices:
            pl.semaphore_signal(semaphore, inc=1, device_id=device, device_id_type=MESH)

    chain_line = []
    for offset in (1, -1, 2, -2, 3, -3):
        inside = (sub_low + offset + half_groups) // half_groups
        crosses = lax.bitwise_xor(inside, 1)
        flip = 2 * jnp.minimum(crosses, 1)
        chain_line.append((near_by(offset), lax.bitwise_xor(dom, flip)))
        if abs(offset) == 1:
            chain_line.append((near_by(offset), lax.bitwise_xor(dom, 2 - flip)))
    group_line = [(sub, lax.bitwise_xor(dom, other)) for other in (1, 2, 3)]
    greeted = chain_line + group_line + z_line + y_line + x_line
    signal_all(barrier, greeted)

    pl.semaphore_wait(barrier, len(greeted))
    started = []

    def push(copies, send_sem, recv_sem):
        for source, target, device in copies:
            pltpu.make_async_remote_copy(
                src_ref=source,
                dst_ref=target,
                send_sem=send_sem,
                recv_sem=recv_sem,
                device_id=device,
                device_id_type=MESH,
            ).start()

    def whole(ref, send_sem, recv_sem):
        return pltpu.make_async_remote_copy(
            src_ref=ref,
            dst_ref=ref,
            send_sem=send_sem,
            recv_sem=recv_sem,
            device_id=(sub, lax.bitwise_xor(dom, 1)),
            device_id_type=MESH,
        )

    own_slot = REACH * 4 + dom

    def halo_push(buffer, rows, send, recv):
        at = lambda slot, count=1: buffer.at[pl.ds(slot, count), pl.ds(0, rows)]
        push(
            [(at(own_slot), at(slot), device) for device, slot in halo_partners], send, recv
        )
        return whole(at(0, TILES - 1), send, recv)

    loads[0].wait()
    sibling = lax.bitwise_xor(dom, 1)
    across = lax.bitwise_xor(dom, 2)
    to_sibling = (sub, sibling)
    to_across = (sub, across)

    to_next = lax.bitwise_xor(dom, 2 * (sub_low // (half_groups - 1)))
    to_last = lax.bitwise_xor(dom, 2 * (lax.rem(sub_low + half_groups - 1, half_groups) // (half_groups - 1)))

    def window_copy(number, part, slot, device):
        at = window.at[pl.ds(slot * ROWS + part * PART, PART)]
        return pltpu.make_async_remote_copy(
            src_ref=at,
            dst_ref=at,
            send_sem=win_send.at[number, part],
            recv_sem=win_recv.at[slot, part],
            device_id=device,
            device_id_type=MESH,
        )

    def window_copy_to(number, part, slot, slot_there, device):
        at = window.at[pl.ds(slot * ROWS + part * PART, PART)]
        there = window.at[pl.ds(slot_there * ROWS + part * PART, PART)]
        return pltpu.make_async_remote_copy(
            src_ref=at,
            dst_ref=there,
            send_sem=win_send.at[number, part],
            recv_sem=win_recv.at[slot_there, part],
            device_id=device,
            device_id_type=MESH,
        )

    def window_send(number, part, slot, device, slot_there=None):
        slot_there = slot if slot_there is None else slot_there
        copy = window_copy_to(number, part, slot, slot_there, device)
        copy.start()
        started.append(copy)

    def window_wait(part, slot):
        window_copy(0, part, slot, to_sibling).wait_recv()

    for part in range(PARTS):
        window_send(0, part, 4 + dom, (near_by(1), to_next), dom)
        window_send(1, part, 4 + dom, (near_by(-1), to_last), 8 + dom)
    for part in range(1, PARTS):
        window_send(4, part, 4 + dom, (near_by(1), lax.bitwise_xor(to_next, 2)), dom)
        window_send(5, part, 4 + dom, (near_by(-1), lax.bitwise_xor(to_last, 2)), 8 + dom)
    for part in range(PARTS):
        window_send(2, part, 4 + dom, to_across)
    for part in range(PARTS):
        window_send(3, part, 4 + dom, to_sibling)
    for number in (5, 6, 7):
        loads[number].wait()
    lane_row = iota((1, 128), 1)
    row = jnp.zeros((1, 128), F32)
    edge_of_row = iota((EDGES, 128), 0)
    own_target = jnp.zeros((EDGES, 128), jnp.int32)
    for edge in range(EDGES):
        value = target_ref[edge // EDGE_SCAN, edge % EDGE_SCAN]
        row = jnp.where(lane_row == edge, value.astype(F32), row)
        own_target = jnp.where(edge_of_row == edge, value, own_target)
    for scan in range(SCAN_DEV):
        row = jnp.where(lane_row == EDGES + scan, anchor_ref[scan], row)
    early[pl.ds(own_slot, 1)] = row.reshape(1, 1, 128)
    signal_all(word.at[0], y_line)
    signal_all(word.at[2], group_line)
    pl.semaphore_wait(word.at[2], len(group_line))
    early_copies = halo_push(early, 1, early_send, early_recv)
    started.append(early_copies)
    early[pl.ds(TILES, 4)] = jnp.zeros((4, 1, 128), F32)
    for step in range(GN_ITERS):
        gram[step, pl.ds(TILES, 4)] = jnp.zeros((4, 8, 128), F32)
        gram[step, pl.ds(0, TILES), pl.ds(6, 2)] = jnp.zeros((TILES, 2, 128), F32)

    def gather_scan(scan):
        indices = corr_source_ref[scan].reshape(EDGE_SCAN * CT, 128)
        low = lax.bitwise_and(indices, 127)
        high = lax.shift_right_logical(indices, 7)

        def gather_blocks(group, found):
            found = list(found)
            for number in range(8):
                block = group * 8 + number
                here = high == block
                for comp in range(3):
                    at = pl.multiple_of(block * 128, 128)
                    line = source_ref[comp, pl.ds(scan, 1), pl.ds(at, 128)]
                    wide = jnp.broadcast_to(line, (EDGE_SCAN * CT, 128))
                    value = jnp.take_along_axis(wide, low, axis=1, mode="promise_in_bounds")
                    found[comp] = jnp.where(here, value, found[comp])
            return tuple(found)

        empty = jnp.zeros((EDGE_SCAN * CT, 128), F32)
        found = lax.fori_loop(0, 4, gather_blocks, (empty, empty, empty))
        for comp in range(3):
            picked[comp, pl.ds(scan * 16, 16), :] = found[comp]

    loads[1].wait()
    loads[2].wait()
    for part in range(PARTS):
        gather_scan(part)
        for number, slot in ((4, to_last), (5, 8 + to_next)):
            window_wait(part, slot)
            if part == 0:
                window_send(number, part, slot, to_across)
            window_send(number + 2, part, slot, to_sibling)
        window_wait(part, 4 + across)
        window_send(8, part, 4 + across, to_sibling)
    pl.semaphore_wait(word.at[0], len(y_line))
    signal_all(word.at[1], x_line)
    gather_scan(2)
    gather_scan(3)
    for part in range(PARTS):
        for number, slot in (
            (9, lax.bitwise_xor(to_last, 2)),
            (10, 8 + lax.bitwise_xor(to_next, 2)),
        ):
            window_wait(part, slot)
            window_send(number, part, slot, to_sibling)

    loads[3].wait()
    start = near_by(-REACH) * 16
    first_tile = start // 128
    next_tile = lax.rem(first_tile + 1, groups * 16 // 128)
    pair = jnp.concatenate(
        [
            poses_ref[:, pl.ds(pl.multiple_of(first_tile * 128, 128), 128)],
            poses_ref[:, pl.ds(pl.multiple_of(next_tile * 128, 128), 128)],
        ],
        axis=1,
    )
    shift = lax.rem(256 - lax.rem(start, 128), 256)
    rolled = pltpu.roll(pair, shift, 1)[:, :128]
    pose = [rolled[k : k + 1] for k in range(12)]

    lane16 = iota((EDGES, 128), 1)
    own_source_lane = REACH * 16 + dom * SCAN_DEV + edge_of_row // EDGE_SCAN
    own_ends = jnp.concatenate(
        [
            (lane16 == own_source_lane).astype(F32),
            (lane16 == own_target + (REACH - 1) * 16).astype(F32),
        ],
        axis=0,
    ).astype(BF16)

    row_of = iota((16, 6 * 128), 0) == lax.shift_right_logical(iota((16, 6 * 128), 1), 7)
    into_rows = jnp.where(row_of, 1.0, 0.0).astype(BF16)

    pose_rows = jnp.concatenate(pose + [jnp.zeros((4, 128), F32)], axis=0)
    pose_ends = pick_turned(own_ends, pose_rows)
    end_poses = [
        [
            jnp.broadcast_to(
                pose_ends[end * EDGES : (end + 1) * EDGES, k : k + 1], (EDGES, 128)
            )
            for k in range(12)
        ]
        for end in range(2)
    ]

    lane8 = iota((8, 128), 1)
    row8 = iota((8, 128), 0)
    for part in range(PARTS):
        for other in (sibling, lax.bitwise_xor(dom, 3)):
            for offset in range(3):
                window_wait(part, offset * 4 + other)
    pl.semaphore_wait(word.at[1], len(x_line))
    loads[4].wait()

    def gather_edge(edge, carry):
        scan = edge // EDGE_SCAN
        slot = lax.rem(edge, EDGE_SCAN)
        first = target_ref[scan, slot] * 48
        lanes = corr_lane_ref[scan, slot]
        for chunk in range(CT):
            tile = window[pl.ds(first + tile_ref[scan, slot, chunk], 8, stride=8), :]
            spread = jnp.broadcast_to(lanes[chunk : chunk + 1], (8, 128))
            value = jnp.take_along_axis(tile, spread, axis=1, mode="promise_in_bounds")
            chosen[pl.ds(pl.multiple_of(edge * 32 + chunk * 8, 8), 8), :] = value
        return carry

    lax.fori_loop(0, EDGES, gather_edge, 0, unroll=True)
    for chunk in range(CT):
        for comp in range(3):
            comps[comp, chunk] = picked[comp, pl.ds(chunk, EDGES, stride=CT), :]
        for comp in range(6):
            comps[3 + comp, chunk] = chosen[pl.ds(chunk * 8 + comp, EDGES, stride=32), :]


    for step in range(GN_ITERS):
        here, there = end_poses
        sums = {}
        for chunk in range(CT):
            data = [comps[k, chunk] for k in range(9)]

            def turn(matrix, vector):
                return [
                    matrix[3 * i] * vector[0]
                    + matrix[3 * i + 1] * vector[1]
                    + matrix[3 * i + 2] * vector[2]
                    for i in range(3)
                ]

            placed = [v + t for v, t in zip(turn(here[:9], data[0:3]), here[9:])]
            target = [v + t for v, t in zip(turn(there[:9], data[3:6]), there[9:])]
            normal = turn(there[:9], data[6:9])
            offset = [q - p for q, p in zip(target, placed)]
            misfit = normal[0] * offset[0] + normal[1] * offset[1] + normal[2] * offset[2]
            jac = [
                placed[1] * normal[2] - placed[2] * normal[1],
                placed[2] * normal[0] - placed[0] * normal[2],
                placed[0] * normal[1] - placed[1] * normal[0],
            ] + normal
            for a, b in PAIRS:
                term = jac[a] * jac[b]
                sums[a, b] = sums[a, b] + term if chunk else term
            for a in range(6):
                term = jac[a] * misfit
                sums[a, 6] = sums[a, 6] + term if chunk else term
        nothing = jnp.zeros((EDGES, 128), F32)
        message = None
        split = {key: parts_of(value) for key, value in sums.items()}
        for part in range(2):
            spread = jnp.concatenate(
                [
                    jnp.concatenate(
                        [split[min(a, b), max(a, b)][part] for b in range(7)]
                        + [nothing.astype(BF16)],
                        axis=0,
                    )
                    for a in range(6)
                ],
                axis=1,
            )
            term = lax.dot_general(
                into_rows, spread, (((1,), (1,)), ((), ())), preferred_element_type=F32
            )
            message = term if message is None else message + term
        message = message[:8] * (1.0 / SAMPLES)
        gram[step, pl.ds(own_slot, 1)] = message.reshape(1, 8, 128)
        gram_copies = halo_push(gram.at[step], 6, gram_send.at[step], gram_recv.at[step])
        if step == 0:
            for copy in started:
                copy.wait_send()
            started = []
            early_copies.wait_recv()
            rows = early[...].reshape(PAD, 128)
            rows_turned = jnp.concatenate([rows, jnp.zeros((128 - PAD, 128), F32)], axis=0).T
            lane8 = iota((8, 128), 1)
            row8 = iota((8, 128), 0)
            for tile in range(TILES):
                target = rows_turned[:EDGES, tile : tile + 1]
                target_lane = target + float((tile // 4 - 1) * 16)
                source_lane = tile * 4 + edge_of_row // EDGE_SCAN
                ends[pl.ds(tile * EDGES, EDGES), :] = (lane16 == source_lane).astype(F32) - (
                    lane16.astype(F32) == target_lane
                ).astype(F32)
            ends[pl.ds(TILES * EDGES, (PAD - TILES) * EDGES), :] = jnp.zeros(
                ((PAD - TILES) * EDGES, 128), F32
            )
            ends_f32 = ends[...]
            ends_out = ends_f32.astype(BF16)
            ends_abs = jnp.abs(ends_f32).astype(BF16)
            node_of = iota((128, PAD * EDGES), 0)
            ends_turned = ends_f32.T
            far_end = jnp.sum(
                jnp.where(ends_turned < 0.0, node_of, 0), axis=0, keepdims=True
            )
            near_lanes = []
            far_lanes = []
            for group in range(PAD // 8):
                near_lanes.append(group * 32 + lane8 // EDGE_SCAN)
                far_lanes.append(
                    jnp.broadcast_to(far_end[:, group * 128 : group * 128 + 128], (8, 128))
                )

            def along_edges(value, group):
                near = jnp.take_along_axis(value, near_lanes[group], axis=1, mode="promise_in_bounds")
                far_value = jnp.take_along_axis(
                    value, far_lanes[group], axis=1, mode="promise_in_bounds"
                )
                return near - far_value

            of_tile = jnp.where(iota((128, 128), 0) == iota((128, 128), 1) // 4, 1.0, 0.0).astype(BF16)
            anchor_rows = rows_times(rows_turned[EDGES : EDGES + 8], of_tile)
            anchor = jnp.sum(
                jnp.where(row8 == lax.bitwise_and(lane8, 3), anchor_rows, 0.0), axis=0, keepdims=True
            )
            anchor = jnp.broadcast_to(anchor, (8, 128))
            anchor = jnp.where(lane8 < TILES * 4, anchor, 1.0)
        gram_copies.wait_recv()
        tiles = gram[step]
        grouped = [regroup([tiles[8 * g + t] for t in range(8)]) for g in range(PAD // 8)]
        blocks = [
            jnp.concatenate([group[b] for group in grouped], axis=1) for b in range(7)
        ]
        diagonal_terms = jnp.zeros((8, PAD * EDGES), F32)
        row_all = iota((8, PAD * EDGES), 0)
        for b in range(6):
            diagonal_terms = jnp.where(row_all == b, blocks[b], diagonal_terms)
        residual = rows_times(blocks[6], ends_out)
        diagonal = rows_times(diagonal_terms, ends_abs) + anchor
        inverse = 1.0 / diagonal
        scaled = residual * inverse

        def push_edges(group, difference):
            pushed = grouped[group][0] * difference[0:1]
            for b in range(1, 6):
                pushed = pushed + grouped[group][b] * difference[b : b + 1]
            return pushed

        pushed = jnp.concatenate(
            [push_edges(group, along_edges(scaled, group)) for group in range(PAD // 8)],
            axis=1,
        )
        image = rows_times(pushed, ends_out) + anchor * scaled
        second = image * inverse
        own_diff = along_edges(second, 1)
        own_pushed = push_edges(1, own_diff)

        own = slice(REACH * 16, REACH * 16 + 16)
        packed = jnp.concatenate(
            [
                (residual * scaled)[:, own],
                (scaled * image)[:, own],
                (second * image)[:, own],
                (anchor * second * second)[:, own],
                (own_pushed * own_diff)[:, 64:],
            ],
            axis=1,
        )
        sums_row = jnp.sum(jnp.where(row8 < 6, packed, 0.0), axis=0, keepdims=True)

        far[step, pl.ds(sub, 1)] = sums_row.reshape(1, 1, 128)
        own_sum = far.at[step, pl.ds(sub, 1)]
        push(
            [(own_sum, far.at[step, pl.ds(at, 1)], device) for device, at in sum_partners],
            far_send.at[step],
            far_recv.at[step],
        )
        sum_copies = whole(
            far.at[step, pl.ds(0, groups - 1)], far_send.at[step], far_recv.at[step]
        )
        gram_copies.wait_send()
        if step + 1 < GN_ITERS:
            both = pick_turned(own_ends, jnp.concatenate([scaled, second], axis=0))
            first_ends, second_ends = [
                [
                    [
                        jnp.broadcast_to(
                            both[end * EDGES : (end + 1) * EDGES, at + k : at + k + 1],
                            (EDGES, 128),
                        )
                        for k in range(6)
                    ]
                    for end in range(2)
                ]
                for at in (0, 8)
            ]
        sum_copies.wait_recv()
        started.append(sum_copies)
        sums_row = jnp.sum(far[step].reshape(groups, 128), axis=0, keepdims=True)

        part_of = jnp.minimum(lane_row // 16, 3)
        energy, curve, cross, bend = [
            jnp.sum(jnp.where(part_of == k, sums_row, 0.0), axis=1, keepdims=True)
            for k in range(4)
        ]
        step_one = energy / curve
        renewed = step_one * step_one * cross - energy
        ratio = renewed / energy
        curve_two = (
            curve
            - 2.0 * step_one * cross
            + step_one * step_one * bend
            + 2.0 * ratio * (curve - step_one * cross)
            + ratio * ratio * curve
        )
        step_two = renewed / curve_two
        first_factor = step_one + step_two * (1.0 + ratio)
        second_factor = -step_two * step_one
        increment = first_factor * scaled + second_factor * second
        pose = moved_pose(pose, [increment[k : k + 1] for k in range(6)])
        if step + 1 < GN_ITERS:
            end_poses = [
                moved_pose(
                    end_poses[end],
                    [
                        first_factor * first_ends[end][k] + second_factor * second_ends[end][k]
                        for k in range(6)
                    ],
                )
                for end in range(2)
            ]

    final = jnp.concatenate(pose + [jnp.zeros((4, 128), F32)], axis=0)
    final = pltpu.roll(final, 128 - (REACH * 16 + dom * SCAN_DEV), 1)
    out_ref[...] = final.T[:SCAN_DEV, :12]

    for copy in started:
        copy.wait_send()


def local(groups, source_points, boundary, poses, anchor, edge_target, corr_tile, corr_source, corr_lane):
    vmem = pl.BlockSpec(memory_space=pltpu.VMEM)
    hbm = pl.BlockSpec(memory_space=pl.ANY)
    dma = pltpu.SemaphoreType.DMA
    return pl.pallas_call(
        functools.partial(kernel, groups),
        out_shape=pltpu.VMEM((SCAN_DEV, 12), F32),
        in_specs=[hbm] * 8,
        out_specs=vmem,
        scratch_shapes=[
            pltpu.SMEM(anchor.shape, F32),
            pltpu.SMEM(edge_target.shape, jnp.int32),
            pltpu.SMEM(corr_tile.shape, jnp.int32),
            pltpu.VMEM(corr_source.shape, jnp.int32),
            pltpu.VMEM(corr_lane.shape, jnp.int32),
            pltpu.VMEM((3, SCAN_DEV, source_points.shape[2]), F32),
            pltpu.VMEM(poses.shape, F32),
            pltpu.VMEM((12 * ROWS + 16, 128), F32),
            pltpu.VMEM((PAD, 1, 128), F32),
            pltpu.VMEM((GN_ITERS, PAD, 8, 128), F32),
            pltpu.VMEM((GN_ITERS, groups, 1, 128), F32),
            pltpu.VMEM((3, 64, 128), F32),
            pltpu.VMEM((512, 128), F32),
            pltpu.VMEM((9, CT, EDGES, 128), F32),
            pltpu.VMEM((PAD * EDGES, 128), F32),
            dma((11, PARTS)),
            dma((12, PARTS)),
            dma,
            dma,
            dma((GN_ITERS,)),
            dma((GN_ITERS,)),
            dma((GN_ITERS,)),
            dma((GN_ITERS,)),
            dma((8,)),
            pltpu.SemaphoreType.REGULAR((3,)),
        ],
        compiler_params=pltpu.CompilerParams(collective_id=0, has_side_effects=True),
    )(
        source_points.transpose(1, 0, 2),
        boundary.transpose(0, 2, 1, 3).reshape(ROWS, 128),
        poses,
        anchor,
        edge_target,
        corr_tile,
        corr_source,
        corr_lane,
    ).T


def solution(mesh):
    both = ("sub", "dom")
    return jax.shard_map(
        functools.partial(local, mesh.shape["sub"]),
        mesh=mesh,
        in_specs=(
            P(both, None, None),
            P(both, None, None, None),
            P(),
            P(both),
            P(both, None),
            P(both, None, None),
            P(both, None, None, None),
            P(both, None, None, None),
        ),
        out_specs=P(None, both),
        check_vma=False,
    )
```

```python
import functools

import jax
import jax.numpy as jnp
from jax import lax
from jax.experimental import pallas as pl
from jax.experimental.pallas import tpu as pltpu
from jax.sharding import PartitionSpec as P

MESH = pl.DeviceIdType.MESH
F32 = jnp.float32
BF16 = jnp.bfloat16
GN_ITERS = 2
SCAN_DEV = 4
EDGE_SCAN = 4
CT = 4
EDGES = SCAN_DEV * EDGE_SCAN
REACH = 3
SLOTS = 2 * REACH + 1
TILES = 4 * SLOTS
PAD = 32
SAMPLES = CT * 128
ROWS = SCAN_DEV * 6 * 8
PARTS = 2
PART = ROWS // PARTS
PAIRS = [(a, b) for a in range(6) for b in range(a, 6)]


def iota(shape, dim):
    return lax.broadcasted_iota(jnp.int32, shape, dim)


def parts_of(value, count=2):
    parts = []
    for _ in range(count):
        parts.append(value.astype(BF16))
        value = value - parts[-1].astype(F32)
    return parts[::-1]


def dot(a, b):
    return jnp.dot(a, b, preferred_element_type=F32)


def moved_pose(pose, inc):
    turn_mat = cayley(0.5 * inc[0], 0.5 * inc[1], 0.5 * inc[2])
    rotated = [
        turn_mat[3 * i] * pose[j]
        + turn_mat[3 * i + 1] * pose[3 + j]
        + turn_mat[3 * i + 2] * pose[6 + j]
        for i in range(3)
        for j in range(3)
    ]
    moved = [
        turn_mat[3 * i] * pose[9]
        + turn_mat[3 * i + 1] * pose[10]
        + turn_mat[3 * i + 2] * pose[11]
        + inc[3 + i]
        for i in range(3)
    ]
    return rotated + moved


def rows_times(value, select):
    stacked = jnp.concatenate([part.astype(F32) for part in parts_of(value, 3)], axis=0)
    product = dot(stacked.astype(BF16), select)
    return (product[0:8] + product[8:16]) + product[16:24]


def regroup(tiles):
    group = lax.shift_right_logical(iota((8, 128), 1), 4)
    for bit in range(3):
        size = 1 << bit
        low = lax.bitwise_and(group, size) == 0
        tiles = list(tiles)
        for first in range(8):
            if first & size:
                continue
            one, two = tiles[first], tiles[first + size]
            tiles[first] = jnp.where(low, one, pltpu.roll(two, size * 16, 1))
            tiles[first + size] = jnp.where(low, pltpu.roll(one, 128 - size * 16, 1), two)
    return tiles


def pick_turned(select, value):
    turned = (((1,), (1,)), ((), ()))
    third, second, first = [
        lax.dot_general(select, part, turned, preferred_element_type=F32)
        for part in parts_of(value, 3)
    ]
    return (third + second) + first


def cayley(first, second, third):
    length_sq = first * first + second * second + third * third
    inverse = 1.0 / (1.0 + length_sq)
    trace_part = 1.0 - length_sq
    entries = [
        trace_part + 2.0 * first * first,
        2.0 * first * second - 2.0 * third,
        2.0 * first * third + 2.0 * second,
        2.0 * first * second + 2.0 * third,
        trace_part + 2.0 * second * second,
        2.0 * second * third - 2.0 * first,
        2.0 * first * third - 2.0 * second,
        2.0 * second * third + 2.0 * first,
        trace_part + 2.0 * third * third,
    ]
    return [entry * inverse for entry in entries]


def kernel(
    groups,
    source_hbm,
    boundary_hbm,
    poses_hbm,
    anchor_hbm,
    target_hbm,
    tile_hbm,
    corr_source_hbm,
    corr_lane_hbm,
    out_ref,
    anchor_ref,
    target_ref,
    tile_ref,
    corr_source_ref,
    corr_lane_ref,
    source_ref,
    poses_ref,
    window,
    early,
    gram,
    far,
    picked,
    chosen,
    comps,
    ends,
    win_send,
    win_recv,
    early_send,
    early_recv,
    gram_send,
    gram_recv,
    far_send,
    far_recv,
    load_sem,
    word,
):
    sub = lax.axis_index("sub")
    dom = lax.axis_index("dom")
    half_groups = groups // 2
    sub_low = lax.rem(sub, half_groups)
    sub_high = sub // half_groups

    def near_by(offset):
        return lax.rem(sub + offset + groups, groups)

    halo_partners = [
        ((near_by(offset), lax.bitwise_xor(dom, other)), (REACH - offset) * 4 + dom)
        for distance in range(REACH, -1, -1)
        for offset in ((distance, -distance) if distance else (0,))
        for other in range(4)
        if distance or other
    ]
    z_size = groups // 8
    z_spot = lax.rem(sub, z_size)
    y_spot = lax.rem(sub // z_size, 4)

    def hops(step, size):
        return min(step, size - step)

    moves = [
        (x_step, y_step, z_step)
        for x_step in range(2)
        for y_step in range(4)
        for z_step in range(z_size)
        if x_step or y_step or z_step
    ]
    moves.sort(key=lambda move: -(move[0] + hops(move[1], 4) + hops(move[2], z_size)))
    sum_partners = []
    for x_step, y_step, z_step in moves:
        half = 1 - sub_high if x_step else sub_high
        y_there = lax.rem(y_spot + y_step, 4)
        z_there = lax.rem(z_spot + z_step, z_size)
        place = half * half_groups + y_there * z_size + z_there
        sum_partners.append(((place, lax.bitwise_xor(dom, 2 * x_step)), sub))

    loads = [
        pltpu.make_async_copy(source, target, load_sem.at[number])
        for number, (source, target) in enumerate(
            (
                (boundary_hbm, window.at[pl.ds((4 + dom) * ROWS, ROWS)]),
                (corr_source_hbm, corr_source_ref),
                (source_hbm, source_ref),
                (poses_hbm, poses_ref),
                (corr_lane_hbm, corr_lane_ref),
                (anchor_hbm, anchor_ref),
                (target_hbm, target_ref),
                (tile_hbm, tile_ref),
            )
        )
    ]
    for load in loads:
        load.start()
    barrier = pltpu.get_barrier_semaphore()
    z_line = [
        (sub - z_spot + lax.rem(z_spot + turn, z_size), dom) for turn in range(1, z_size)
    ]
    y_line = [
        (
            sub_high * half_groups + lax.rem(y_spot + turn, 4) * z_size + z_spot,
            dom,
        )
        for turn in range(1, 4)
    ]
    x_line = [((1 - sub_high) * half_groups + sub_low, lax.bitwise_xor(dom, 2))]

    def signal_all(semaphore, devices):
        for device in devices:
            pl.semaphore_signal(semaphore, inc=1, device_id=device, device_id_type=MESH)

    chain_line = []
    for offset in (1, -1, 2, -2, 3, -3):
        inside = (sub_low + offset + half_groups) // half_groups
        crosses = lax.bitwise_xor(inside, 1)
        flip = 2 * jnp.minimum(crosses, 1)
        chain_line.append((near_by(offset), lax.bitwise_xor(dom, flip)))
        if abs(offset) == 1:
            chain_line.append((near_by(offset), lax.bitwise_xor(dom, 2 - flip)))
    group_line = [(sub, lax.bitwise_xor(dom, other)) for other in (1, 2, 3)]
    greeted = chain_line + group_line + z_line + y_line + x_line
    signal_all(barrier, greeted)

    pl.semaphore_wait(barrier, len(greeted))
    started = []

    def push(copies, send_sem, recv_sem):
        for source, target, device in copies:
            pltpu.make_async_remote_copy(
                src_ref=source,
                dst_ref=target,
                send_sem=send_sem,
                recv_sem=recv_sem,
                device_id=device,
                device_id_type=MESH,
            ).start()

    def whole(ref, send_sem, recv_sem):
        return pltpu.make_async_remote_copy(
            src_ref=ref,
            dst_ref=ref,
            send_sem=send_sem,
            recv_sem=recv_sem,
            device_id=(sub, lax.bitwise_xor(dom, 1)),
            device_id_type=MESH,
        )

    own_slot = REACH * 4 + dom

    def halo_push(buffer, rows, send, recv):
        at = lambda slot, count=1: buffer.at[pl.ds(slot, count), pl.ds(0, rows)]
        push(
            [(at(own_slot), at(slot), device) for device, slot in halo_partners], send, recv
        )
        return whole(at(0, TILES - 1), send, recv)

    loads[0].wait()
    sibling = lax.bitwise_xor(dom, 1)
    across = lax.bitwise_xor(dom, 2)
    to_sibling = (sub, sibling)
    to_across = (sub, across)

    to_next = lax.bitwise_xor(dom, 2 * (sub_low // (half_groups - 1)))
    to_last = lax.bitwise_xor(dom, 2 * (lax.rem(sub_low + half_groups - 1, half_groups) // (half_groups - 1)))

    def window_copy(number, part, slot, device):
        at = window.at[pl.ds(slot * ROWS + part * PART, PART)]
        return pltpu.make_async_remote_copy(
            src_ref=at,
            dst_ref=at,
            send_sem=win_send.at[number, part],
            recv_sem=win_recv.at[slot, part],
            device_id=device,
            device_id_type=MESH,
        )

    def window_copy_to(number, part, slot, slot_there, device):
        at = window.at[pl.ds(slot * ROWS + part * PART, PART)]
        there = window.at[pl.ds(slot_there * ROWS + part * PART, PART)]
        return pltpu.make_async_remote_copy(
            src_ref=at,
            dst_ref=there,
            send_sem=win_send.at[number, part],
            recv_sem=win_recv.at[slot_there, part],
            device_id=device,
            device_id_type=MESH,
        )

    def window_send(number, part, slot, device, slot_there=None):
        slot_there = slot if slot_there is None else slot_there
        copy = window_copy_to(number, part, slot, slot_there, device)
        copy.start()
        started.append(copy)

    def window_wait(part, slot):
        window_copy(0, part, slot, to_sibling).wait_recv()

    for part in range(PARTS):
        window_send(2, part, 4 + dom, to_across)
        window_send(3, part, 4 + dom, to_sibling)
    for part in range(PARTS):
        window_send(0, part, 4 + dom, (near_by(1), to_next), dom)
        window_send(1, part, 4 + dom, (near_by(-1), to_last), 8 + dom)
    for part in range(1, PARTS):
        window_send(4, part, 4 + dom, (near_by(1), lax.bitwise_xor(to_next, 2)), dom)
        window_send(5, part, 4 + dom, (near_by(-1), lax.bitwise_xor(to_last, 2)), 8 + dom)
    for number in (5, 6, 7):
        loads[number].wait()
    lane_row = iota((1, 128), 1)
    row = jnp.zeros((1, 128), F32)
    edge_of_row = iota((EDGES, 128), 0)
    own_target = jnp.zeros((EDGES, 128), jnp.int32)
    for edge in range(EDGES):
        value = target_ref[edge // EDGE_SCAN, edge % EDGE_SCAN]
        row = jnp.where(lane_row == edge, value.astype(F32), row)
        own_target = jnp.where(edge_of_row == edge, value, own_target)
    for scan in range(SCAN_DEV):
        row = jnp.where(lane_row == EDGES + scan, anchor_ref[scan], row)
    early[pl.ds(own_slot, 1)] = row.reshape(1, 1, 128)
    signal_all(word.at[0], y_line)
    signal_all(word.at[2], group_line)
    pl.semaphore_wait(word.at[2], len(group_line))
    early_copies = halo_push(early, 1, early_send, early_recv)
    started.append(early_copies)
    early[pl.ds(TILES, 4)] = jnp.zeros((4, 1, 128), F32)
    for step in range(GN_ITERS):
        gram[step, pl.ds(TILES, 4)] = jnp.zeros((4, 8, 128), F32)
        gram[step, pl.ds(0, TILES), pl.ds(6, 2)] = jnp.zeros((TILES, 2, 128), F32)

    def gather_scan(scan):
        indices = corr_source_ref[scan].reshape(EDGE_SCAN * CT, 128)
        low = lax.bitwise_and(indices, 127)
        high = lax.shift_right_logical(indices, 7)

        def gather_blocks(group, found):
            found = list(found)
            for number in range(8):
                block = group * 8 + number
                here = high == block
                for comp in range(3):
                    at = pl.multiple_of(block * 128, 128)
                    line = source_ref[comp, pl.ds(scan, 1), pl.ds(at, 128)]
                    wide = jnp.broadcast_to(line, (EDGE_SCAN * CT, 128))
                    value = jnp.take_along_axis(wide, low, axis=1, mode="promise_in_bounds")
                    found[comp] = jnp.where(here, value, found[comp])
            return tuple(found)

        empty = jnp.zeros((EDGE_SCAN * CT, 128), F32)
        found = lax.fori_loop(0, 4, gather_blocks, (empty, empty, empty))
        for comp in range(3):
            picked[comp, pl.ds(scan * 16, 16), :] = found[comp]

    loads[1].wait()
    loads[2].wait()
    for part in range(PARTS):
        gather_scan(part)
        window_wait(part, 4 + across)
        window_send(8, part, 4 + across, to_sibling)
        for number, slot in ((4, to_last), (5, 8 + to_next)):
            window_wait(part, slot)
            if part == 0:
                window_send(number, part, slot, to_across)
            window_send(number + 2, part, slot, to_sibling)
    pl.semaphore_wait(word.at[0], len(y_line))
    signal_all(word.at[1], x_line)
    gather_scan(2)
    gather_scan(3)
    for part in range(PARTS):
        for number, slot in (
            (9, lax.bitwise_xor(to_last, 2)),
            (10, 8 + lax.bitwise_xor(to_next, 2)),
        ):
            window_wait(part, slot)
            window_send(number, part, slot, to_sibling)

    loads[3].wait()
    start = near_by(-REACH) * 16
    first_tile = start // 128
    next_tile = lax.rem(first_tile + 1, groups * 16 // 128)
    pair = jnp.concatenate(
        [
            poses_ref[:, pl.ds(pl.multiple_of(first_tile * 128, 128), 128)],
            poses_ref[:, pl.ds(pl.multiple_of(next_tile * 128, 128), 128)],
        ],
        axis=1,
    )
    shift = lax.rem(256 - lax.rem(start, 128), 256)
    rolled = pltpu.roll(pair, shift, 1)[:, :128]
    pose = [rolled[k : k + 1] for k in range(12)]

    lane16 = iota((EDGES, 128), 1)
    own_source_lane = REACH * 16 + dom * SCAN_DEV + edge_of_row // EDGE_SCAN
    own_ends = jnp.concatenate(
        [
            (lane16 == own_source_lane).astype(F32),
            (lane16 == own_target + (REACH - 1) * 16).astype(F32),
        ],
        axis=0,
    ).astype(BF16)

    row_of = iota((16, 6 * 128), 0) == lax.shift_right_logical(iota((16, 6 * 128), 1), 7)
    into_rows = jnp.where(row_of, 1.0, 0.0).astype(BF16)

    pose_rows = jnp.concatenate(pose + [jnp.zeros((4, 128), F32)], axis=0)
    pose_ends = pick_turned(own_ends, pose_rows)
    end_poses = [
        [
            jnp.broadcast_to(
                pose_ends[end * EDGES : (end + 1) * EDGES, k : k + 1], (EDGES, 128)
            )
            for k in range(12)
        ]
        for end in range(2)
    ]

    lane8 = iota((8, 128), 1)
    row8 = iota((8, 128), 0)
    for part in range(PARTS):
        for other in (sibling, lax.bitwise_xor(dom, 3)):
            for offset in range(3):
                window_wait(part, offset * 4 + other)
    pl.semaphore_wait(word.at[1], len(x_line))
    loads[4].wait()

    def gather_edge(edge, carry):
        scan = edge // EDGE_SCAN
        slot = lax.rem(edge, EDGE_SCAN)
        first = target_ref[scan, slot] * 48
        lanes = corr_lane_ref[scan, slot]
        for chunk in range(CT):
            tile = window[pl.ds(first + tile_ref[scan, slot, chunk], 8, stride=8), :]
            spread = jnp.broadcast_to(lanes[chunk : chunk + 1], (8, 128))
            value = jnp.take_along_axis(tile, spread, axis=1, mode="promise_in_bounds")
            chosen[pl.ds(pl.multiple_of(edge * 32 + chunk * 8, 8), 8), :] = value
        return carry

    lax.fori_loop(0, EDGES, gather_edge, 0, unroll=True)
    for chunk in range(CT):
        for comp in range(3):
            comps[comp, chunk] = picked[comp, pl.ds(chunk, EDGES, stride=CT), :]
        for comp in range(6):
            comps[3 + comp, chunk] = chosen[pl.ds(chunk * 8 + comp, EDGES, stride=32), :]


    for step in range(GN_ITERS):
        here, there = end_poses
        sums = {}
        for chunk in range(CT):
            data = [comps[k, chunk] for k in range(9)]

            def turn(matrix, vector):
                return [
                    matrix[3 * i] * vector[0]
                    + matrix[3 * i + 1] * vector[1]
                    + matrix[3 * i + 2] * vector[2]
                    for i in range(3)
                ]

            placed = [v + t for v, t in zip(turn(here[:9], data[0:3]), here[9:])]
            target = [v + t for v, t in zip(turn(there[:9], data[3:6]), there[9:])]
            normal = turn(there[:9], data[6:9])
            offset = [q - p for q, p in zip(target, placed)]
            misfit = normal[0] * offset[0] + normal[1] * offset[1] + normal[2] * offset[2]
            jac = [
                placed[1] * normal[2] - placed[2] * normal[1],
                placed[2] * normal[0] - placed[0] * normal[2],
                placed[0] * normal[1] - placed[1] * normal[0],
            ] + normal
            for a, b in PAIRS:
                term = jac[a] * jac[b]
                sums[a, b] = sums[a, b] + term if chunk else term
            for a in range(6):
                term = jac[a] * misfit
                sums[a, 6] = sums[a, 6] + term if chunk else term
        nothing = jnp.zeros((EDGES, 128), F32)
        message = None
        split = {key: parts_of(value) for key, value in sums.items()}
        for part in range(2):
            spread = jnp.concatenate(
                [
                    jnp.concatenate(
                        [split[min(a, b), max(a, b)][part] for b in range(7)]
                        + [nothing.astype(BF16)],
                        axis=0,
                    )
                    for a in range(6)
                ],
                axis=1,
            )
            term = lax.dot_general(
                into_rows, spread, (((1,), (1,)), ((), ())), preferred_element_type=F32
            )
            message = term if message is None else message + term
        message = message[:8] * (1.0 / SAMPLES)
        gram[step, pl.ds(own_slot, 1)] = message.reshape(1, 8, 128)
        gram_copies = halo_push(gram.at[step], 6, gram_send.at[step], gram_recv.at[step])
        if step == 0:
            for copy in started:
                copy.wait_send()
            started = []
            early_copies.wait_recv()
            rows = early[...].reshape(PAD, 128)
            rows_turned = jnp.concatenate([rows, jnp.zeros((128 - PAD, 128), F32)], axis=0).T
            lane8 = iota((8, 128), 1)
            row8 = iota((8, 128), 0)
            for tile in range(TILES):
                target = rows_turned[:EDGES, tile : tile + 1]
                target_lane = target + float((tile // 4 - 1) * 16)
                source_lane = tile * 4 + edge_of_row // EDGE_SCAN
                ends[pl.ds(tile * EDGES, EDGES), :] = (lane16 == source_lane).astype(F32) - (
                    lane16.astype(F32) == target_lane
                ).astype(F32)
            ends[pl.ds(TILES * EDGES, (PAD - TILES) * EDGES), :] = jnp.zeros(
                ((PAD - TILES) * EDGES, 128), F32
            )
            ends_f32 = ends[...]
            ends_out = ends_f32.astype(BF16)
            ends_abs = jnp.abs(ends_f32).astype(BF16)
            node_of = iota((128, PAD * EDGES), 0)
            ends_turned = ends_f32.T
            far_end = jnp.sum(
                jnp.where(ends_turned < 0.0, node_of, 0), axis=0, keepdims=True
            )
            near_lanes = []
            far_lanes = []
            for group in range(PAD // 8):
                near_lanes.append(group * 32 + lane8 // EDGE_SCAN)
                far_lanes.append(
                    jnp.broadcast_to(far_end[:, group * 128 : group * 128 + 128], (8, 128))
                )

            def along_edges(value, group):
                near = jnp.take_along_axis(value, near_lanes[group], axis=1, mode="promise_in_bounds")
                far_value = jnp.take_along_axis(
                    value, far_lanes[group], axis=1, mode="promise_in_bounds"
                )
                return near - far_value

            of_tile = jnp.where(iota((128, 128), 0) == iota((128, 128), 1) // 4, 1.0, 0.0).astype(BF16)
            anchor_rows = rows_times(rows_turned[EDGES : EDGES + 8], of_tile)
            anchor = jnp.sum(
                jnp.where(row8 == lax.bitwise_and(lane8, 3), anchor_rows, 0.0), axis=0, keepdims=True
            )
            anchor = jnp.broadcast_to(anchor, (8, 128))
            anchor = jnp.where(lane8 < TILES * 4, anchor, 1.0)
        gram_copies.wait_recv()
        tiles = gram[step]
        grouped = [regroup([tiles[8 * g + t] for t in range(8)]) for g in range(PAD // 8)]
        blocks = [
            jnp.concatenate([group[b] for group in grouped], axis=1) for b in range(7)
        ]
        diagonal_terms = jnp.zeros((8, PAD * EDGES), F32)
        row_all = iota((8, PAD * EDGES), 0)
        for b in range(6):
            diagonal_terms = jnp.where(row_all == b, blocks[b], diagonal_terms)
        residual = rows_times(blocks[6], ends_out)
        diagonal = rows_times(diagonal_terms, ends_abs) + anchor
        inverse = 1.0 / diagonal
        scaled = residual * inverse

        def push_edges(group, difference):
            pushed = grouped[group][0] * difference[0:1]
            for b in range(1, 6):
                pushed = pushed + grouped[group][b] * difference[b : b + 1]
            return pushed

        pushed = jnp.concatenate(
            [push_edges(group, along_edges(scaled, group)) for group in range(PAD // 8)],
            axis=1,
        )
        image = rows_times(pushed, ends_out) + anchor * scaled
        second = image * inverse
        own_diff = along_edges(second, 1)
        own_pushed = push_edges(1, own_diff)

        own = slice(REACH * 16, REACH * 16 + 16)
        packed = jnp.concatenate(
            [
                (residual * scaled)[:, own],
                (scaled * image)[:, own],
                (second * image)[:, own],
                (anchor * second * second)[:, own],
                (own_pushed * own_diff)[:, 64:],
            ],
            axis=1,
        )
        sums_row = jnp.sum(jnp.where(row8 < 6, packed, 0.0), axis=0, keepdims=True)

        far[step, pl.ds(sub, 1)] = sums_row.reshape(1, 1, 128)
        own_sum = far.at[step, pl.ds(sub, 1)]
        push(
            [(own_sum, far.at[step, pl.ds(at, 1)], device) for device, at in sum_partners],
            far_send.at[step],
            far_recv.at[step],
        )
        sum_copies = whole(
            far.at[step, pl.ds(0, groups - 1)], far_send.at[step], far_recv.at[step]
        )
        gram_copies.wait_send()
        if step + 1 < GN_ITERS:
            both = pick_turned(own_ends, jnp.concatenate([scaled, second], axis=0))
            first_ends, second_ends = [
                [
                    [
                        jnp.broadcast_to(
                            both[end * EDGES : (end + 1) * EDGES, at + k : at + k + 1],
                            (EDGES, 128),
                        )
                        for k in range(6)
                    ]
                    for end in range(2)
                ]
                for at in (0, 8)
            ]
        sum_copies.wait_recv()
        started.append(sum_copies)
        sums_row = jnp.sum(far[step].reshape(groups, 128), axis=0, keepdims=True)

        part_of = jnp.minimum(lane_row // 16, 3)
        energy, curve, cross, bend = [
            jnp.sum(jnp.where(part_of == k, sums_row, 0.0), axis=1, keepdims=True)
            for k in range(4)
        ]
        step_one = energy / curve
        renewed = step_one * step_one * cross - energy
        ratio = renewed / energy
        curve_two = (
            curve
            - 2.0 * step_one * cross
            + step_one * step_one * bend
            + 2.0 * ratio * (curve - step_one * cross)
            + ratio * ratio * curve
        )
        step_two = renewed / curve_two
        first_factor = step_one + step_two * (1.0 + ratio)
        second_factor = -step_two * step_one
        increment = first_factor * scaled + second_factor * second
        pose = moved_pose(pose, [increment[k : k + 1] for k in range(6)])
        if step + 1 < GN_ITERS:
            end_poses = [
                moved_pose(
                    end_poses[end],
                    [
                        first_factor * first_ends[end][k] + second_factor * second_ends[end][k]
                        for k in range(6)
                    ],
                )
                for end in range(2)
            ]

    final = jnp.concatenate(pose + [jnp.zeros((4, 128), F32)], axis=0)
    final = pltpu.roll(final, 128 - (REACH * 16 + dom * SCAN_DEV), 1)
    out_ref[...] = final.T[:SCAN_DEV, :12]

    for copy in started:
        copy.wait_send()


def local(groups, source_points, boundary, poses, anchor, edge_target, corr_tile, corr_source, corr_lane):
    vmem = pl.BlockSpec(memory_space=pltpu.VMEM)
    hbm = pl.BlockSpec(memory_space=pl.ANY)
    dma = pltpu.SemaphoreType.DMA
    return pl.pallas_call(
        functools.partial(kernel, groups),
        out_shape=pltpu.VMEM((SCAN_DEV, 12), F32),
        in_specs=[hbm] * 8,
        out_specs=vmem,
        scratch_shapes=[
            pltpu.SMEM(anchor.shape, F32),
            pltpu.SMEM(edge_target.shape, jnp.int32),
            pltpu.SMEM(corr_tile.shape, jnp.int32),
            pltpu.VMEM(corr_source.shape, jnp.int32),
            pltpu.VMEM(corr_lane.shape, jnp.int32),
            pltpu.VMEM((3, SCAN_DEV, source_points.shape[2]), F32),
            pltpu.VMEM(poses.shape, F32),
            pltpu.VMEM((12 * ROWS + 64, 128), F32),
            pltpu.VMEM((PAD, 1, 128), F32),
            pltpu.VMEM((GN_ITERS, PAD, 8, 128), F32),
            pltpu.VMEM((GN_ITERS, groups, 1, 128), F32),
            pltpu.VMEM((3, 72, 128), F32),
            pltpu.VMEM((544, 128), F32),
            pltpu.VMEM((9, CT, EDGES, 128), F32),
            pltpu.VMEM((PAD * EDGES, 128), F32),
            dma((11, PARTS)),
            dma((12, PARTS)),
            dma,
            dma,
            dma((GN_ITERS,)),
            dma((GN_ITERS,)),
            dma((GN_ITERS,)),
            dma((GN_ITERS,)),
            dma((8,)),
            pltpu.SemaphoreType.REGULAR((3,)),
        ],
        compiler_params=pltpu.CompilerParams(collective_id=0, has_side_effects=True),
    )(
        source_points.transpose(1, 0, 2),
        boundary.transpose(0, 2, 1, 3).reshape(ROWS, 128),
        poses,
        anchor,
        edge_target,
        corr_tile,
        corr_source,
        corr_lane,
    ).T


def solution(mesh):
    both = ("sub", "dom")
    return jax.shard_map(
        functools.partial(local, mesh.shape["sub"]),
        mesh=mesh,
        in_specs=(
            P(both, None, None),
            P(both, None, None, None),
            P(),
            P(both),
            P(both, None),
            P(both, None, None),
            P(both, None, None, None),
            P(both, None, None, None),
        ),
        out_specs=P(None, both),
        check_vma=False,
    )
```

```python
import functools

import jax
import jax.numpy as jnp
from jax import lax
from jax.experimental import pallas as pl
from jax.experimental.pallas import tpu as pltpu
from jax.sharding import PartitionSpec as P

MESH = pl.DeviceIdType.MESH
F32 = jnp.float32
BF16 = jnp.bfloat16
GN_ITERS = 2
SCAN_DEV = 4
EDGE_SCAN = 4
CT = 4
EDGES = SCAN_DEV * EDGE_SCAN
REACH = 3
SLOTS = 2 * REACH + 1
TILES = 4 * SLOTS
PAD = 32
SAMPLES = CT * 128
ROWS = SCAN_DEV * 6 * 8
PARTS = 2
PART = ROWS // PARTS
PAIRS = [(a, b) for a in range(6) for b in range(a, 6)]


def iota(shape, dim):
    return lax.broadcasted_iota(jnp.int32, shape, dim)


def parts_of(value, count=2):
    parts = []
    for _ in range(count):
        parts.append(value.astype(BF16))
        value = value - parts[-1].astype(F32)
    return parts[::-1]


def dot(a, b):
    return jnp.dot(a, b, preferred_element_type=F32)


def moved_pose(pose, inc):
    turn_mat = cayley(0.5 * inc[0], 0.5 * inc[1], 0.5 * inc[2])
    rotated = [
        turn_mat[3 * i] * pose[j]
        + turn_mat[3 * i + 1] * pose[3 + j]
        + turn_mat[3 * i + 2] * pose[6 + j]
        for i in range(3)
        for j in range(3)
    ]
    moved = [
        turn_mat[3 * i] * pose[9]
        + turn_mat[3 * i + 1] * pose[10]
        + turn_mat[3 * i + 2] * pose[11]
        + inc[3 + i]
        for i in range(3)
    ]
    return rotated + moved


def rows_times(value, select):
    stacked = jnp.concatenate([part.astype(F32) for part in parts_of(value)], axis=0)
    product = dot(stacked.astype(BF16), select)
    return product[0:8] + product[8:16]


def regroup(tiles):
    group = lax.shift_right_logical(iota((8, 128), 1), 4)
    for bit in range(3):
        size = 1 << bit
        low = lax.bitwise_and(group, size) == 0
        tiles = list(tiles)
        for first in range(8):
            if first & size:
                continue
            one, two = tiles[first], tiles[first + size]
            tiles[first] = jnp.where(low, one, pltpu.roll(two, size * 16, 1))
            tiles[first + size] = jnp.where(low, pltpu.roll(one, 128 - size * 16, 1), two)
    return tiles


def pick_turned(select, value):
    turned = (((1,), (1,)), ((), ()))
    third, second, first = [
        lax.dot_general(select, part, turned, preferred_element_type=F32)
        for part in parts_of(value, 3)
    ]
    return (third + second) + first


def cayley(first, second, third):
    length_sq = first * first + second * second + third * third
    inverse = 1.0 / (1.0 + length_sq)
    trace_part = 1.0 - length_sq
    entries = [
        trace_part + 2.0 * first * first,
        2.0 * first * second - 2.0 * third,
        2.0 * first * third + 2.0 * second,
        2.0 * first * second + 2.0 * third,
        trace_part + 2.0 * second * second,
        2.0 * second * third - 2.0 * first,
        2.0 * first * third - 2.0 * second,
        2.0 * second * third + 2.0 * first,
        trace_part + 2.0 * third * third,
    ]
    return [entry * inverse for entry in entries]


def kernel(
    groups,
    source_hbm,
    boundary_hbm,
    poses_hbm,
    anchor_hbm,
    target_hbm,
    tile_hbm,
    corr_source_hbm,
    corr_lane_hbm,
    out_ref,
    anchor_ref,
    target_ref,
    tile_ref,
    corr_source_ref,
    corr_lane_ref,
    source_ref,
    poses_ref,
    window,
    early,
    gram,
    far,
    picked,
    chosen,
    comps,
    ends,
    win_send,
    win_recv,
    early_send,
    early_recv,
    gram_send,
    gram_recv,
    far_send,
    far_recv,
    load_sem,
    word,
):
    sub = lax.axis_index("sub")
    dom = lax.axis_index("dom")
    half_groups = groups // 2
    sub_low = lax.rem(sub, half_groups)
    sub_high = sub // half_groups

    def near_by(offset):
        return lax.rem(sub + offset + groups, groups)

    halo_partners = [
        ((near_by(offset), lax.bitwise_xor(dom, other)), (REACH - offset) * 4 + dom)
        for distance in range(REACH, -1, -1)
        for offset in ((distance, -distance) if distance else (0,))
        for other in range(4)
        if distance or other
    ]
    z_size = groups // 8
    z_spot = lax.rem(sub, z_size)
    y_spot = lax.rem(sub // z_size, 4)

    def hops(step, size):
        return min(step, size - step)

    moves = [
        (x_step, y_step, z_step)
        for x_step in range(2)
        for y_step in range(4)
        for z_step in range(z_size)
        if x_step or y_step or z_step
    ]
    moves.sort(key=lambda move: -(move[0] + hops(move[1], 4) + hops(move[2], z_size)))
    sum_partners = []
    for x_step, y_step, z_step in moves:
        half = 1 - sub_high if x_step else sub_high
        y_there = lax.rem(y_spot + y_step, 4)
        z_there = lax.rem(z_spot + z_step, z_size)
        place = half * half_groups + y_there * z_size + z_there
        sum_partners.append(((place, lax.bitwise_xor(dom, 2 * x_step)), sub))

    loads = [
        pltpu.make_async_copy(source, target, load_sem.at[number])
        for number, (source, target) in enumerate(
            (
                (boundary_hbm, window.at[pl.ds((4 + dom) * ROWS, ROWS)]),
                (corr_source_hbm, corr_source_ref),
                (source_hbm, source_ref),
                (poses_hbm, poses_ref),
                (corr_lane_hbm, corr_lane_ref),
                (anchor_hbm, anchor_ref),
                (target_hbm, target_ref),
                (tile_hbm, tile_ref),
            )
        )
    ]
    for load in loads:
        load.start()
    barrier = pltpu.get_barrier_semaphore()
    z_line = [
        (sub - z_spot + lax.rem(z_spot + turn, z_size), dom) for turn in range(1, z_size)
    ]
    y_line = [
        (
            sub_high * half_groups + lax.rem(y_spot + turn, 4) * z_size + z_spot,
            dom,
        )
        for turn in range(1, 4)
    ]
    x_line = [((1 - sub_high) * half_groups + sub_low, lax.bitwise_xor(dom, 2))]

    def signal_all(semaphore, devices):
        for device in devices:
            pl.semaphore_signal(semaphore, inc=1, device_id=device, device_id_type=MESH)

    chain_line = []
    for offset in (1, -1, 2, -2, 3, -3):
        inside = (sub_low + offset + half_groups) // half_groups
        crosses = lax.bitwise_xor(inside, 1)
        flip = 2 * jnp.minimum(crosses, 1)
        chain_line.append((near_by(offset), lax.bitwise_xor(dom, flip)))
        if abs(offset) == 1:
            chain_line.append((near_by(offset), lax.bitwise_xor(dom, 2 - flip)))
    group_line = [(sub, lax.bitwise_xor(dom, other)) for other in (1, 2, 3)]
    greeted = chain_line + group_line + z_line + y_line + x_line
    signal_all(barrier, greeted)

    pl.semaphore_wait(barrier, len(greeted))
    started = []

    def push(copies, send_sem, recv_sem):
        for source, target, device in copies:
            pltpu.make_async_remote_copy(
                src_ref=source,
                dst_ref=target,
                send_sem=send_sem,
                recv_sem=recv_sem,
                device_id=device,
                device_id_type=MESH,
            ).start()

    def whole(ref, send_sem, recv_sem):
        return pltpu.make_async_remote_copy(
            src_ref=ref,
            dst_ref=ref,
            send_sem=send_sem,
            recv_sem=recv_sem,
            device_id=(sub, lax.bitwise_xor(dom, 1)),
            device_id_type=MESH,
        )

    own_slot = REACH * 4 + dom

    def halo_push(buffer, rows, send, recv):
        at = lambda slot, count=1: buffer.at[pl.ds(slot, count), pl.ds(0, rows)]
        push(
            [(at(own_slot), at(slot), device) for device, slot in halo_partners], send, recv
        )
        return whole(at(0, TILES - 1), send, recv)

    loads[0].wait()
    sibling = lax.bitwise_xor(dom, 1)
    across = lax.bitwise_xor(dom, 2)
    to_sibling = (sub, sibling)
    to_across = (sub, across)

    to_next = lax.bitwise_xor(dom, 2 * (sub_low // (half_groups - 1)))
    to_last = lax.bitwise_xor(dom, 2 * (lax.rem(sub_low + half_groups - 1, half_groups) // (half_groups - 1)))

    def window_copy(number, part, slot, device):
        at = window.at[pl.ds(slot * ROWS + part * PART, PART)]
        return pltpu.make_async_remote_copy(
            src_ref=at,
            dst_ref=at,
            send_sem=win_send.at[number, part],
            recv_sem=win_recv.at[slot, part],
            device_id=device,
            device_id_type=MESH,
        )

    def window_copy_to(number, part, slot, slot_there, device):
        at = window.at[pl.ds(slot * ROWS + part * PART, PART)]
        there = window.at[pl.ds(slot_there * ROWS + part * PART, PART)]
        return pltpu.make_async_remote_copy(
            src_ref=at,
            dst_ref=there,
            send_sem=win_send.at[number, part],
            recv_sem=win_recv.at[slot_there, part],
            device_id=device,
            device_id_type=MESH,
        )

    def window_send(number, part, slot, device, slot_there=None):
        slot_there = slot if slot_there is None else slot_there
        copy = window_copy_to(number, part, slot, slot_there, device)
        copy.start()
        started.append(copy)

    def window_wait(part, slot):
        window_copy(0, part, slot, to_sibling).wait_recv()

    for part in range(PARTS):
        window_send(2, part, 4 + dom, to_across)
        window_send(3, part, 4 + dom, to_sibling)
    for part in range(PARTS):
        window_send(0, part, 4 + dom, (near_by(1), to_next), dom)
        window_send(1, part, 4 + dom, (near_by(-1), to_last), 8 + dom)
    for part in range(1, PARTS):
        window_send(4, part, 4 + dom, (near_by(1), lax.bitwise_xor(to_next, 2)), dom)
        window_send(5, part, 4 + dom, (near_by(-1), lax.bitwise_xor(to_last, 2)), 8 + dom)
    for number in (5, 6, 7):
        loads[number].wait()
    lane_row = iota((1, 128), 1)
    row = jnp.zeros((1, 128), F32)
    edge_of_row = iota((EDGES, 128), 0)
    own_target = jnp.zeros((EDGES, 128), jnp.int32)
    for edge in range(EDGES):
        value = target_ref[edge // EDGE_SCAN, edge % EDGE_SCAN]
        row = jnp.where(lane_row == edge, value.astype(F32), row)
        own_target = jnp.where(edge_of_row == edge, value, own_target)
    for scan in range(SCAN_DEV):
        row = jnp.where(lane_row == EDGES + scan, anchor_ref[scan], row)
    early[pl.ds(own_slot, 1)] = row.reshape(1, 1, 128)
    signal_all(word.at[0], y_line)
    signal_all(word.at[2], group_line)
    pl.semaphore_wait(word.at[2], len(group_line))
    early_copies = halo_push(early, 1, early_send, early_recv)
    started.append(early_copies)
    early[pl.ds(TILES, 4)] = jnp.zeros((4, 1, 128), F32)
    for step in range(GN_ITERS):
        gram[step, pl.ds(TILES, 4)] = jnp.zeros((4, 8, 128), F32)
        gram[step, pl.ds(0, TILES), pl.ds(6, 2)] = jnp.zeros((TILES, 2, 128), F32)

    def gather_scan(scan):
        indices = corr_source_ref[scan].reshape(EDGE_SCAN * CT, 128)
        low = lax.bitwise_and(indices, 127)
        high = lax.shift_right_logical(indices, 7)

        def gather_blocks(group, found):
            found = list(found)
            for number in range(8):
                block = group * 8 + number
                here = high == block
                for comp in range(3):
                    at = pl.multiple_of(block * 128, 128)
                    line = source_ref[comp, pl.ds(scan, 1), pl.ds(at, 128)]
                    wide = jnp.broadcast_to(line, (EDGE_SCAN * CT, 128))
                    value = jnp.take_along_axis(wide, low, axis=1, mode="promise_in_bounds")
                    found[comp] = jnp.where(here, value, found[comp])
            return tuple(found)

        empty = jnp.zeros((EDGE_SCAN * CT, 128), F32)
        found = lax.fori_loop(0, 4, gather_blocks, (empty, empty, empty))
        for comp in range(3):
            picked[comp, pl.ds(scan * 16, 16), :] = found[comp]

    loads[1].wait()
    loads[2].wait()
    for part in range(PARTS):
        gather_scan(part)
        window_wait(part, 4 + across)
        window_send(8, part, 4 + across, to_sibling)
        for number, slot in ((4, to_last), (5, 8 + to_next)):
            window_wait(part, slot)
            if part == 0:
                window_send(number, part, slot, to_across)
            window_send(number + 2, part, slot, to_sibling)
    pl.semaphore_wait(word.at[0], len(y_line))
    signal_all(word.at[1], x_line)
    gather_scan(2)
    gather_scan(3)
    for part in range(PARTS):
        for number, slot in (
            (9, lax.bitwise_xor(to_last, 2)),
            (10, 8 + lax.bitwise_xor(to_next, 2)),
        ):
            window_wait(part, slot)
            window_send(number, part, slot, to_sibling)

    loads[3].wait()
    start = near_by(-REACH) * 16
    first_tile = start // 128
    next_tile = lax.rem(first_tile + 1, groups * 16 // 128)
    pair = jnp.concatenate(
        [
            poses_ref[:, pl.ds(pl.multiple_of(first_tile * 128, 128), 128)],
            poses_ref[:, pl.ds(pl.multiple_of(next_tile * 128, 128), 128)],
        ],
        axis=1,
    )
    shift = lax.rem(256 - lax.rem(start, 128), 256)
    rolled = pltpu.roll(pair, shift, 1)[:, :128]
    pose = [rolled[k : k + 1] for k in range(12)]

    lane16 = iota((EDGES, 128), 1)
    own_source_lane = REACH * 16 + dom * SCAN_DEV + edge_of_row // EDGE_SCAN
    own_ends = jnp.concatenate(
        [
            (lane16 == own_source_lane).astype(F32),
            (lane16 == own_target + (REACH - 1) * 16).astype(F32),
        ],
        axis=0,
    ).astype(BF16)

    row_of = iota((16, 6 * 128), 0) == lax.shift_right_logical(iota((16, 6 * 128), 1), 7)
    into_rows = jnp.where(row_of, 1.0, 0.0).astype(BF16)

    pose_rows = jnp.concatenate(pose + [jnp.zeros((4, 128), F32)], axis=0)
    pose_ends = pick_turned(own_ends, pose_rows)
    end_poses = [
        [
            jnp.broadcast_to(
                pose_ends[end * EDGES : (end + 1) * EDGES, k : k + 1], (EDGES, 128)
            )
            for k in range(12)
        ]
        for end in range(2)
    ]

    lane8 = iota((8, 128), 1)
    row8 = iota((8, 128), 0)
    for part in range(PARTS):
        for other in (sibling, lax.bitwise_xor(dom, 3)):
            for offset in range(3):
                window_wait(part, offset * 4 + other)
    pl.semaphore_wait(word.at[1], len(x_line))
    loads[4].wait()

    def gather_edge(edge, carry):
        scan = edge // EDGE_SCAN
        slot = lax.rem(edge, EDGE_SCAN)
        first = target_ref[scan, slot] * 48
        lanes = corr_lane_ref[scan, slot]
        for chunk in range(CT):
            tile = window[pl.ds(first + tile_ref[scan, slot, chunk], 8, stride=8), :]
            spread = jnp.broadcast_to(lanes[chunk : chunk + 1], (8, 128))
            value = jnp.take_along_axis(tile, spread, axis=1, mode="promise_in_bounds")
            chosen[pl.ds(pl.multiple_of(edge * 32 + chunk * 8, 8), 8), :] = value
        return carry

    lax.fori_loop(0, EDGES, gather_edge, 0, unroll=True)
    for chunk in range(CT):
        for comp in range(3):
            comps[comp, chunk] = picked[comp, pl.ds(chunk, EDGES, stride=CT), :]
        for comp in range(6):
            comps[3 + comp, chunk] = chosen[pl.ds(chunk * 8 + comp, EDGES, stride=32), :]


    for step in range(GN_ITERS):
        here, there = end_poses
        sums = {}
        for chunk in range(CT):
            data = [comps[k, chunk] for k in range(9)]

            def turn(matrix, vector):
                return [
                    matrix[3 * i] * vector[0]
                    + matrix[3 * i + 1] * vector[1]
                    + matrix[3 * i + 2] * vector[2]
                    for i in range(3)
                ]

            placed = [v + t for v, t in zip(turn(here[:9], data[0:3]), here[9:])]
            target = [v + t for v, t in zip(turn(there[:9], data[3:6]), there[9:])]
            normal = turn(there[:9], data[6:9])
            offset = [q - p for q, p in zip(target, placed)]
            misfit = normal[0] * offset[0] + normal[1] * offset[1] + normal[2] * offset[2]
            jac = [
                placed[1] * normal[2] - placed[2] * normal[1],
                placed[2] * normal[0] - placed[0] * normal[2],
                placed[0] * normal[1] - placed[1] * normal[0],
            ] + normal
            for a, b in PAIRS:
                term = jac[a] * jac[b]
                sums[a, b] = sums[a, b] + term if chunk else term
            for a in range(6):
                term = jac[a] * misfit
                sums[a, 6] = sums[a, 6] + term if chunk else term
        nothing = jnp.zeros((EDGES, 128), F32)
        message = None
        split = {key: parts_of(value) for key, value in sums.items()}
        for part in range(2):
            spread = jnp.concatenate(
                [
                    jnp.concatenate(
                        [split[min(a, b), max(a, b)][part] for b in range(7)]
                        + [nothing.astype(BF16)],
                        axis=0,
                    )
                    for a in range(6)
                ],
                axis=1,
            )
            term = lax.dot_general(
                into_rows, spread, (((1,), (1,)), ((), ())), preferred_element_type=F32
            )
            message = term if message is None else message + term
        message = message[:8] * (1.0 / SAMPLES)
        gram[step, pl.ds(own_slot, 1)] = message.reshape(1, 8, 128)
        gram_copies = halo_push(gram.at[step], 6, gram_send.at[step], gram_recv.at[step])
        if step == 0:
            for copy in started:
                copy.wait_send()
            started = []
            early_copies.wait_recv()
            rows = early[...].reshape(PAD, 128)
            rows_turned = jnp.concatenate([rows, jnp.zeros((128 - PAD, 128), F32)], axis=0).T
            lane8 = iota((8, 128), 1)
            row8 = iota((8, 128), 0)
            for tile in range(TILES):
                target = rows_turned[:EDGES, tile : tile + 1]
                target_lane = target + float((tile // 4 - 1) * 16)
                source_lane = tile * 4 + edge_of_row // EDGE_SCAN
                ends[pl.ds(tile * EDGES, EDGES), :] = (lane16 == source_lane).astype(F32) - (
                    lane16.astype(F32) == target_lane
                ).astype(F32)
            ends[pl.ds(TILES * EDGES, (PAD - TILES) * EDGES), :] = jnp.zeros(
                ((PAD - TILES) * EDGES, 128), F32
            )
            ends_f32 = ends[...]
            ends_out = ends_f32.astype(BF16)
            ends_abs = jnp.abs(ends_f32).astype(BF16)
            node_of = iota((128, PAD * EDGES), 0)
            ends_turned = ends_f32.T
            far_end = jnp.sum(
                jnp.where(ends_turned < 0.0, node_of, 0), axis=0, keepdims=True
            )
            near_lanes = []
            far_lanes = []
            for group in range(PAD // 8):
                near_lanes.append(group * 32 + lane8 // EDGE_SCAN)
                far_lanes.append(
                    jnp.broadcast_to(far_end[:, group * 128 : group * 128 + 128], (8, 128))
                )

            def along_edges(value, group):
                near = jnp.take_along_axis(value, near_lanes[group], axis=1, mode="promise_in_bounds")
                far_value = jnp.take_along_axis(
                    value, far_lanes[group], axis=1, mode="promise_in_bounds"
                )
                return near - far_value

            of_tile = jnp.where(iota((128, 128), 0) == iota((128, 128), 1) // 4, 1.0, 0.0).astype(BF16)
            anchor_rows = rows_times(rows_turned[EDGES : EDGES + 8], of_tile)
            anchor = jnp.sum(
                jnp.where(row8 == lax.bitwise_and(lane8, 3), anchor_rows, 0.0), axis=0, keepdims=True
            )
            anchor = jnp.broadcast_to(anchor, (8, 128))
            anchor = jnp.where(lane8 < TILES * 4, anchor, 1.0)
        gram_copies.wait_recv()
        tiles = gram[step]
        grouped = [regroup([tiles[8 * g + t] for t in range(8)]) for g in range(PAD // 8)]
        blocks = [
            jnp.concatenate([group[b] for group in grouped], axis=1) for b in range(7)
        ]
        diagonal_terms = jnp.zeros((8, PAD * EDGES), F32)
        row_all = iota((8, PAD * EDGES), 0)
        for b in range(6):
            diagonal_terms = jnp.where(row_all == b, blocks[b], diagonal_terms)
        residual = rows_times(blocks[6], ends_out)
        diagonal = rows_times(diagonal_terms, ends_abs) + anchor
        inverse = 1.0 / diagonal
        scaled = residual * inverse

        def push_edges(group, difference):
            pushed = grouped[group][0] * difference[0:1]
            for b in range(1, 6):
                pushed = pushed + grouped[group][b] * difference[b : b + 1]
            return pushed

        pushed = jnp.concatenate(
            [push_edges(group, along_edges(scaled, group)) for group in range(PAD // 8)],
            axis=1,
        )
        image = rows_times(pushed, ends_out) + anchor * scaled
        second = image * inverse
        own_diff = along_edges(second, 1)
        own_pushed = push_edges(1, own_diff)

        own = slice(REACH * 16, REACH * 16 + 16)
        packed = jnp.concatenate(
            [
                (residual * scaled)[:, own],
                (scaled * image)[:, own],
                (second * image)[:, own],
                (anchor * second * second)[:, own],
                (own_pushed * own_diff)[:, 64:],
            ],
            axis=1,
        )
        sums_row = jnp.sum(jnp.where(row8 < 6, packed, 0.0), axis=0, keepdims=True)

        far[step, pl.ds(sub, 1)] = sums_row.reshape(1, 1, 128)
        own_sum = far.at[step, pl.ds(sub, 1)]
        push(
            [(own_sum, far.at[step, pl.ds(at, 1)], device) for device, at in sum_partners],
            far_send.at[step],
            far_recv.at[step],
        )
        sum_copies = whole(
            far.at[step, pl.ds(0, groups - 1)], far_send.at[step], far_recv.at[step]
        )
        gram_copies.wait_send()
        if step + 1 < GN_ITERS:
            both = pick_turned(own_ends, jnp.concatenate([scaled, second], axis=0))
            first_ends, second_ends = [
                [
                    [
                        jnp.broadcast_to(
                            both[end * EDGES : (end + 1) * EDGES, at + k : at + k + 1],
                            (EDGES, 128),
                        )
                        for k in range(6)
                    ]
                    for end in range(2)
                ]
                for at in (0, 8)
            ]
        sum_copies.wait_recv()
        started.append(sum_copies)
        sums_row = jnp.sum(far[step].reshape(groups, 128), axis=0, keepdims=True)

        part_of = jnp.minimum(lane_row // 16, 3)
        energy, curve, cross, bend = [
            jnp.sum(jnp.where(part_of == k, sums_row, 0.0), axis=1, keepdims=True)
            for k in range(4)
        ]
        step_one = energy / curve
        renewed = step_one * step_one * cross - energy
        ratio = renewed / energy
        curve_two = (
            curve
            - 2.0 * step_one * cross
            + step_one * step_one * bend
            + 2.0 * ratio * (curve - step_one * cross)
            + ratio * ratio * curve
        )
        step_two = renewed / curve_two
        first_factor = step_one + step_two * (1.0 + ratio)
        second_factor = -step_two * step_one
        increment = first_factor * scaled + second_factor * second
        pose = moved_pose(pose, [increment[k : k + 1] for k in range(6)])
        if step + 1 < GN_ITERS:
            end_poses = [
                moved_pose(
                    end_poses[end],
                    [
                        first_factor * first_ends[end][k] + second_factor * second_ends[end][k]
                        for k in range(6)
                    ],
                )
                for end in range(2)
            ]

    final = jnp.concatenate(pose + [jnp.zeros((4, 128), F32)], axis=0)
    final = pltpu.roll(final, 128 - (REACH * 16 + dom * SCAN_DEV), 1)
    out_ref[...] = final.T[:SCAN_DEV, :12]

    for copy in started:
        copy.wait_send()


def local(groups, source_points, boundary, poses, anchor, edge_target, corr_tile, corr_source, corr_lane):
    vmem = pl.BlockSpec(memory_space=pltpu.VMEM)
    hbm = pl.BlockSpec(memory_space=pl.ANY)
    dma = pltpu.SemaphoreType.DMA
    return pl.pallas_call(
        functools.partial(kernel, groups),
        out_shape=pltpu.VMEM((SCAN_DEV, 12), F32),
        in_specs=[hbm] * 8,
        out_specs=vmem,
        scratch_shapes=[
            pltpu.SMEM(anchor.shape, F32),
            pltpu.SMEM(edge_target.shape, jnp.int32),
            pltpu.SMEM(corr_tile.shape, jnp.int32),
            pltpu.VMEM(corr_source.shape, jnp.int32),
            pltpu.VMEM(corr_lane.shape, jnp.int32),
            pltpu.VMEM((3, SCAN_DEV, source_points.shape[2]), F32),
            pltpu.VMEM(poses.shape, F32),
            pltpu.VMEM((12 * ROWS + 64, 128), F32),
            pltpu.VMEM((PAD, 1, 128), F32),
            pltpu.VMEM((GN_ITERS, PAD, 8, 128), F32),
            pltpu.VMEM((GN_ITERS, groups, 1, 128), F32),
            pltpu.VMEM((3, 72, 128), F32),
            pltpu.VMEM((544, 128), F32),
            pltpu.VMEM((9, CT, EDGES, 128), F32),
            pltpu.VMEM((PAD * EDGES, 128), F32),
            dma((11, PARTS)),
            dma((12, PARTS)),
            dma,
            dma,
            dma((GN_ITERS,)),
            dma((GN_ITERS,)),
            dma((GN_ITERS,)),
            dma((GN_ITERS,)),
            dma((8,)),
            pltpu.SemaphoreType.REGULAR((3,)),
        ],
        compiler_params=pltpu.CompilerParams(collective_id=0, has_side_effects=True),
    )(
        source_points.transpose(1, 0, 2),
        boundary.transpose(0, 2, 1, 3).reshape(ROWS, 128),
        poses,
        anchor,
        edge_target,
        corr_tile,
        corr_source,
        corr_lane,
    ).T


def solution(mesh):
    both = ("sub", "dom")
    return jax.shard_map(
        functools.partial(local, mesh.shape["sub"]),
        mesh=mesh,
        in_specs=(
            P(both, None, None),
            P(both, None, None, None),
            P(),
            P(both),
            P(both, None),
            P(both, None, None),
            P(both, None, None, None),
            P(both, None, None, None),
        ),
        out_specs=P(None, both),
        check_vma=False,
    )
```
